512 devices in a mesh: seq: 64 (over z_hi, x, y, core), head: 8 (over z_lo).
Axes of the slice: x: 4, y: 4, z: 16 (z_hi: 2, z_lo: 8; z = z_hi * 8 + z_lo), core: 2. Of those that a mesh axis runs over, the one named last changes fastest.
Arguments:
- queries: bfloat16 [16384, 2048], P('seq', 'head'), may hold values from -6 to 6
- keys: bfloat16 [16384, 2048], P('seq', 'head'), may hold values from -6 to 6
- values: bfloat16 [16384, 2048], P('seq', 'head'), may hold values from -6 to 6
- partner: int32 [16, 64], P('head'), may hold values from 0 to 63, each once within a row
Outputs:
- attended: bfloat16 [16384, 2048], P('seq', 'head')
The draws below stay inside these ranges and needn't reach their ends.
Inputs may be any that keep to these rules, and one draw needn't show every extreme that they name: `partner`: each row is a permutation of the 64 block indices.
All inputs are finite; a program needn't handle non-finite values.
Results may differ from the reference program's by a relative error of at most 0.0049.
Values may be sent and summed in bfloat16 or wider, within the bound.
A program may use at most 64 MiB of HBM per device.

```python
import math
import jax
import jax.numpy as jnp
from jax import lax

HEADS = 16
DH = 128
BS = 256
SINK_ITERS = 8
NB = 64
TOKENS = 16384


def both_fields(key):
    feat_width = HEADS * DH
    query_field = jnp.clip(jax.random.normal(jax.random.fold_in(key, 11), (TOKENS, feat_width), jnp.float32), -5.8, 5.8)
    key_field = jnp.clip(jax.random.normal(jax.random.fold_in(key, 12), (TOKENS, feat_width), jnp.float32), -5.8, 5.8)
    return (query_field, key_field)


def draw_queries(key, part):
    return both_fields(key)[0].astype(jnp.bfloat16)


def draw_keys(key, part):
    return both_fields(key)[1].astype(jnp.bfloat16)


def steps_of(rng, shape, pieces, smallest, top_value):
    loudness, own = 1.0, jax.random.fold_in(rng, 6)
    for position, blocks in pieces:
        heights = jnp.exp(jax.random.uniform(jax.random.fold_in(own, position), (blocks,), jnp.float32, smallest / len(pieces), top_value / len(pieces)))
        loudness = loudness * jnp.repeat(heights, shape[position] // blocks).reshape([-1 if axis == position else 1 for axis in range(len(shape))])
    return loudness


def noise(key, dims, scale, most, cuts=(), kind=jnp.bfloat16):
    entries = scale * jax.random.normal(key, dims, jnp.float32)
    if cuts:
        entries = entries * steps_of(key, dims, cuts, -0.22, 0.18)
    return jnp.clip(entries, -most, most).astype(kind)


def setup_inputs(seed: int = 0) -> dict:
    splits = jax.random.split(jax.random.key(seed), 5)
    queries = draw_queries(jax.random.fold_in(splits[4], 71), 0)
    keys = draw_keys(jax.random.fold_in(splits[4], 71), 0)
    values = noise(splits[2], (TOKENS, HEADS * DH), 1.0, 6.0, ((0, 64), (1, 8)))
    partner = jax.vmap(lambda own: jax.random.permutation(own, NB))(jax.random.split(splits[3], HEADS)).reshape((HEADS, NB)).astype(jnp.int32)
    return {"queries": queries, "keys": keys, "values": values, "partner": partner}


sharpness = 2.0

def log_sum(values_in, along):
    col_top = lax.optimization_barrier(jnp.max(values_in, axis=along, keepdims=True))
    return col_top + jnp.log(lax.optimization_barrier(jnp.sum(jnp.exp(values_in - col_top), axis=along, keepdims=True)))

def block_attention(query_blk, key_prev, key_local, key_part, val_prev, val_local, val_part, bias_blk, keep_prev):
    inv_scale = 1.0 / math.sqrt(DH)
    query_f = query_blk.astype(jnp.float32)
    logit_prev = jnp.einsum('gqd,gkd->gqk', query_f, key_prev.astype(jnp.float32)) * inv_scale
    logit_prev = jnp.where(keep_prev[:, None, None], logit_prev, -jnp.inf)
    logit_local = jnp.einsum('gqd,gkd->gqk', query_f, key_local.astype(jnp.float32)) * inv_scale
    logit_part = jnp.einsum('gqd,gkd->gqk', query_f, key_part.astype(jnp.float32)) * inv_scale + bias_blk[:, None, None]
    logits = jnp.concatenate([logit_prev, logit_local, logit_part], axis=2)
    row_top = lax.optimization_barrier(jnp.max(logits, axis=2, keepdims=True))
    expo = jnp.exp(logits - row_top)
    weights = (expo / lax.optimization_barrier(jnp.sum(expo, axis=2, keepdims=True))).astype(jnp.bfloat16)
    value_cat = jnp.concatenate([val_prev, val_local, val_part], axis=1)
    result = jnp.einsum('gqk,gkd->gqd', weights.astype(jnp.float32), value_cat.astype(jnp.float32))
    return result.astype(jnp.bfloat16)

def reference(queries, keys, values, partner):
    feat_width = HEADS * DH
    query_blocks = queries.reshape(NB, BS, feat_width)
    key_blocks = keys.reshape(NB, BS, feat_width)
    value_blocks = values.reshape(NB, BS, feat_width)
    pooled_q = lax.optimization_barrier(jnp.sum(query_blocks, axis=1, dtype=jnp.float32)) / math.sqrt(BS)
    pooled_k = lax.optimization_barrier(jnp.sum(key_blocks, axis=1, dtype=jnp.float32)) / math.sqrt(BS)
    scores = jnp.dot(pooled_q, pooled_k.T, precision=lax.Precision.HIGHEST, preferred_element_type=jnp.float32) * (sharpness / math.sqrt(feat_width))
    log_plan = scores
    for sweep in range(SINK_ITERS):
        log_plan = log_plan - log_sum(log_plan, 1)
        log_plan = log_plan - log_sum(log_plan, 0)
    block_ids = jnp.arange(NB, dtype=jnp.int32)
    partner_bias = math.log(NB) + log_plan[block_ids[None, :], partner]
    group_size = math.gcd(NB, 16)
    groups = NB // group_size
    keep_prev = (block_ids > 0).reshape(groups, group_size)

    def one_head(head_index):
        start = (head_index * DH).astype(jnp.int32)
        q_head = lax.dynamic_slice_in_dim(query_blocks, start, DH, 2)
        k_head = lax.dynamic_slice_in_dim(key_blocks, start, DH, 2)
        v_head = lax.dynamic_slice_in_dim(value_blocks, start, DH, 2)
        zero_blk = jnp.zeros((1, BS, DH), jnp.bfloat16)
        k_prev = jnp.concatenate([zero_blk, k_head[:-1]], axis=0)
        v_prev = jnp.concatenate([zero_blk, v_head[:-1]], axis=0)
        k_part = jnp.take(k_head, partner[head_index], axis=0)
        v_part = jnp.take(v_head, partner[head_index], axis=0)
        bias_head = partner_bias[head_index]

        def split(arr):
            return arr.reshape((groups, group_size) + arr.shape[1:])
        packed = (split(q_head), split(k_prev), split(k_head), split(k_part), split(v_prev), split(v_head), split(v_part), split(bias_head), keep_prev)
        outs = lax.map(lambda items: block_attention(*items), packed)
        return outs.reshape(NB, BS, DH)
    per_head = lax.map(one_head, jnp.arange(HEADS, dtype=jnp.int32))
    return jnp.transpose(per_head, (1, 2, 0, 3)).reshape(TOKENS, feat_width)
```

```python
import functools
import math

import jax
import jax.numpy as jnp
from jax import lax
from jax.experimental import pallas as pl
from jax.experimental.pallas import tpu as pltpu
from jax.sharding import PartitionSpec as P

DH = 128
BS = 256
SINK_ITERS = 8
SHARPNESS = 2.0
CHUNKS = 4
HIGHEST = lax.Precision.HIGHEST
MESH = pl.DeviceIdType.MESH


def bytes_wait(ref, sem):
    pltpu.make_async_copy(ref, ref, sem).wait()


def exchange_kernel(
    plane,
    groups,
    partner,
    q_hbm,
    k_hbm,
    v_hbm,
    part_out,
    prev_out,
    plan_out,
    qs,
    kv,
    held_a,
    held_b,
    pick,
    pk_all,
    pq,
    parts,
    rows_all,
    load_sem,
    own_sem,
    pk_send,
    pk_recv,
    fwd_send,
    fwd_recv,
    mir_send,
    mir_recv,
    head_send,
    head_recv,
    row_send,
    row_recv,
    spread_send,
    spread_recv,
    z_send,
    z_recv,
    back_send,
    back_recv,
    prev_send,
    extra_send,
    prev_recv,
):
    held = (held_a, held_b)
    s = lax.axis_index("seq")
    g = lax.axis_index("head")
    p = s // plane
    i = s % plane
    base = p * plane
    mirror = (s + plane) % (2 * plane)
    half = plane // 2
    step = plane // CHUNKS
    before = (base + 2 * plane - 1) % (2 * plane)

    def peer(o):
        j = (i + o) % plane
        return j, base + j

    def remote(src, dst, ss, rs, seq, head=None):
        return pltpu.make_async_remote_copy(
            src_ref=src,
            dst_ref=dst,
            send_sem=ss,
            recv_sem=rs,
            device_id=(seq, g if head is None else head),
            device_id_type=MESH,
        )

    def each_peer(body):
        def wrapped(o, c):
            body(*peer(o))
            return c

        lax.fori_loop(1, plane, wrapped, 0)

    def each_group(body):
        def wrapped(o, c):
            body((g + o) % groups)
            return c

        lax.fori_loop(1, groups, wrapped, 0)

    barrier = pltpu.get_barrier_semaphore()
    pl.semaphore_signal(barrier, inc=1, device_id=(mirror, g), device_id_type=MESH)
    each_group(
        lambda og: pl.semaphore_signal(barrier, inc=1, device_id=(s, og), device_id_type=MESH)
    )
    each_peer(
        lambda j, d: pl.semaphore_signal(barrier, inc=1, device_id=(d, g), device_id_type=MESH)
    )

    loads = (
        pltpu.make_async_copy(q_hbm, qs, load_sem.at[0]),
        pltpu.make_async_copy(k_hbm, kv.at[pl.ds(0, half)], load_sem.at[1]),
        pltpu.make_async_copy(v_hbm, kv.at[pl.ds(half, half)], load_sem.at[2]),
    )
    for c in loads:
        c.start()
    for c in loads:
        c.wait()
    pooled_q = jnp.sum(jnp.sum(qs[...].astype(jnp.float32), axis=0), axis=0, keepdims=True)
    pooled_k = jnp.sum(
        jnp.sum(kv[pl.ds(0, half)].astype(jnp.float32), axis=0), axis=0, keepdims=True
    )
    for h in range(2):
        lanes = slice(h * DH, (h + 1) * DH)
        pq[0, h : h + 1, :] = pooled_q[:, lanes] / math.sqrt(BS)
        pk_all[s, h : h + 1, :] = pooled_k[:, lanes] / math.sqrt(BS)

    pl.semaphore_wait(barrier, plane - 1 + 1 + groups - 1)

    to_mirror = (
        remote(pk_all.at[s], pk_all.at[s], mir_send.at[0], mir_recv.at[0], mirror),
        remote(pq.at[0], pq.at[1], mir_send.at[1], mir_recv.at[1], mirror),
    )
    for c in to_mirror:
        c.start()

    def spread(h):
        lanes = pl.ds(h * DH, DH)
        pltpu.make_async_copy(kv.at[i, :, lanes], held[h].at[s], spread_recv.at[h]).start()
        each_peer(
            lambda j, d: remote(
                kv.at[j, :, lanes], held[h].at[s], spread_send.at[h], spread_recv.at[h], d
            ).start()
        )

    def exchange(h, c):
        rows = pl.ds(base + c * step, step)
        return remote(
            held[h].at[rows], held[h].at[rows], z_send.at[h, c], z_recv.at[h, c], mirror
        )

    def arrived(h, c):
        rows = pl.ds((plane - base) + c * step, step)
        bytes_wait(held[h].at[rows], z_recv.at[h, c])

    spread(0)
    each_peer(lambda j, d: remote(pk_all.at[s], pk_all.at[s], pk_send, pk_recv, d).start())
    spread(1)

    @pl.when(i < plane - 1)
    def _():
        for h in range(2):
            lanes = pl.ds(h * DH, DH)
            remote(
                kv.at[:, :, lanes], prev_out.at[h], prev_send.at[h], prev_recv.at[h], s + 1
            ).start()

    bytes_wait(held[0].at[pl.ds(0, plane)], spread_recv.at[0])
    exchange(0, 0).start()
    exchange(0, 1).start()
    for c in to_mirror:
        c.wait_recv()
    each_peer(
        lambda j, d: remote(
            pk_all.at[mirror], pk_all.at[mirror], fwd_send, fwd_recv, d
        ).start()
    )
    bytes_wait(held[1].at[pl.ds(0, plane)], spread_recv.at[1])
    exchange(0, 2).start()

    bytes_wait(pk_all.at[pl.ds(0, plane - 1)], pk_recv)
    bytes_wait(pk_all.at[pl.ds(0, plane - 1)], fwd_recv)
    total = jnp.zeros((2, 2 * plane), jnp.float32)
    for h in range(2):
        total = total + lax.dot_general(
            pq[:, h, :],
            pk_all[:, h, :],
            (((1,), (1,)), ((), ())),
            precision=HIGHEST,
            preferred_element_type=jnp.float32,
        )
    total = total * (SHARPNESS / math.sqrt(2 * DH * groups))
    parts[g, :, 0 : 2 * plane] = total
    each_group(
        lambda og: remote(parts.at[g], parts.at[g], head_send, head_recv, s, og).start()
    )
    exchange(0, 3).start()
    for c in range(CHUNKS):
        exchange(1, c).start()

    bytes_wait(parts.at[pl.ds(0, groups - 1)], head_recv)
    rows_all[i] = jnp.sum(parts[...], axis=0)
    each_peer(lambda j, d: remote(rows_all.at[i], rows_all.at[i], row_send, row_recv, d).start())

    def give_back(h):
        for c in range(CHUNKS):
            arrived(h, c)

        def choose(j, carry):
            pick[h, j] = held[h][partner[h, base + j]]
            return carry

        lax.fori_loop(0, plane, choose, 0)
        each_peer(
            lambda j, d: remote(
                pick.at[h, j], part_out.at[h, i], back_send.at[h], back_recv.at[h], d
            ).start()
        )
        pltpu.make_async_copy(pick.at[h, i], part_out.at[h, i], back_recv.at[h]).start()

        @pl.when(i == 0)
        def _():
            pltpu.make_async_copy(held[h].at[before], prev_out.at[h, 0], prev_recv.at[h]).start()

        @pl.when(i > 0)
        def _():
            remote(
                held[h].at[before],
                prev_out.at[h, i],
                extra_send.at[h],
                prev_recv.at[h],
                base,
            ).start()

    give_back(0)

    bytes_wait(rows_all.at[pl.ds(0, plane - 1)], row_recv)
    plan = jnp.concatenate([rows_all[:, 0, :], rows_all[:, 1, :]], axis=0)[:, : 2 * plane]

    def sweep(_, x):
        for along in (1, 0):
            top = jnp.max(x, axis=along, keepdims=True)
            x = x - (top + jnp.log(jnp.sum(jnp.exp(x - top), axis=along, keepdims=True)))
        return x

    plan_out[...] = lax.fori_loop(0, SINK_ITERS, sweep, plan)

    give_back(1)

    for h in range(2):
        bytes_wait(part_out.at[h], back_recv.at[h])
        bytes_wait(prev_out.at[h], prev_recv.at[h])
        bytes_wait(held[h].at[pl.ds(0, plane - 1)], spread_send.at[h])
        bytes_wait(pick.at[h, pl.ds(0, plane - 1)], back_send.at[h])
        for c in range(CHUNKS):
            exchange(h, c).wait_send()
    for c in to_mirror:
        c.wait_send()
    bytes_wait(pk_all.at[pl.ds(0, plane - 1)], pk_send)
    bytes_wait(pk_all.at[pl.ds(0, plane - 1)], fwd_send)
    bytes_wait(parts.at[pl.ds(0, groups - 1)], head_send)
    bytes_wait(rows_all.at[pl.ds(0, plane - 1)], row_send)

    @pl.when(i < plane - 1)
    def _():
        for h in range(2):
            bytes_wait(prev_out.at[h], prev_send.at[h])

    @pl.when(i > 0)
    def _():
        for h in range(2):
            bytes_wait(held[h].at[0], extra_send.at[h])


def attend_kernel(plane, partner, q_ref, k_ref, v_ref, part, prev, plan, out_ref):
    s = lax.axis_index("seq")
    i = s % plane
    half = plane // 2
    inv_scale = 1.0 / math.sqrt(DH)
    log_plan = plan[...]
    row_id = lax.broadcasted_iota(jnp.int32, log_plan.shape, 0)
    col_id = lax.broadcasted_iota(jnp.int32, log_plan.shape, 1)
    for h in range(2):
        lanes = slice(h * DH, (h + 1) * DH)
        chosen = (row_id == i) & (col_id == partner[h, s])
        bias = math.log(2 * plane) + jnp.sum(jnp.where(chosen, log_plan, 0.0))
        q = q_ref[:, lanes]
        keys = (
            prev[h, 0:half].reshape(BS, DH),
            k_ref[:, lanes],
            part[h, 0:half].reshape(BS, DH),
        )
        vals = (
            prev[h, half:plane].reshape(BS, DH),
            v_ref[:, lanes],
            part[h, half:plane].reshape(BS, DH),
        )
        logits = [
            lax.dot_general(q, key, (((1,), (1,)), ((), ())), preferred_element_type=jnp.float32)
            * inv_scale
            for key in keys
        ]
        logits[0] = jnp.where(s > 0, logits[0], -jnp.inf)
        logits[2] = logits[2] + bias
        top = jnp.maximum(jnp.maximum(logits[0], logits[1]), logits[2])
        top = jnp.max(top, axis=1, keepdims=True)
        expo = [jnp.exp(x - top) for x in logits]
        denom = jnp.sum(expo[0] + expo[1] + expo[2], axis=1, keepdims=True)
        inverse = 1.0 / denom
        mixed = jnp.zeros((BS, DH), jnp.float32)
        for e, val in zip(expo, vals):
            mixed = mixed + jnp.dot(
                (e * inverse).astype(jnp.bfloat16), val, preferred_element_type=jnp.float32
            )
        out_ref[:, lanes] = mixed.astype(jnp.bfloat16)


def solution(mesh):
    seq, groups = mesh.shape["seq"], mesh.shape["head"]
    plane = seq // 2
    piece = 2 * BS // plane
    half = plane // 2
    width = 2 * DH

    def body(queries, keys, values, partner):
        vmem = pl.BlockSpec(memory_space=pltpu.VMEM)
        smem = pl.BlockSpec(memory_space=pltpu.SMEM)
        hbm = pl.BlockSpec(memory_space=pl.ANY)
        dma = pltpu.SemaphoreType.DMA
        blocks = jax.ShapeDtypeStruct((2, plane, piece, DH), jnp.bfloat16)
        folded = (half, piece, width)
        part, prev, plan = pl.pallas_call(
            functools.partial(exchange_kernel, plane, groups),
            out_shape=(blocks, blocks, jax.ShapeDtypeStruct((seq, seq), jnp.float32)),
            in_specs=[smem, hbm, hbm, hbm],
            out_specs=(vmem, vmem, vmem),
            scratch_shapes=[
                pltpu.VMEM(folded, jnp.bfloat16),
                pltpu.VMEM((plane, piece, width), jnp.bfloat16),
                pltpu.VMEM((seq, piece, DH), jnp.bfloat16),
                pltpu.VMEM((seq, piece, DH), jnp.bfloat16),
                pltpu.VMEM((2, plane, piece, DH), jnp.bfloat16),
                pltpu.VMEM((seq, 2, DH), jnp.float32),
                pltpu.VMEM((2, 2, DH), jnp.float32),
                pltpu.VMEM((groups, 2, DH), jnp.float32),
                pltpu.VMEM((plane, 2, DH), jnp.float32),
                dma((3,)),
                dma(()),
                dma(()),
                dma(()),
                dma(()),
                dma(()),
                dma((2,)),
                dma((2,)),
                dma(()),
                dma(()),
                dma(()),
                dma(()),
                dma((2,)),
                dma((2,)),
                dma((2, CHUNKS)),
                dma((2, CHUNKS)),
                dma((2,)),
                dma((2,)),
                dma((2,)),
                dma((2,)),
                dma((2,)),
            ],
            compiler_params=pltpu.CompilerParams(collective_id=0, has_side_effects=True),
            name="exchange",
        )(partner, queries.reshape(folded), keys.reshape(folded), values.reshape(folded))
        return pl.pallas_call(
            functools.partial(attend_kernel, plane),
            out_shape=jax.ShapeDtypeStruct(queries.shape, queries.dtype),
            in_specs=[smem] + [vmem] * 6,
            out_specs=vmem,
            name="attend",
        )(partner, queries, keys, values, part, prev, plan)

    return jax.shard_map(
        body,
        mesh=mesh,
        in_specs=(P("seq", "head"), P("seq", "head"), P("seq", "head"), P("head", None)),
        out_specs=P("seq", "head"),
        check_vma=False,
    )
```

```python
import functools
import math

import jax
import jax.numpy as jnp
from jax import lax
from jax.experimental import pallas as pl
from jax.experimental.pallas import tpu as pltpu
from jax.sharding import PartitionSpec as P

DH = 128
BS = 256
SINK_ITERS = 8
SHARPNESS = 2.0
CHUNKS = 4
HIGHEST = lax.Precision.HIGHEST
MESH = pl.DeviceIdType.MESH


def bytes_wait(ref, sem):
    pltpu.make_async_copy(ref, ref, sem).wait()


def sparse_attention_kernel(
    plane,
    groups,
    partner,
    q_hbm,
    k_hbm,
    v_hbm,
    out,
    qs,
    kv,
    held_a,
    held_b,
    pick,
    part,
    prev,
    pk_all,
    pq,
    parts,
    rows_all,
    bias,
    top_all,
    den_all,
    mix_all,
    load_sem,
    pk_send,
    pk_recv,
    fwd_send,
    fwd_recv,
    mir_send,
    mir_recv,
    head_send,
    head_recv,
    row_send,
    row_recv,
    bias_send,
    bias_recv,
    spread_send,
    spread_recv,
    z_send,
    z_recv,
    back_send,
    back_recv,
    prev_send,
    extra_send,
    prev_recv,
    ready,
):
    held = (held_a, held_b)
    s = lax.axis_index("seq")
    g = lax.axis_index("head")
    p = s // plane
    i = s % plane
    base = p * plane
    mirror = (s + plane) % (2 * plane)
    half = plane // 2
    step = plane // CHUNKS
    before = (base + 2 * plane - 1) % (2 * plane)
    inv_scale = 1.0 / math.sqrt(DH)

    def remote(src, dst, ss, rs, seq, head=None):
        return pltpu.make_async_remote_copy(
            src_ref=src,
            dst_ref=dst,
            send_sem=ss,
            recv_sem=rs,
            device_id=(seq, g if head is None else head),
            device_id_type=MESH,
        )

    def signal(sem, seq, head=None):
        pl.semaphore_signal(
            sem,
            inc=1,
            device_id=(seq, g if head is None else head),
            device_id_type=MESH,
        )

    def each_peer(body):
        def wrapped(o, c):
            j = (i + o) % plane
            body(j, base + j)
            return c

        lax.fori_loop(1, plane, wrapped, 0)

    def each_group(body):
        def wrapped(o, c):
            body((g + o) % groups)
            return c

        lax.fori_loop(1, groups, wrapped, 0)

    barrier = pltpu.get_barrier_semaphore()

    @pl.when(p == 0)
    def _():
        signal(barrier, mirror)
        each_group(lambda og: signal(barrier, s, og))

    each_peer(lambda j, d: signal(barrier, d))

    loads = (
        pltpu.make_async_copy(q_hbm, qs, load_sem.at[0]),
        pltpu.make_async_copy(k_hbm, kv.at[pl.ds(0, half)], load_sem.at[1]),
        pltpu.make_async_copy(v_hbm, kv.at[pl.ds(half, half)], load_sem.at[2]),
    )
    for c in loads:
        c.start()
    for c in loads:
        c.wait()
    pooled_q = jnp.sum(jnp.sum(qs[...].astype(jnp.float32), axis=0), axis=0, keepdims=True)
    pooled_k = jnp.sum(
        jnp.sum(kv[pl.ds(0, half)].astype(jnp.float32), axis=0), axis=0, keepdims=True
    )
    for h in range(2):
        lanes = slice(h * DH, (h + 1) * DH)
        pq[0, h : h + 1, :] = pooled_q[:, lanes] / math.sqrt(BS)
        pk_all[s, h : h + 1, :] = pooled_k[:, lanes] / math.sqrt(BS)

    to_mirror = (
        remote(pk_all.at[s], pk_all.at[s], mir_send.at[0], mir_recv.at[0], mirror),
        remote(pq.at[0], pq.at[1], mir_send.at[1], mir_recv.at[1], mirror),
    )
    bias_copy = remote(bias.at[1], bias.at[0], bias_send, bias_recv, mirror)

    def spread(h):
        lanes = pl.ds(h * DH, DH)
        pltpu.make_async_copy(kv.at[i, :, lanes], held[h].at[s], spread_recv.at[h]).start()
        each_peer(
            lambda j, d: remote(
                kv.at[j, :, lanes], held[h].at[s], spread_send.at[h], spread_recv.at[h], d
            ).start()
        )

    def hand_on():
        @pl.when(i < plane - 1)
        def _():
            for h in range(2):
                lanes = pl.ds(h * DH, DH)
                remote(
                    kv.at[:, :, lanes], prev.at[h], prev_send.at[h], prev_recv.at[h], s + 1
                ).start()

    def exchange(h, c):
        rows = pl.ds(base + c * step, step)
        return remote(
            held[h].at[rows], held[h].at[rows], z_send.at[h, c], z_recv.at[h, c], mirror
        )

    def spread_done(h):
        bytes_wait(held[h].at[pl.ds(0, plane)], spread_recv.at[h])

    def give_back(h):
        for c in range(CHUNKS):
            rows = pl.ds((plane - base) + c * step, step)
            bytes_wait(held[h].at[rows], z_recv.at[h, c])

        def choose(j, carry):
            pick[h, j] = held[h][partner[h, base + j]]
            return carry

        lax.fori_loop(0, plane, choose, 0)
        each_peer(
            lambda j, d: remote(
                pick.at[h, j], part.at[h, i], back_send.at[h], back_recv.at[h], d
            ).start()
        )
        pltpu.make_async_copy(pick.at[h, i], part.at[h, i], back_recv.at[h]).start()

        @pl.when(i == 0)
        def _():
            pltpu.make_async_copy(held[h].at[before], prev.at[h, 0], prev_recv.at[h]).start()

        @pl.when(i > 0)
        def _():
            remote(
                held[h].at[before], prev.at[h, i], extra_send.at[h], prev_recv.at[h], base
            ).start()

    def query(h):
        return qs[:, :, h * DH : (h + 1) * DH].reshape(BS, DH)

    def scored(h, key):
        x = lax.dot_general(
            query(h), key, (((1,), (1,)), ((), ())), preferred_element_type=jnp.float32
        )
        return x * inv_scale

    def stacked(ref, h):
        return (
            ref[h, 0:half].reshape(BS, DH),
            ref[h, half:plane].reshape(BS, DH),
        )

    def local():
        for h in range(2):
            lanes = slice(h * DH, (h + 1) * DH)
            x = scored(h, kv[0:half, :, lanes].reshape(BS, DH))
            top = jnp.max(x, axis=1, keepdims=True)
            e = jnp.exp(x - top)
            top_all[h] = top
            den_all[h] = jnp.sum(e, axis=1, keepdims=True)
            mix_all[h] = jnp.dot(
                e.astype(jnp.bfloat16),
                kv[half:plane, :, lanes].reshape(BS, DH),
                preferred_element_type=jnp.float32,
            )

    def merged(h, ref, shift):
        key, val = stacked(ref, h)
        x = scored(h, key)
        if shift is not None:
            x = x + shift
        old = top_all[h]
        top = jnp.maximum(old, jnp.max(x, axis=1, keepdims=True))
        keep = jnp.exp(old - top)
        e = jnp.exp(x - top)
        den = den_all[h] * keep + jnp.sum(e, axis=1, keepdims=True)
        mix = mix_all[h] * keep + jnp.dot(
            e.astype(jnp.bfloat16), val, preferred_element_type=jnp.float32
        )
        return top, den, mix

    def previous(h):
        top, den, mix = merged(h, prev, None)
        top_all[h] = top
        den_all[h] = den
        mix_all[h] = mix

    def early_previous():
        @pl.when(i > 0)
        def _():
            for h in range(2):
                bytes_wait(prev.at[h], prev_recv.at[h])
                previous(h)

    def late_previous(h):
        @pl.when(i == 0)
        def _():
            bytes_wait(prev.at[h], prev_recv.at[h])

        @pl.when(s == plane)
        def _():
            previous(h)

    def finish(h):
        late_previous(h)
        bytes_wait(part.at[h], back_recv.at[h])
        _, den, mix = merged(h, part, bias[0, h : h + 1, 0:1])
        out[:, h * DH : (h + 1) * DH] = (mix * (1.0 / den)).astype(jnp.bfloat16)

    def scores():
        total = jnp.zeros((2, 2 * plane), jnp.float32)
        for h in range(2):
            total = total + lax.dot_general(
                pq[:, h, :],
                pk_all[:, h, :],
                (((1,), (1,)), ((), ())),
                precision=HIGHEST,
                preferred_element_type=jnp.float32,
            )
        parts[g, :, 0 : 2 * plane] = total * (SHARPNESS / math.sqrt(2 * DH * groups))

    def sinkhorn():
        x = jnp.concatenate([rows_all[:, 0, :], rows_all[:, 1, :]], axis=0)[:, : 2 * plane]

        def sweep(_, x):
            for along in (1, 0):
                top = jnp.max(x, axis=along, keepdims=True)
                x = x - (top + jnp.log(jnp.sum(jnp.exp(x - top), axis=along, keepdims=True)))
            return x

        x = lax.fori_loop(0, SINK_ITERS, sweep, x)
        row = lax.broadcasted_iota(jnp.int32, x.shape, 0)
        col = lax.broadcasted_iota(jnp.int32, x.shape, 1)
        for which, block in ((0, s), (1, mirror)):
            for h in range(2):
                chosen = (row == i + which * plane) & (col == partner[h, block])
                value = jnp.sum(
                    jnp.sum(jnp.where(chosen, x, 0.0), axis=1, keepdims=True), axis=0, keepdims=True
                )
                bias[which, h : h + 1, :] = jnp.broadcast_to(
                    value + math.log(2 * plane), (1, DH)
                )

    @pl.when(p == 0)
    def _():
        pl.semaphore_wait(barrier, plane - 1 + groups - 1)
        spread(0)
        each_peer(lambda j, d: remote(pk_all.at[s], pk_all.at[s], pk_send, pk_recv, d).start())
        spread(1)
        hand_on()
        local()
        spread_done(0)
        pl.semaphore_wait(ready, 1)
        exchange(0, 0).start()
        exchange(0, 1).start()
        for c in to_mirror:
            c.wait_recv()
        each_peer(
            lambda j, d: remote(
                pk_all.at[mirror], pk_all.at[mirror], fwd_send, fwd_recv, d
            ).start()
        )
        spread_done(1)
        bytes_wait(pk_all.at[pl.ds(0, plane - 1)], pk_recv)
        bytes_wait(pk_all.at[pl.ds(0, plane - 1)], fwd_recv)
        scores()
        each_group(
            lambda og: remote(parts.at[g], parts.at[g], head_send, head_recv, s, og).start()
        )
        for c in range(2, CHUNKS):
            exchange(0, c).start()
        for c in range(CHUNKS):
            exchange(1, c).start()
        early_previous()
        bytes_wait(parts.at[pl.ds(0, groups - 1)], head_recv)
        rows_all[i] = jnp.sum(parts[...], axis=0)
        each_peer(
            lambda j, d: remote(rows_all.at[i], rows_all.at[i], row_send, row_recv, d).start()
        )
        give_back(0)
        bytes_wait(rows_all.at[pl.ds(0, plane - 1)], row_recv)
        sinkhorn()
        bias_copy.start()
        finish(0)
        give_back(1)
        finish(1)
        bytes_wait(pk_all.at[pl.ds(0, plane - 1)], pk_send)
        bytes_wait(pk_all.at[pl.ds(0, plane - 1)], fwd_send)
        bytes_wait(parts.at[pl.ds(0, groups - 1)], head_send)
        bytes_wait(rows_all.at[pl.ds(0, plane - 1)], row_send)
        bias_copy.wait_send()

    @pl.when(p == 1)
    def _():
        pl.semaphore_wait(barrier, plane - 1 + 1)
        signal(ready, mirror)
        for c in to_mirror:
            c.start()
        spread(0)
        spread(1)
        hand_on()
        for h in range(2):
            spread_done(h)
            for c in range(CHUNKS):
                exchange(h, c).start()
        local()
        early_previous()
        give_back(0)
        give_back(1)
        bias_copy.wait_recv()
        finish(0)
        finish(1)
        for c in to_mirror:
            c.wait_send()

    for h in range(2):
        bytes_wait(held[h].at[pl.ds(0, plane - 1)], spread_send.at[h])
        bytes_wait(pick.at[h, pl.ds(0, plane - 1)], back_send.at[h])
        for c in range(CHUNKS):
            exchange(h, c).wait_send()

    @pl.when(i < plane - 1)
    def _():
        for h in range(2):
            bytes_wait(prev.at[h], prev_send.at[h])

    @pl.when(i > 0)
    def _():
        for h in range(2):
            bytes_wait(held[h].at[0], extra_send.at[h])


def solution(mesh):
    seq, groups = mesh.shape["seq"], mesh.shape["head"]
    plane = seq // 2
    piece = 2 * BS // plane
    half = plane // 2
    width = 2 * DH

    def body(queries, keys, values, partner):
        hbm = pl.BlockSpec(memory_space=pl.ANY)
        dma = pltpu.SemaphoreType.DMA
        folded = (half, piece, width)
        pieces = pltpu.VMEM((2, plane, piece, DH), jnp.bfloat16)
        return pl.pallas_call(
            functools.partial(sparse_attention_kernel, plane, groups),
            out_shape=jax.ShapeDtypeStruct(queries.shape, queries.dtype),
            in_specs=[pl.BlockSpec(memory_space=pltpu.SMEM), hbm, hbm, hbm],
            out_specs=pl.BlockSpec(memory_space=pltpu.VMEM),
            scratch_shapes=[
                pltpu.VMEM(folded, jnp.bfloat16),
                pltpu.VMEM((plane, piece, width), jnp.bfloat16),
                pltpu.VMEM((seq, piece, DH), jnp.bfloat16),
                pltpu.VMEM((seq, piece, DH), jnp.bfloat16),
                pieces,
                pieces,
                pieces,
                pltpu.VMEM((seq, 2, DH), jnp.float32),
                pltpu.VMEM((2, 2, DH), jnp.float32),
                pltpu.VMEM((groups, 2, DH), jnp.float32),
                pltpu.VMEM((plane, 2, DH), jnp.float32),
                pltpu.VMEM((2, 2, DH), jnp.float32),
                pltpu.VMEM((2, BS, 1), jnp.float32),
                pltpu.VMEM((2, BS, 1), jnp.float32),
                pltpu.VMEM((2, BS, DH), jnp.float32),
                dma((3,)),
                dma(()),
                dma(()),
                dma(()),
                dma(()),
                dma((2,)),
                dma((2,)),
                dma(()),
                dma(()),
                dma(()),
                dma(()),
                dma(()),
                dma(()),
                dma((2,)),
                dma((2,)),
                dma((2, CHUNKS)),
                dma((2, CHUNKS)),
                dma((2,)),
                dma((2,)),
                dma((2,)),
                dma((2,)),
                dma((2,)),
                pltpu.SemaphoreType.REGULAR,
            ],
            compiler_params=pltpu.CompilerParams(collective_id=0, has_side_effects=True),
            name="sparse_attention",
        )(partner, queries.reshape(folded), keys.reshape(folded), values.reshape(folded))

    return jax.shard_map(
        body,
        mesh=mesh,
        in_specs=(P("seq", "head"), P("seq", "head"), P("seq", "head"), P("head", None)),
        out_specs=P("seq", "head"),
        check_vma=False,
    )
```

```python
import functools
import math

import jax
import jax.numpy as jnp
from jax import lax
from jax.experimental import pallas as pl
from jax.experimental.pallas import tpu as pltpu
from jax.sharding import PartitionSpec as P

DH = 128
BS = 256
SINK_ITERS = 8
SHARPNESS = 2.0
HIGHEST = lax.Precision.HIGHEST
MESH = pl.DeviceIdType.MESH


def bytes_wait(ref, sem):
    pltpu.make_async_copy(ref, ref, sem).wait()


def sparse_attention_kernel(
    plane,
    groups,
    slots,
    partner,
    q_hbm,
    k_hbm,
    v_hbm,
    out,
    crowd,
    qs,
    kv,
    own_a,
    own_b,
    pack_a,
    pack_b,
    slot_a,
    slot_b,
    edge,
    pick,
    part,
    prev,
    col,
    feat,
    partial,
    counts,
    bias,
    top_all,
    den_all,
    mix_all,
    after,
    load_sem,
    col_send,
    col_recv,
    count_send,
    count_recv,
    feat_send,
    feat_recv,
    partial_send,
    partial_recv,
    bias_send,
    bias_recv,
    spread_send,
    spread_recv,
    z_send,
    z_recv,
    edge_send,
    edge_recv,
    back_send,
    back_recv,
    prev_send,
    extra_send,
    prev_recv,
    ready,
):
    own = (own_a, own_b)
    pack = (pack_a, pack_b)
    slot = (slot_a, slot_b)
    s = lax.axis_index("seq")
    g = lax.axis_index("head")
    p = s // plane
    i = s % plane
    base = p * plane
    mirror = (s + plane) % (2 * plane)
    half = plane // 2
    across = plane - base
    slices = 2 * groups
    stride = plane // slices
    inv_scale = 1.0 / math.sqrt(DH)

    def remote(src, dst, ss, rs, seq, head=None):
        return pltpu.make_async_remote_copy(
            src_ref=src,
            dst_ref=dst,
            send_sem=ss,
            recv_sem=rs,
            device_id=(seq, g if head is None else head),
            device_id_type=MESH,
        )

    def signal(sem, seq, head=None):
        pl.semaphore_signal(
            sem,
            inc=1,
            device_id=(seq, g if head is None else head),
            device_id_type=MESH,
        )

    def each_peer(body):
        def wrapped(o, c):
            j = (i + o) % plane
            body(j, base + j)
            return c

        lax.fori_loop(1, plane, wrapped, 0)

    def each_group(body):
        def wrapped(o, c):
            body((g + o) % groups)
            return c

        lax.fori_loop(1, groups, wrapped, 0)

    barrier = pltpu.get_barrier_semaphore()

    @pl.when(p == 0)
    def _():
        for og in range(groups):
            signal(barrier, mirror, og)
        each_group(lambda og: signal(barrier, s, og))

    each_peer(lambda j, d: signal(barrier, d))

    loads = (
        pltpu.make_async_copy(q_hbm, qs, load_sem.at[0]),
        pltpu.make_async_copy(k_hbm, kv.at[pl.ds(0, half)], load_sem.at[1]),
        pltpu.make_async_copy(v_hbm, kv.at[pl.ds(half, half)], load_sem.at[2]),
    )
    for c in loads:
        c.start()
    for c in loads:
        c.wait()
    pooled_q = jnp.sum(jnp.sum(qs[...].astype(jnp.float32), axis=0), axis=0, keepdims=True)
    pooled_k = jnp.sum(
        jnp.sum(kv[pl.ds(0, half)].astype(jnp.float32), axis=0), axis=0, keepdims=True
    )
    for h in range(2):
        lanes = slice(h * DH, (h + 1) * DH)
        col[p, 2 * g + h] = pooled_q[:, lanes] / math.sqrt(BS)
        col[2 + p, 2 * g + h] = pooled_k[:, lanes] / math.sqrt(BS)

    def here(block):
        return (block >= base) & (block < base + plane)

    def tables():
        for h in range(2):
            after[h, plane] = plane
            after[h, plane + 1] = plane

            def link(o, c):
                d = plane - 1 - o
                after[h, d] = jnp.where(here(partner[h, across + d]), d, after[h, d + 1])
                return c

            lax.fori_loop(0, plane, link, 0)

    def count(h):
        def add(d, n):
            return n + jnp.where(here(partner[h, across + d]), 1, 0)

        return lax.fori_loop(0, plane, add, 0)

    def to_column(seq, head):
        rows = pl.ds(2 * g, 2)
        for kind in (p, 2 + p):
            remote(col.at[kind, rows], col.at[kind, rows], col_send, col_recv, seq, head).start()

    bias_copy = remote(bias.at[1], bias.at[0], bias_send, bias_recv, mirror)

    def spread(h):
        lanes = pl.ds(h * DH, DH)
        pltpu.make_async_copy(kv.at[i, :, lanes], own[h].at[i], spread_recv.at[h]).start()
        each_peer(
            lambda j, d: remote(
                kv.at[j, :, lanes], own[h].at[i], spread_send.at[h], spread_recv.at[h], d
            ).start()
        )

    def hand_on():
        @pl.when(i < plane - 1)
        def _():
            for h in range(2):
                lanes = pl.ds(h * DH, DH)
                remote(
                    kv.at[:, :, lanes], prev.at[h], prev_send.at[h], prev_recv.at[h], s + 1
                ).start()

    def exchange(h):
        return remote(pack[h], slot[h], z_send.at[h], z_recv.at[h], mirror)

    def edge_copy(h):
        return remote(own[h].at[plane - 1], edge.at[h], edge_send.at[h], edge_recv.at[h], mirror)

    def spread_done(h):
        bytes_wait(own[h], spread_recv.at[h])

    def fill(h):
        def take(k, at):
            d = after[h, at]
            block = partner[h, across + jnp.minimum(d, plane - 1)]
            pack[h][k] = own[h][jnp.clip(block - base, 0, plane - 1)]
            return d + 1

        lax.fori_loop(0, slots, take, 0)

    def give_back(h):
        bytes_wait(slot[h], z_recv.at[h])

        def choose(j, taken):
            block = partner[h, base + j]
            near = here(block)
            mine = own[h][jnp.clip(block - base, 0, plane - 1)]
            theirs = slot[h][jnp.minimum(taken, slots - 1)]
            pick[h, j] = jnp.where(near, mine, theirs)
            return taken + jnp.where(near, 0, 1)

        lax.fori_loop(0, plane, choose, 0)
        each_peer(
            lambda j, d: remote(
                pick.at[h, j], part.at[h, i], back_send.at[h], back_recv.at[h], d
            ).start()
        )
        pltpu.make_async_copy(pick.at[h, i], part.at[h, i], back_recv.at[h]).start()

        @pl.when(s == plane)
        def _():
            bytes_wait(edge.at[h], edge_recv.at[h])
            pltpu.make_async_copy(edge.at[h], prev.at[h, 0], prev_recv.at[h]).start()

        @pl.when(s > plane)
        def _():
            bytes_wait(edge.at[h], edge_recv.at[h])
            remote(edge.at[h], prev.at[h, i], extra_send.at[h], prev_recv.at[h], base).start()

    def query(h):
        return qs[:, :, h * DH : (h + 1) * DH].reshape(BS, DH)

    def scored(h, key):
        x = lax.dot_general(
            query(h), key, (((1,), (1,)), ((), ())), preferred_element_type=jnp.float32
        )
        return x * inv_scale

    def stacked(ref, h):
        return (
            ref[h, 0:half].reshape(BS, DH),
            ref[h, half:plane].reshape(BS, DH),
        )

    def local():
        for h in range(2):
            lanes = slice(h * DH, (h + 1) * DH)
            x = scored(h, kv[0:half, :, lanes].reshape(BS, DH))
            top = jnp.max(x, axis=1, keepdims=True)
            e = jnp.exp(x - top)
            top_all[h] = top
            den_all[h] = jnp.sum(e, axis=1, keepdims=True)
            mix_all[h] = jnp.dot(
                e.astype(jnp.bfloat16),
                kv[half:plane, :, lanes].reshape(BS, DH),
                preferred_element_type=jnp.float32,
            )

    def merged(h, ref, shift):
        key, val = stacked(ref, h)
        x = scored(h, key)
        if shift is not None:
            x = x + shift
        old = top_all[h]
        top = jnp.maximum(old, jnp.max(x, axis=1, keepdims=True))
        keep = jnp.exp(old - top)
        e = jnp.exp(x - top)
        den = den_all[h] * keep + jnp.sum(e, axis=1, keepdims=True)
        mix = mix_all[h] * keep + jnp.dot(
            e.astype(jnp.bfloat16), val, preferred_element_type=jnp.float32
        )
        return top, den, mix

    def previous(h):
        top, den, mix = merged(h, prev, None)
        top_all[h] = top
        den_all[h] = den
        mix_all[h] = mix

    def early_previous():
        @pl.when(i > 0)
        def _():
            for h in range(2):
                bytes_wait(prev.at[h], prev_recv.at[h])
                previous(h)

    def late_previous(h):
        @pl.when(s == plane)
        def _():
            bytes_wait(prev.at[h], prev_recv.at[h])
            previous(h)

    def finish(h):
        late_previous(h)
        bytes_wait(part.at[h], back_recv.at[h])
        _, den, mix = merged(h, part, bias[0, h : h + 1, 0:1])
        out[:, h * DH : (h + 1) * DH] = (mix * (1.0 / den)).astype(jnp.bfloat16)

    def owned():
        mine = i // stride
        each_peer(
            lambda j, d: remote(
                partial.at[mine], partial.at[mine], partial_send, partial_recv, d
            ).start()
        )

    def scores():
        queries = jnp.concatenate([feat[:, 0, 0, :], feat[:, 1, 0, :]], axis=0)
        keys = jnp.concatenate([feat[:, 2, 0, :], feat[:, 3, 0, :]], axis=0)
        x = lax.dot_general(
            queries,
            keys,
            (((1,), (1,)), ((), ())),
            precision=HIGHEST,
            preferred_element_type=jnp.float32,
        )
        x = x * (SHARPNESS / math.sqrt(2 * DH * groups))
        partial[i // stride, :, 0 : 2 * plane] = x[0:plane]
        partial[i // stride, :, 2 * plane : 4 * plane] = x[plane : 2 * plane]

    def sinkhorn():
        both = jnp.sum(partial[...], axis=0)
        x = jnp.concatenate([both[:, 0 : 2 * plane], both[:, 2 * plane : 4 * plane]], axis=0)

        def sweep(_, x):
            for along in (1, 0):
                top = jnp.max(x, axis=along, keepdims=True)
                x = x - (top + jnp.log(jnp.sum(jnp.exp(x - top), axis=along, keepdims=True)))
            return x

        x = lax.fori_loop(0, SINK_ITERS, sweep, x)
        row = lax.broadcasted_iota(jnp.int32, x.shape, 0)
        col = lax.broadcasted_iota(jnp.int32, x.shape, 1)
        for which, block in ((0, s), (1, mirror)):
            for h in range(2):
                chosen = (row == i + which * plane) & (col == partner[h, block])
                value = jnp.sum(
                    jnp.sum(jnp.where(chosen, x, 0.0), axis=1, keepdims=True), axis=0, keepdims=True
                )
                bias[which, h : h + 1, :] = jnp.broadcast_to(
                    value + math.log(2 * plane), (1, DH)
                )
            bias[which, 2:3, :] = jnp.max(counts[...], axis=0)

    @pl.when(p == 0)
    def _():
        most = jnp.maximum(count(0), count(1))
        counts[g] = jnp.full((1, DH), most, jnp.int32).astype(jnp.float32)
        pl.semaphore_wait(barrier, plane - 1 + groups - 1)
        each_group(lambda og: to_column(s, og))
        each_group(
            lambda og: remote(
                counts.at[g], counts.at[g], count_send, count_recv, s, og
            ).start()
        )
        spread(0)
        spread(1)
        hand_on()
        tables()
        local()
        spread_done(0)
        fill(0)
        pl.semaphore_wait(ready, 1)
        edge_copy(0).start()
        exchange(0).start()
        bytes_wait(feat.at[pl.ds(0, 2 * groups - 1)], col_recv)

        def to_owner(sl, c):
            owner = sl * stride

            @pl.when(owner != i)
            def _():
                remote(col.at[:, sl], feat.at[i], feat_send, feat_recv, base + owner).start()

            @pl.when(owner == i)
            def _():
                pltpu.make_async_copy(col.at[:, sl], feat.at[i], feat_recv).start()

            return c

        lax.fori_loop(0, slices, to_owner, 0)
        spread_done(1)
        fill(1)
        edge_copy(1).start()
        exchange(1).start()

        @pl.when(i % stride == 0)
        def _():
            bytes_wait(feat, feat_recv)
            scores()
            owned()

        early_previous()
        bytes_wait(counts.at[pl.ds(0, groups - 1)], count_recv)

        @pl.when(i % stride == 0)
        def _():
            bytes_wait(partial.at[pl.ds(0, slices - 1)], partial_recv)
            bytes_wait(feat.at[pl.ds(0, slices - 1)], feat_send)

        @pl.when(i % stride != 0)
        def _():
            bytes_wait(partial, partial_recv)
            bytes_wait(feat.at[pl.ds(0, slices)], feat_send)

        sinkhorn()
        crowd[...] = bias[0, 2:3, :]
        bias_copy.start()
        give_back(0)
        finish(0)
        give_back(1)
        finish(1)
        bytes_wait(col.at[pl.ds(0, 2), pl.ds(0, 2 * (groups - 1))], col_send)

        @pl.when(i % stride == 0)
        def _():
            for _ in range(plane - 1):
                bytes_wait(partial.at[0], partial_send)

        bytes_wait(counts.at[pl.ds(0, groups - 1)], count_send)
        for h in range(2):
            edge_copy(h).wait_send()
        bias_copy.wait_send()

    @pl.when(p == 1)
    def _():
        pl.semaphore_wait(barrier, plane - 1 + groups)
        signal(ready, mirror)
        for og in range(groups):
            to_column(mirror, og)
        spread(0)
        spread(1)
        hand_on()
        tables()
        for h in range(2):
            spread_done(h)
            fill(h)
            exchange(h).start()
        local()
        early_previous()
        give_back(0)
        give_back(1)
        bias_copy.wait_recv()
        crowd[...] = bias[0, 2:3, :]
        finish(0)
        finish(1)
        bytes_wait(col.at[pl.ds(0, 2), pl.ds(0, slices)], col_send)

    for h in range(2):
        bytes_wait(own[h].at[pl.ds(0, plane - 1)], spread_send.at[h])
        bytes_wait(pick.at[h, pl.ds(0, plane - 1)], back_send.at[h])
        exchange(h).wait_send()

    @pl.when(i < plane - 1)
    def _():
        for h in range(2):
            bytes_wait(prev.at[h], prev_send.at[h])

    @pl.when(s > plane)
    def _():
        for h in range(2):
            bytes_wait(edge.at[h], extra_send.at[h])


def attention(plane, groups, slots, collective_id, name):
    piece = 2 * BS // plane
    seq = 2 * plane
    half = plane // 2
    width = 2 * DH
    slices = 2 * groups
    dma = pltpu.SemaphoreType.DMA
    hbm = pl.BlockSpec(memory_space=pl.ANY)
    vmem = pl.BlockSpec(memory_space=pltpu.VMEM)
    folded = (half, piece, width)
    one, two = dma(()), dma((2,))
    pieces = pltpu.VMEM((2, plane, piece, DH), jnp.bfloat16)
    head_pieces = pltpu.VMEM((plane, piece, DH), jnp.bfloat16)
    head_slots = pltpu.VMEM((slots, piece, DH), jnp.bfloat16)

    def call(queries, keys, values, partner):
        return pl.pallas_call(
            functools.partial(sparse_attention_kernel, plane, groups, slots),
            out_shape=(
                jax.ShapeDtypeStruct(queries.shape, queries.dtype),
                jax.ShapeDtypeStruct((1, DH), jnp.float32),
            ),
            in_specs=[pl.BlockSpec(memory_space=pltpu.SMEM), hbm, hbm, hbm],
            out_specs=(vmem, vmem),
            scratch_shapes=[
                pltpu.VMEM(folded, jnp.bfloat16),
                pltpu.VMEM((plane, piece, width), jnp.bfloat16),
                head_pieces,
                head_pieces,
                head_slots,
                head_slots,
                head_slots,
                head_slots,
                pltpu.VMEM((2, piece, DH), jnp.bfloat16),
                pieces,
                pieces,
                pieces,
                pltpu.VMEM((4, slices, 1, DH), jnp.float32),
                pltpu.VMEM((plane, 4, 1, DH), jnp.float32),
                pltpu.VMEM((slices, plane, max(DH, 2 * seq)), jnp.float32),
                pltpu.VMEM((groups, 1, DH), jnp.float32),
                pltpu.VMEM((2, 3, DH), jnp.float32),
                pltpu.VMEM((2, BS, 1), jnp.float32),
                pltpu.VMEM((2, BS, 1), jnp.float32),
                pltpu.VMEM((2, BS, DH), jnp.float32),
                pltpu.SMEM((2, plane + 2), jnp.int32),
                dma((3,)),
            ]
            + [one] * 10
            + [two] * 11
            + [pltpu.SemaphoreType.REGULAR],
            compiler_params=pltpu.CompilerParams(
                collective_id=collective_id, has_side_effects=True
            ),
            name=name,
        )(partner, queries.reshape(folded), keys.reshape(folded), values.reshape(folded))

    return call


def solution(mesh):
    seq, groups = mesh.shape["seq"], mesh.shape["head"]
    plane = seq // 2
    whole = attention(plane, groups, plane, 0, "whole")

    def body(queries, keys, values, partner):
        return whole(queries, keys, values, partner)[0]

    return jax.shard_map(
        body,
        mesh=mesh,
        in_specs=(P("seq", "head"), P("seq", "head"), P("seq", "head"), P("head", None)),
        out_specs=P("seq", "head"),
        check_vma=False,
    )
```

```python
import functools
import math

import jax
import jax.numpy as jnp
from jax import lax
from jax.experimental import pallas as pl
from jax.experimental.pallas import tpu as pltpu
from jax.sharding import PartitionSpec as P

DH = 128
BS = 256
SINK_ITERS = 8
SHARPNESS = 2.0
SLOT_SHARE = 22
HIGHEST = lax.Precision.HIGHEST
MESH = pl.DeviceIdType.MESH


def bytes_wait(ref, sem):
    pltpu.make_async_copy(ref, ref, sem).wait()


def sparse_attention_kernel(
    plane,
    groups,
    slots,
    partner,
    q_hbm,
    k_hbm,
    v_hbm,
    out,
    crowd,
    qs,
    kv,
    own_a,
    own_b,
    pack_a,
    pack_b,
    slot_a,
    slot_b,
    edge,
    pick,
    part,
    prev,
    col,
    feat,
    partial,
    counts,
    bias,
    top_all,
    den_all,
    mix_all,
    after,
    load_sem,
    col_send,
    col_recv,
    count_send,
    count_recv,
    feat_send,
    feat_recv,
    partial_send,
    partial_recv,
    bias_send,
    bias_recv,
    spread_send,
    spread_recv,
    z_send,
    z_recv,
    edge_send,
    edge_recv,
    back_send,
    back_recv,
    prev_send,
    extra_send,
    prev_recv,
    ready,
):
    own = (own_a, own_b)
    pack = (pack_a, pack_b)
    slot = (slot_a, slot_b)
    s = lax.axis_index("seq")
    g = lax.axis_index("head")
    p = s // plane
    i = s % plane
    base = p * plane
    mirror = (s + plane) % (2 * plane)
    half = plane // 2
    across = plane - base
    slices = 2 * groups
    stride = plane // slices
    inv_scale = 1.0 / math.sqrt(DH)

    def remote(src, dst, ss, rs, seq, head=None):
        return pltpu.make_async_remote_copy(
            src_ref=src,
            dst_ref=dst,
            send_sem=ss,
            recv_sem=rs,
            device_id=(seq, g if head is None else head),
            device_id_type=MESH,
        )

    def signal(sem, seq, head=None):
        pl.semaphore_signal(
            sem,
            inc=1,
            device_id=(seq, g if head is None else head),
            device_id_type=MESH,
        )

    def each_peer(body):
        def wrapped(o, c):
            j = (i + o) % plane
            body(j, base + j)
            return c

        lax.fori_loop(1, plane, wrapped, 0)

    def each_group(body):
        def wrapped(o, c):
            body((g + o) % groups)
            return c

        lax.fori_loop(1, groups, wrapped, 0)

    barrier = pltpu.get_barrier_semaphore()

    @pl.when(p == 0)
    def _():
        for og in range(groups):
            signal(barrier, mirror, og)
        each_group(lambda og: signal(barrier, s, og))

    each_peer(lambda j, d: signal(barrier, d))

    loads = (
        pltpu.make_async_copy(q_hbm, qs, load_sem.at[0]),
        pltpu.make_async_copy(k_hbm, kv.at[pl.ds(0, half)], load_sem.at[1]),
        pltpu.make_async_copy(v_hbm, kv.at[pl.ds(half, half)], load_sem.at[2]),
    )
    for c in loads:
        c.start()
    for c in loads:
        c.wait()
    pooled_q = jnp.sum(jnp.sum(qs[...].astype(jnp.float32), axis=0), axis=0, keepdims=True)
    pooled_k = jnp.sum(
        jnp.sum(kv[pl.ds(0, half)].astype(jnp.float32), axis=0), axis=0, keepdims=True
    )
    for h in range(2):
        lanes = slice(h * DH, (h + 1) * DH)
        col[p, 2 * g + h] = pooled_q[:, lanes] / math.sqrt(BS)
        col[2 + p, 2 * g + h] = pooled_k[:, lanes] / math.sqrt(BS)

    def here(block):
        return (block >= base) & (block < base + plane)

    def tables():
        for h in range(2):
            after[h, plane] = plane
            after[h, plane + 1] = plane

            def link(o, c):
                d = plane - 1 - o
                after[h, d] = jnp.where(here(partner[h, across + d]), d, after[h, d + 1])
                return c

            lax.fori_loop(0, plane, link, 0)

    def count(h):
        def add(d, n):
            return n + jnp.where(here(partner[h, across + d]), 1, 0)

        return lax.fori_loop(0, plane, add, 0)

    def to_column(seq, head):
        rows = pl.ds(2 * g, 2)
        for kind in (p, 2 + p):
            remote(col.at[kind, rows], col.at[kind, rows], col_send, col_recv, seq, head).start()

    bias_copy = remote(bias.at[1], bias.at[0], bias_send, bias_recv, mirror)

    def spread(h):
        lanes = pl.ds(h * DH, DH)
        pltpu.make_async_copy(kv.at[i, :, lanes], own[h].at[i], spread_recv.at[h]).start()
        each_peer(
            lambda j, d: remote(
                kv.at[j, :, lanes], own[h].at[i], spread_send.at[h], spread_recv.at[h], d
            ).start()
        )

    def hand_on():
        @pl.when(i < plane - 1)
        def _():
            for h in range(2):
                lanes = pl.ds(h * DH, DH)
                remote(
                    kv.at[:, :, lanes], prev.at[h], prev_send.at[h], prev_recv.at[h], s + 1
                ).start()

    def exchange(h):
        return remote(pack[h], slot[h], z_send.at[h], z_recv.at[h], mirror)

    def edge_copy(h):
        return remote(own[h].at[plane - 1], edge.at[h], edge_send.at[h], edge_recv.at[h], mirror)

    def spread_done(h):
        bytes_wait(own[h], spread_recv.at[h])

    def fill(h):
        def take(k, at):
            d = after[h, at]
            block = partner[h, across + jnp.minimum(d, plane - 1)]
            pack[h][k] = own[h][jnp.clip(block - base, 0, plane - 1)]
            return d + 1

        lax.fori_loop(0, slots, take, 0)

    def give_back(h):
        bytes_wait(slot[h], z_recv.at[h])

        def choose(j, taken):
            block = partner[h, base + j]
            near = here(block)
            mine = own[h][jnp.clip(block - base, 0, plane - 1)]
            theirs = slot[h][jnp.minimum(taken, slots - 1)]
            pick[h, j] = jnp.where(near, mine, theirs)
            return taken + jnp.where(near, 0, 1)

        lax.fori_loop(0, plane, choose, 0)
        each_peer(
            lambda j, d: remote(
                pick.at[h, j], part.at[h, i], back_send.at[h], back_recv.at[h], d
            ).start()
        )
        pltpu.make_async_copy(pick.at[h, i], part.at[h, i], back_recv.at[h]).start()

        @pl.when(s == plane)
        def _():
            bytes_wait(edge.at[h], edge_recv.at[h])
            pltpu.make_async_copy(edge.at[h], prev.at[h, 0], prev_recv.at[h]).start()

        @pl.when(s > plane)
        def _():
            bytes_wait(edge.at[h], edge_recv.at[h])
            remote(edge.at[h], prev.at[h, i], extra_send.at[h], prev_recv.at[h], base).start()

    def query(h):
        return qs[:, :, h * DH : (h + 1) * DH].reshape(BS, DH)

    def scored(h, key):
        x = lax.dot_general(
            query(h), key, (((1,), (1,)), ((), ())), preferred_element_type=jnp.float32
        )
        return x * inv_scale

    def stacked(ref, h):
        return (
            ref[h, 0:half].reshape(BS, DH),
            ref[h, half:plane].reshape(BS, DH),
        )

    def local():
        for h in range(2):
            lanes = slice(h * DH, (h + 1) * DH)
            x = scored(h, kv[0:half, :, lanes].reshape(BS, DH))
            top = jnp.max(x, axis=1, keepdims=True)
            e = jnp.exp(x - top)
            top_all[h] = top
            den_all[h] = jnp.sum(e, axis=1, keepdims=True)
            mix_all[h] = jnp.dot(
                e.astype(jnp.bfloat16),
                kv[half:plane, :, lanes].reshape(BS, DH),
                preferred_element_type=jnp.float32,
            )

    def merged(h, ref, shift):
        key, val = stacked(ref, h)
        x = scored(h, key)
        if shift is not None:
            x = x + shift
        old = top_all[h]
        top = jnp.maximum(old, jnp.max(x, axis=1, keepdims=True))
        keep = jnp.exp(old - top)
        e = jnp.exp(x - top)
        den = den_all[h] * keep + jnp.sum(e, axis=1, keepdims=True)
        mix = mix_all[h] * keep + jnp.dot(
            e.astype(jnp.bfloat16), val, preferred_element_type=jnp.float32
        )
        return top, den, mix

    def previous(h):
        top, den, mix = merged(h, prev, None)
        top_all[h] = top
        den_all[h] = den
        mix_all[h] = mix

    def early_previous():
        @pl.when(i > 0)
        def _():
            for h in range(2):
                bytes_wait(prev.at[h], prev_recv.at[h])
                previous(h)

    def late_previous(h):
        @pl.when(s == plane)
        def _():
            bytes_wait(prev.at[h], prev_recv.at[h])
            previous(h)

    def finish(h):
        late_previous(h)
        bytes_wait(part.at[h], back_recv.at[h])
        _, den, mix = merged(h, part, bias[0, h : h + 1, 0:1])
        out[:, h * DH : (h + 1) * DH] = (mix * (1.0 / den)).astype(jnp.bfloat16)

    def owned():
        mine = i // stride
        each_peer(
            lambda j, d: remote(
                partial.at[mine], partial.at[mine], partial_send, partial_recv, d
            ).start()
        )

    def scores():
        queries = jnp.concatenate([feat[:, 0, 0, :], feat[:, 1, 0, :]], axis=0)
        keys = jnp.concatenate([feat[:, 2, 0, :], feat[:, 3, 0, :]], axis=0)
        x = lax.dot_general(
            queries,
            keys,
            (((1,), (1,)), ((), ())),
            precision=HIGHEST,
            preferred_element_type=jnp.float32,
        )
        x = x * (SHARPNESS / math.sqrt(2 * DH * groups))
        partial[i // stride, :, 0 : 2 * plane] = x[0:plane]
        partial[i // stride, :, 2 * plane : 4 * plane] = x[plane : 2 * plane]

    def sinkhorn():
        both = jnp.sum(partial[...], axis=0)
        x = jnp.concatenate([both[:, 0 : 2 * plane], both[:, 2 * plane : 4 * plane]], axis=0)

        def sweep(_, x):
            for along in (1, 0):
                top = jnp.max(x, axis=along, keepdims=True)
                x = x - (top + jnp.log(jnp.sum(jnp.exp(x - top), axis=along, keepdims=True)))
            return x

        x = lax.fori_loop(0, SINK_ITERS, sweep, x)
        row = lax.broadcasted_iota(jnp.int32, x.shape, 0)
        col = lax.broadcasted_iota(jnp.int32, x.shape, 1)
        for which, block in ((0, s), (1, mirror)):
            for h in range(2):
                chosen = (row == i + which * plane) & (col == partner[h, block])
                value = jnp.sum(
                    jnp.sum(jnp.where(chosen, x, 0.0), axis=1, keepdims=True), axis=0, keepdims=True
                )
                bias[which, h : h + 1, :] = jnp.broadcast_to(
                    value + math.log(2 * plane), (1, DH)
                )
            bias[which, 2:3, :] = jnp.max(counts[...], axis=0)

    @pl.when(p == 0)
    def _():
        most = jnp.maximum(count(0), count(1))
        counts[g] = jnp.full((1, DH), most, jnp.int32).astype(jnp.float32)
        pl.semaphore_wait(barrier, plane - 1 + groups - 1)
        each_group(lambda og: to_column(s, og))
        each_group(
            lambda og: remote(
                counts.at[g], counts.at[g], count_send, count_recv, s, og
            ).start()
        )
        spread(0)
        spread(1)
        hand_on()
        tables()
        local()
        spread_done(0)
        fill(0)
        pl.semaphore_wait(ready, 1)
        edge_copy(0).start()
        exchange(0).start()
        bytes_wait(feat.at[pl.ds(0, 2 * groups - 1)], col_recv)

        def to_owner(sl, c):
            owner = sl * stride

            @pl.when(owner != i)
            def _():
                remote(col.at[:, sl], feat.at[i], feat_send, feat_recv, base + owner).start()

            @pl.when(owner == i)
            def _():
                pltpu.make_async_copy(col.at[:, sl], feat.at[i], feat_recv).start()

            return c

        lax.fori_loop(0, slices, to_owner, 0)
        spread_done(1)
        fill(1)
        edge_copy(1).start()
        exchange(1).start()

        @pl.when(i % stride == 0)
        def _():
            bytes_wait(feat, feat_recv)
            scores()
            owned()

        early_previous()
        bytes_wait(counts.at[pl.ds(0, groups - 1)], count_recv)

        @pl.when(i % stride == 0)
        def _():
            bytes_wait(partial.at[pl.ds(0, slices - 1)], partial_recv)
            bytes_wait(feat.at[pl.ds(0, slices - 1)], feat_send)

        @pl.when(i % stride != 0)
        def _():
            bytes_wait(partial, partial_recv)
            bytes_wait(feat.at[pl.ds(0, slices)], feat_send)

        sinkhorn()
        crowd[...] = bias[0, 2:3, :]
        bias_copy.start()
        give_back(0)
        give_back(1)
        finish(0)
        finish(1)
        bytes_wait(col.at[pl.ds(0, 2), pl.ds(0, 2 * (groups - 1))], col_send)

        @pl.when(i % stride == 0)
        def _():
            for _ in range(plane - 1):
                bytes_wait(partial.at[0], partial_send)

        bytes_wait(counts.at[pl.ds(0, groups - 1)], count_send)
        for h in range(2):
            edge_copy(h).wait_send()
        bias_copy.wait_send()

    @pl.when(p == 1)
    def _():
        pl.semaphore_wait(barrier, plane - 1 + groups)
        signal(ready, mirror)
        for og in range(groups):
            to_column(mirror, og)
        spread(0)
        spread(1)
        hand_on()
        tables()
        for h in range(2):
            spread_done(h)
            fill(h)
            exchange(h).start()
        local()
        early_previous()
        give_back(0)
        give_back(1)
        bias_copy.wait_recv()
        crowd[...] = bias[0, 2:3, :]
        finish(0)
        finish(1)
        bytes_wait(col.at[pl.ds(0, 2), pl.ds(0, slices)], col_send)

    for h in range(2):
        bytes_wait(own[h].at[pl.ds(0, plane - 1)], spread_send.at[h])
        bytes_wait(pick.at[h, pl.ds(0, plane - 1)], back_send.at[h])
        exchange(h).wait_send()

    @pl.when(i < plane - 1)
    def _():
        for h in range(2):
            bytes_wait(prev.at[h], prev_send.at[h])

    @pl.when(s > plane)
    def _():
        for h in range(2):
            bytes_wait(edge.at[h], extra_send.at[h])


def attention(plane, groups, slots, collective_id, name):
    piece = 2 * BS // plane
    seq = 2 * plane
    half = plane // 2
    width = 2 * DH
    slices = 2 * groups
    dma = pltpu.SemaphoreType.DMA
    hbm = pl.BlockSpec(memory_space=pl.ANY)
    vmem = pl.BlockSpec(memory_space=pltpu.VMEM)
    folded = (half, piece, width)
    one, two = dma(()), dma((2,))
    pieces = pltpu.VMEM((2, plane, piece, DH), jnp.bfloat16)
    head_pieces = pltpu.VMEM((plane, piece, DH), jnp.bfloat16)
    head_slots = pltpu.VMEM((slots, piece, DH), jnp.bfloat16)

    def call(queries, keys, values, partner):
        return pl.pallas_call(
            functools.partial(sparse_attention_kernel, plane, groups, slots),
            out_shape=(
                jax.ShapeDtypeStruct(queries.shape, queries.dtype),
                jax.ShapeDtypeStruct((1, DH), jnp.float32),
            ),
            in_specs=[pl.BlockSpec(memory_space=pltpu.SMEM), hbm, hbm, hbm],
            out_specs=(vmem, vmem),
            scratch_shapes=[
                pltpu.VMEM(folded, jnp.bfloat16),
                pltpu.VMEM((plane, piece, width), jnp.bfloat16),
                head_pieces,
                head_pieces,
                head_slots,
                head_slots,
                head_slots,
                head_slots,
                pltpu.VMEM((2, piece, DH), jnp.bfloat16),
                pieces,
                pieces,
                pieces,
                pltpu.VMEM((4, slices, 1, DH), jnp.float32),
                pltpu.VMEM((plane, 4, 1, DH), jnp.float32),
                pltpu.VMEM((slices, plane, max(DH, 2 * seq)), jnp.float32),
                pltpu.VMEM((groups, 1, DH), jnp.float32),
                pltpu.VMEM((2, 3, DH), jnp.float32),
                pltpu.VMEM((2, BS, 1), jnp.float32),
                pltpu.VMEM((2, BS, 1), jnp.float32),
                pltpu.VMEM((2, BS, DH), jnp.float32),
                pltpu.SMEM((2, plane + 2), jnp.int32),
                dma((3,)),
            ]
            + [one] * 10
            + [two] * 11
            + [pltpu.SemaphoreType.REGULAR],
            compiler_params=pltpu.CompilerParams(
                collective_id=collective_id, has_side_effects=True
            ),
            name=name,
        )(partner, queries.reshape(folded), keys.reshape(folded), values.reshape(folded))

    return call


def solution(mesh):
    seq, groups = mesh.shape["seq"], mesh.shape["head"]
    plane = seq // 2
    slots = plane * SLOT_SHARE // 32
    packed = attention(plane, groups, slots, 0, "packed")
    whole = attention(plane, groups, plane, 1, "whole")

    def body(queries, keys, values, partner):
        attended, crowd = packed(queries, keys, values, partner)
        return lax.cond(
            crowd[0, 0] > slots,
            lambda: whole(queries, keys, values, partner)[0],
            lambda: attended,
        )

    return jax.shard_map(
        body,
        mesh=mesh,
        in_specs=(P("seq", "head"), P("seq", "head"), P("seq", "head"), P("head", None)),
        out_specs=P("seq", "head"),
        check_vma=False,
    )
```

```python
import functools
import math

import jax
import jax.numpy as jnp
from jax import lax
from jax.experimental import pallas as pl
from jax.experimental.pallas import tpu as pltpu
from jax.sharding import PartitionSpec as P

DH = 128
BS = 256
SINK_ITERS = 8
SHARPNESS = 2.0
SLOT_SHARE = 22
TURNS = ((3, 1), (5, 1), (7, 1), )
HIGHEST = lax.Precision.HIGHEST
MESH = pl.DeviceIdType.MESH


def farther(at, k):
    return (at + jnp.where(k == 3, 0, jnp.where(k == 0, 2, 2 * k - 1))) % 4


def bytes_wait(ref, sem):
    pltpu.make_async_copy(ref, ref, sem).wait()


def sparse_attention_kernel(
    plane,
    groups,
    slots,
    partner_hbm,
    q_hbm,
    k_hbm,
    v_hbm,
    out,
    crowd,
    qs,
    kv,
    own_a,
    own_b,
    pack_a,
    pack_b,
    slot_a,
    slot_b,
    edge,
    pick,
    part,
    prev,
    col,
    feat,
    partial,
    counts,
    bias,
    top_all,
    den_all,
    mix_all,
    after,
    partner,
    load_sem,
    col_send,
    col_recv,
    count_send,
    count_recv,
    feat_send,
    feat_recv,
    partial_send,
    partial_recv,
    bias_send,
    bias_recv,
    spread_send,
    spread_recv,
    z_send,
    z_recv,
    edge_send,
    edge_recv,
    back_send,
    back_recv,
    prev_send,
    extra_send,
    prev_recv,
    ready,
    turn,
):
    own = (own_a, own_b)
    pack = (pack_a, pack_b)
    slot = (slot_a, slot_b)
    s = lax.axis_index("seq")
    g = lax.axis_index("head")
    p = s // plane
    i = s % plane
    base = p * plane
    mirror = (s + plane) % (2 * plane)
    half = plane // 2
    across = plane - base
    slices = 2 * groups
    stride = plane // slices
    inv_scale = 1.0 / math.sqrt(DH)

    def remote(src, dst, ss, rs, seq, head=None):
        return pltpu.make_async_remote_copy(
            src_ref=src,
            dst_ref=dst,
            send_sem=ss,
            recv_sem=rs,
            device_id=(seq, g if head is None else head),
            device_id_type=MESH,
        )

    def signal(sem, seq, head=None):
        pl.semaphore_signal(
            sem,
            inc=1,
            device_id=(seq, g if head is None else head),
            device_id_type=MESH,
        )

    def each_peer(body):
        def wrapped(o, c):
            j = (farther(i // 8, o // 8) * 4 + farther(i // 2 % 4, o // 2 % 4)) * 2
            j = j + (i + o + 1) % 2
            body(j, base + j)
            return c

        lax.fori_loop(0, plane - 1, wrapped, 0)

    def each_group(body):
        def wrapped(o, c):
            body((g + o) % groups)
            return c

        lax.fori_loop(1, groups, wrapped, 0)

    turns = [(f, l) for f, l in TURNS if f < groups]
    barrier = pltpu.get_barrier_semaphore()

    @pl.when(p == 0)
    def _():
        for og in range(groups):
            signal(barrier, mirror, og)
        each_group(lambda og: signal(barrier, s, og))

    for follower, leader in turns:

        @pl.when((p == 1) & (g == follower))
        def _():
            signal(barrier, s, leader)

    each_peer(lambda j, d: signal(barrier, d))

    loads = (
        pltpu.make_async_copy(partner_hbm, partner, load_sem.at[3]),
        pltpu.make_async_copy(q_hbm, qs, load_sem.at[0]),
        pltpu.make_async_copy(k_hbm, kv.at[pl.ds(0, half)], load_sem.at[1]),
        pltpu.make_async_copy(v_hbm, kv.at[pl.ds(half, half)], load_sem.at[2]),
    )
    for c in loads:
        c.start()
    for c in loads:
        c.wait()
    pooled_q = jnp.sum(jnp.sum(qs[...].astype(jnp.float32), axis=0), axis=0, keepdims=True)
    pooled_k = jnp.sum(
        jnp.sum(kv[pl.ds(0, half)].astype(jnp.float32), axis=0), axis=0, keepdims=True
    )
    for h in range(2):
        lanes = slice(h * DH, (h + 1) * DH)
        col[p, 2 * g + h] = pooled_q[:, lanes] / math.sqrt(BS)
        col[2 + p, 2 * g + h] = pooled_k[:, lanes] / math.sqrt(BS)

    def here(block):
        return (block >= base) & (block < base + plane)

    def tables():
        for h in range(2):
            after[h, plane] = plane
            after[h, plane + 1] = plane

            def link(o, c):
                d = plane - 1 - o
                after[h, d] = jnp.where(here(partner[h, across + d]), d, after[h, d + 1])
                return c

            lax.fori_loop(0, plane, link, 0)

    def count(h):
        def add(d, n):
            return n + jnp.where(here(partner[h, across + d]), 1, 0)

        return lax.fori_loop(0, plane, add, 0)

    def to_column(seq, head):
        rows = pl.ds(2 * g, 2)
        for kind in (p, 2 + p):
            remote(col.at[kind, rows], col.at[kind, rows], col_send, col_recv, seq, head).start()

    bias_copy = remote(bias.at[1], bias.at[0], bias_send, bias_recv, mirror)

    def spread(h):
        lanes = pl.ds(h * DH, DH)
        pltpu.make_async_copy(kv.at[i, :, lanes], own[h].at[i], spread_recv.at[h]).start()
        each_peer(
            lambda j, d: remote(
                kv.at[j, :, lanes], own[h].at[i], spread_send.at[h], spread_recv.at[h], d
            ).start()
        )

    def hand_on():
        @pl.when(i < plane - 1)
        def _():
            for h in range(2):
                lanes = pl.ds(h * DH, DH)
                remote(
                    kv.at[:, :, lanes], prev.at[h], prev_send.at[h], prev_recv.at[h], s + 1
                ).start()

    cuts = (0, slots - slots * 5 // 8, slots)

    def exchange(h, part_id):
        rows = pl.ds(cuts[part_id], cuts[part_id + 1] - cuts[part_id])
        sems = 2 * h + part_id
        return remote(
            pack[h].at[rows], slot[h].at[rows], z_send.at[sems], z_recv.at[sems], mirror
        )

    def exchange_start(h):
        exchange(h, 0).start()
        exchange(h, 1).start()

    def edge_copy(h):
        return remote(own[h].at[plane - 1], edge.at[h], edge_send.at[h], edge_recv.at[h], mirror)

    def spread_done(h):
        bytes_wait(own[h], spread_recv.at[h])

    def fill(h):
        def take(k, at):
            d = after[h, at]
            block = partner[h, across + jnp.minimum(d, plane - 1)]
            pack[h][k] = own[h][jnp.clip(block - base, 0, plane - 1)]
            return d + 1

        lax.fori_loop(0, slots, take, 0)

    def give_back(h):
        exchange(h, 0).wait_recv()
        exchange(h, 1).wait_recv()

        def choose(j, taken):
            block = partner[h, base + j]
            near = here(block)
            mine = own[h][jnp.clip(block - base, 0, plane - 1)]
            theirs = slot[h][jnp.minimum(taken, slots - 1)]
            pick[h, j] = jnp.where(near, mine, theirs)
            return taken + jnp.where(near, 0, 1)

        lax.fori_loop(0, plane, choose, 0)
        each_peer(
            lambda j, d: remote(
                pick.at[h, j], part.at[h, i], back_send.at[h], back_recv.at[h], d
            ).start()
        )
        pltpu.make_async_copy(pick.at[h, i], part.at[h, i], back_recv.at[h]).start()

        @pl.when(s == plane)
        def _():
            bytes_wait(edge.at[h], edge_recv.at[h])
            pltpu.make_async_copy(edge.at[h], prev.at[h, 0], prev_recv.at[h]).start()

        @pl.when(s > plane)
        def _():
            bytes_wait(edge.at[h], edge_recv.at[h])
            remote(edge.at[h], prev.at[h, i], extra_send.at[h], prev_recv.at[h], base).start()

    def query(h):
        return qs[:, :, h * DH : (h + 1) * DH].reshape(BS, DH)

    def scored(h, key):
        x = lax.dot_general(
            query(h), key, (((1,), (1,)), ((), ())), preferred_element_type=jnp.float32
        )
        return x * inv_scale

    def stacked(ref, h):
        return (
            ref[h, 0:half].reshape(BS, DH),
            ref[h, half:plane].reshape(BS, DH),
        )

    def local():
        for h in range(2):
            lanes = slice(h * DH, (h + 1) * DH)
            x = scored(h, kv[0:half, :, lanes].reshape(BS, DH))
            top = jnp.max(x, axis=1, keepdims=True)
            e = jnp.exp(x - top)
            top_all[h] = top
            den_all[h] = jnp.sum(e, axis=1, keepdims=True)
            mix_all[h] = jnp.dot(
                e.astype(jnp.bfloat16),
                kv[half:plane, :, lanes].reshape(BS, DH),
                preferred_element_type=jnp.float32,
            )

    def merged(h, ref, shift):
        key, val = stacked(ref, h)
        x = scored(h, key)
        if shift is not None:
            x = x + shift
        old = top_all[h]
        top = jnp.maximum(old, jnp.max(x, axis=1, keepdims=True))
        keep = jnp.exp(old - top)
        e = jnp.exp(x - top)
        den = den_all[h] * keep + jnp.sum(e, axis=1, keepdims=True)
        mix = mix_all[h] * keep + jnp.dot(
            e.astype(jnp.bfloat16), val, preferred_element_type=jnp.float32
        )
        return top, den, mix

    def previous(h):
        top, den, mix = merged(h, prev, None)
        top_all[h] = top
        den_all[h] = den
        mix_all[h] = mix

    def early_previous():
        @pl.when(i > 0)
        def _():
            for h in range(2):
                bytes_wait(prev.at[h], prev_recv.at[h])
                previous(h)

    def late_previous(h):
        @pl.when(s == plane)
        def _():
            bytes_wait(prev.at[h], prev_recv.at[h])
            previous(h)

    def finish(h):
        late_previous(h)
        bytes_wait(part.at[h], back_recv.at[h])
        _, den, mix = merged(h, part, bias[0, h : h + 1, 0:1])
        out[:, h * DH : (h + 1) * DH] = (mix * (1.0 / den)).astype(jnp.bfloat16)

    def owned():
        mine = i // stride
        each_peer(
            lambda j, d: remote(
                partial.at[mine], partial.at[mine], partial_send, partial_recv, d
            ).start()
        )

    def scores():
        queries = jnp.concatenate([feat[:, 0, 0, :], feat[:, 1, 0, :]], axis=0)
        keys = jnp.concatenate([feat[:, 2, 0, :], feat[:, 3, 0, :]], axis=0)
        x = lax.dot_general(
            queries,
            keys,
            (((1,), (1,)), ((), ())),
            precision=HIGHEST,
            preferred_element_type=jnp.float32,
        )
        x = x * (SHARPNESS / math.sqrt(2 * DH * groups))
        partial[i // stride, :, 0 : 2 * plane] = x[0:plane]
        partial[i // stride, :, 2 * plane : 4 * plane] = x[plane : 2 * plane]

    def sinkhorn():
        both = jnp.sum(partial[...], axis=0)
        x = jnp.concatenate([both[:, 0 : 2 * plane], both[:, 2 * plane : 4 * plane]], axis=0)

        def sweep(_, x):
            for along in (1, 0):
                top = jnp.max(x, axis=along, keepdims=True)
                x = x - (top + jnp.log(jnp.sum(jnp.exp(x - top), axis=along, keepdims=True)))
            return x

        x = lax.fori_loop(0, SINK_ITERS, sweep, x)
        row = lax.broadcasted_iota(jnp.int32, x.shape, 0)
        col = lax.broadcasted_iota(jnp.int32, x.shape, 1)
        for which, block in ((0, s), (1, mirror)):
            for h in range(2):
                chosen = (row == i + which * plane) & (col == partner[h, block])
                value = jnp.sum(
                    jnp.sum(jnp.where(chosen, x, 0.0), axis=1, keepdims=True), axis=0, keepdims=True
                )
                bias[which, h : h + 1, :] = jnp.broadcast_to(
                    value + math.log(2 * plane), (1, DH)
                )
            bias[which, 2:3, :] = jnp.max(counts[...], axis=0)

    @pl.when(p == 0)
    def _():
        most = jnp.maximum(count(0), count(1))
        counts[g] = jnp.full((1, DH), most, jnp.int32).astype(jnp.float32)
        pl.semaphore_wait(barrier, plane - 1 + groups - 1)
        each_group(lambda og: to_column(s, og))
        each_group(
            lambda og: remote(
                counts.at[g], counts.at[g], count_send, count_recv, s, og
            ).start()
        )
        spread(0)
        spread(1)
        hand_on()
        tables()
        local()
        spread_done(0)
        fill(0)
        pl.semaphore_wait(ready, 1)
        bytes_wait(feat.at[pl.ds(0, 2 * groups - 1)], col_recv)

        def to_owner(sl, c):
            owner = sl * stride

            @pl.when(owner != i)
            def _():
                remote(col.at[:, sl], feat.at[i], feat_send, feat_recv, base + owner).start()

            @pl.when(owner == i)
            def _():
                pltpu.make_async_copy(col.at[:, sl], feat.at[i], feat_recv).start()

            return c

        lax.fori_loop(0, slices, to_owner, 0)
        spread_done(1)
        fill(1)

        @pl.when(i % stride == 0)
        def _():
            bytes_wait(feat, feat_recv)
            scores()
            owned()

        for h in range(2):
            edge_copy(h).start()
            exchange_start(h)
        early_previous()
        bytes_wait(counts.at[pl.ds(0, groups - 1)], count_recv)

        @pl.when(i % stride == 0)
        def _():
            bytes_wait(partial.at[pl.ds(0, slices - 1)], partial_recv)
            bytes_wait(feat.at[pl.ds(0, slices - 1)], feat_send)

        @pl.when(i % stride != 0)
        def _():
            bytes_wait(partial, partial_recv)
            bytes_wait(feat.at[pl.ds(0, slices)], feat_send)

        sinkhorn()
        crowd[...] = bias[0, 2:3, :]
        bias_copy.start()
        give_back(0)
        give_back(1)
        finish(0)
        finish(1)
        bytes_wait(col.at[pl.ds(0, 2), pl.ds(0, 2 * (groups - 1))], col_send)

        @pl.when(i % stride == 0)
        def _():
            for _ in range(plane - 1):
                bytes_wait(partial.at[0], partial_send)

        bytes_wait(counts.at[pl.ds(0, groups - 1)], count_send)
        for h in range(2):
            edge_copy(h).wait_send()
            exchange(h, 0).wait_send()
            exchange(h, 1).wait_send()
        bias_copy.wait_send()

    @pl.when(p == 1)
    def _():
        followers = sum(jnp.where(g == leader, 1, 0) for _, leader in turns)
        pl.semaphore_wait(barrier, plane - 1 + groups + followers)
        signal(ready, mirror)
        for og in range(groups):
            to_column(mirror, og)
        spread(0)
        spread(1)
        tables()
        spread_done(0)
        fill(0)

        for follower, _ in turns:

            @pl.when(g == follower)
            def _():
                pl.semaphore_wait(turn, 1)

        exchange_start(0)
        spread_done(1)
        fill(1)
        exchange_start(1)
        hand_on()
        exchange(0, 0).wait_send()
        exchange(0, 1).wait_send()
        exchange(1, 0).wait_send()

        for follower, leader in turns:

            @pl.when(g == leader)
            def _():
                signal(turn, s, follower)

        local()
        early_previous()
        give_back(0)
        give_back(1)
        bias_copy.wait_recv()
        crowd[...] = bias[0, 2:3, :]
        finish(0)
        finish(1)
        exchange(1, 1).wait_send()
        bytes_wait(col.at[pl.ds(0, 2), pl.ds(0, slices)], col_send)

    for h in range(2):
        bytes_wait(own[h].at[pl.ds(0, plane - 1)], spread_send.at[h])
        bytes_wait(pick.at[h, pl.ds(0, plane - 1)], back_send.at[h])

    @pl.when(i < plane - 1)
    def _():
        for h in range(2):
            bytes_wait(prev.at[h], prev_send.at[h])

    @pl.when(s > plane)
    def _():
        for h in range(2):
            bytes_wait(edge.at[h], extra_send.at[h])


def attention(plane, groups, slots, collective_id, name):
    piece = 2 * BS // plane
    seq = 2 * plane
    half = plane // 2
    width = 2 * DH
    slices = 2 * groups
    dma = pltpu.SemaphoreType.DMA
    hbm = pl.BlockSpec(memory_space=pl.ANY)
    vmem = pl.BlockSpec(memory_space=pltpu.VMEM)
    folded = (half, piece, width)
    one, two = dma(()), dma((2,))
    pieces = pltpu.VMEM((2, plane, piece, DH), jnp.bfloat16)
    head_pieces = pltpu.VMEM((plane, piece, DH), jnp.bfloat16)
    head_slots = pltpu.VMEM((slots, piece, DH), jnp.bfloat16)

    def call(queries, keys, values, partner):
        return pl.pallas_call(
            functools.partial(sparse_attention_kernel, plane, groups, slots),
            out_shape=(
                jax.ShapeDtypeStruct(queries.shape, queries.dtype),
                pltpu.VMEM((1, DH), jnp.float32),
            ),
            in_specs=[pl.BlockSpec(memory_space=pltpu.HBM), hbm, hbm, hbm],
            out_specs=(vmem, vmem),
            scratch_shapes=[
                pltpu.VMEM(folded, jnp.bfloat16),
                pltpu.VMEM((plane, piece, width), jnp.bfloat16),
                head_pieces,
                head_pieces,
                head_slots,
                head_slots,
                head_slots,
                head_slots,
                pltpu.VMEM((2, piece, DH), jnp.bfloat16),
                pieces,
                pieces,
                pieces,
                pltpu.VMEM((4, slices, 1, DH), jnp.float32),
                pltpu.VMEM((plane, 4, 1, DH), jnp.float32),
                pltpu.VMEM((slices, plane, max(DH, 2 * seq)), jnp.float32),
                pltpu.VMEM((groups, 1, DH), jnp.float32),
                pltpu.VMEM((2, 3, DH), jnp.float32),
                pltpu.VMEM((2, BS, 1), jnp.float32),
                pltpu.VMEM((2, BS, 1), jnp.float32),
                pltpu.VMEM((2, BS, DH), jnp.float32),
                pltpu.SMEM((2, plane + 2), jnp.int32),
                pltpu.SMEM((2, seq), jnp.int32),
                dma((4,)),
            ]
            + [one] * 10
            + [two] * 2
            + [dma((4,))] * 2
            + [two] * 7
            + [pltpu.SemaphoreType.REGULAR] * 2,
            compiler_params=pltpu.CompilerParams(
                collective_id=collective_id, has_side_effects=True
            ),
            name=name,
        )(partner, queries.reshape(folded), keys.reshape(folded), values.reshape(folded))

    return call


def solution(mesh):
    seq, groups = mesh.shape["seq"], mesh.shape["head"]
    plane = seq // 2
    slots = plane * SLOT_SHARE // 32
    packed = attention(plane, groups, slots, 0, "packed")
    whole = attention(plane, groups, plane, 1, "whole")

    def body(queries, keys, values, partner):
        attended, crowd = packed(queries, keys, values, partner)
        return lax.cond(
            crowd[0, 0] > slots,
            lambda: whole(queries, keys, values, partner)[0],
            lambda: attended,
        )

    return jax.shard_map(
        body,
        mesh=mesh,
        in_specs=(P("seq", "head"), P("seq", "head"), P("seq", "head"), P("head", None)),
        out_specs=P("seq", "head"),
        check_vma=False,
    )
```

```python
import functools
import math

import jax
import jax.numpy as jnp
from jax import lax
from jax.experimental import pallas as pl
from jax.experimental.pallas import tpu as pltpu
from jax.sharding import PartitionSpec as P

DH = 128
BS = 256
SINK_ITERS = 8
SHARPNESS = 2.0
SLOT_SHARE = 40
TURNS = ((3, 1), (5, 1), (7, 1), )
HIGHEST = lax.Precision.HIGHEST
MESH = pl.DeviceIdType.MESH


def far_first(size):
    return sorted(range(size), key=lambda o: (min(o, size - o) == 0, -min(o, size - o)))


def bytes_wait(ref, sem):
    pltpu.make_async_copy(ref, ref, sem).wait()


def sparse_attention_kernel(
    plane,
    groups,
    slots,
    partner_hbm,
    q_hbm,
    k_hbm,
    v_hbm,
    out,
    crowd,
    qs,
    kv,
    own,
    pack,
    slot,
    edge,
    pick,
    part,
    prev,
    col,
    feat,
    partial,
    counts,
    bias,
    top_all,
    den_all,
    mix_all,
    after,
    partner,
    load_sem,
    col_send,
    col_recv,
    count_send,
    count_recv,
    feat_send,
    feat_recv,
    partial_send,
    partial_recv,
    bias_send,
    bias_recv,
    spread_send,
    spread_recv,
    z_send,
    z_recv,
    edge_send,
    edge_recv,
    back_send,
    back_recv,
    prev_send,
    extra_send,
    prev_recv,
    ready,
    turn,
):
    s = lax.axis_index("seq")
    g = lax.axis_index("head")
    p = s // plane
    i = s % plane
    base = p * plane
    mirror = (s + plane) % (2 * plane)
    half = plane // 2
    across = plane - base
    slices = 2 * groups
    stride = plane // slices
    inv_scale = 1.0 / math.sqrt(DH)

    def remote(src, dst, ss, rs, seq, head=None):
        return pltpu.make_async_remote_copy(
            src_ref=src,
            dst_ref=dst,
            send_sem=ss,
            recv_sem=rs,
            device_id=(seq, g if head is None else head),
            device_id_type=MESH,
        )

    def signal(sem, seq, head=None):
        pl.semaphore_signal(
            sem,
            inc=1,
            device_id=(seq, g if head is None else head),
            device_id_type=MESH,
        )

    x_size = 4 if plane % 8 == 0 else 1
    y_size = plane // (2 * x_size)
    x_at, y_at = i // (2 * y_size), i // 2 % y_size
    y_order = [(y_at + o) % y_size * 2 for o in far_first(y_size)]
    cores = [1 - i % 2, i % 2]

    def each_peer(body):
        def line(k, carry):
            o = 0
            for at, offset in enumerate(far_first(x_size)):
                o = jnp.where(k == at, offset, o)
            x = (x_at + o) % x_size * (2 * y_size)
            near = None
            for y in y_order:
                for core in cores:
                    near = x + y + core
                    if y is y_order[-1] and core is cores[-1]:
                        break
                    body(near, base + near)

            @pl.when(k < x_size - 1)
            def _():
                body(near, base + near)

            return carry

        lax.fori_loop(0, x_size, line, 0)

    def each_group(body):
        def wrapped(o, c):
            body((g + o) % groups)
            return c

        lax.fori_loop(1, groups, wrapped, 0)

    turns = [(f, l) for f, l in TURNS if f < groups]
    barrier = pltpu.get_barrier_semaphore()

    @pl.when(p == 0)
    def _():
        for og in range(groups):
            signal(barrier, mirror, og)
        each_group(lambda og: signal(barrier, s, og))

    for follower, leader in turns:

        @pl.when((p == 1) & (g == follower))
        def _():
            signal(barrier, s, leader)

    each_peer(lambda j, d: signal(barrier, d))

    loads = (
        pltpu.make_async_copy(partner_hbm, partner, load_sem.at[3]),
        pltpu.make_async_copy(q_hbm, qs, load_sem.at[0]),
        pltpu.make_async_copy(k_hbm, kv.at[pl.ds(0, half)], load_sem.at[1]),
        pltpu.make_async_copy(v_hbm, kv.at[pl.ds(half, half)], load_sem.at[2]),
    )
    for c in loads:
        c.start()
    for c in loads:
        c.wait()
    pooled_q = jnp.sum(jnp.sum(qs[...].astype(jnp.float32), axis=0), axis=0, keepdims=True)
    pooled_k = jnp.sum(
        jnp.sum(kv[pl.ds(0, half)].astype(jnp.float32), axis=0), axis=0, keepdims=True
    )
    for h in range(2):
        lanes = slice(h * DH, (h + 1) * DH)
        col[p, 2 * g + h] = pooled_q[:, lanes] / math.sqrt(BS)
        col[2 + p, 2 * g + h] = pooled_k[:, lanes] / math.sqrt(BS)

    def here(block):
        return (block >= base) & (block < base + plane)

    both = 2 * plane

    def wants(c, side):
        h = jnp.where(c >= plane, 1, 0)
        return partner[h, side + c - h * plane]

    def tables():
        after[both] = both
        after[both + 1] = both

        def link(o, carry):
            c = both - 1 - o
            after[c] = jnp.where(here(wants(c, across)), c, after[c + 1])
            return carry

        lax.fori_loop(0, both, link, 0)

    def count(first, last, side, near):
        def add(c, n):
            return n + jnp.where(here(wants(c, side)) == near, 1, 0)

        return lax.fori_loop(first, last, add, 0)

    def to_column(seq, head):
        rows = pl.ds(2 * g, 2)
        for kind in (p, 2 + p):
            remote(col.at[kind, rows], col.at[kind, rows], col_send, col_recv, seq, head).start()

    bias_copy = remote(bias.at[1], bias.at[0], bias_send, bias_recv, mirror)

    def spread():
        pltpu.make_async_copy(kv.at[i], own.at[i], spread_recv).start()
        each_peer(
            lambda j, d: remote(kv.at[j], own.at[i], spread_send, spread_recv, d).start()
        )

    def hand_on():
        @pl.when(i < plane - 1)
        def _():
            remote(kv, prev, prev_send, prev_recv, s + 1).start()

    cuts = (0, slots - slots // 3, slots)

    def exchange(part_id):
        rows = pl.ds(cuts[part_id], cuts[part_id + 1] - cuts[part_id])
        return remote(
            pack.at[rows], slot.at[rows], z_send.at[part_id], z_recv.at[part_id], mirror
        )

    edge_copy = remote(own.at[plane - 1], edge, edge_send, edge_recv, mirror)

    def fill():
        bytes_wait(own, spread_recv)

        def take(k, at):
            c = after[at]
            block = wants(jnp.minimum(c, both - 1), across)
            piece = jnp.clip(block - base, 0, plane - 1)
            pack[k] = jnp.where(c < plane, own[piece, :, 0:DH], own[piece, :, DH : 2 * DH])
            return c + 1

        lax.fori_loop(0, slots, take, 0)

    def give_back():
        exchange(0).wait_recv()
        exchange(1).wait_recv()

        def choose(j, taken):
            later = []
            for h in range(2):
                lanes = slice(h * DH, (h + 1) * DH)
                block = partner[h, base + j]
                near = here(block)
                mine = own[jnp.clip(block - base, 0, plane - 1), :, lanes]
                theirs = slot[jnp.minimum(taken[h], slots - 1)]
                pick[j, :, lanes] = jnp.where(near, mine, theirs)
                later.append(taken[h] + jnp.where(near, 0, 1))
            return tuple(later)

        lax.fori_loop(0, plane, choose, (jnp.int32(0), count(0, plane, base, False)))
        each_peer(
            lambda j, d: remote(pick.at[j], part.at[i], back_send, back_recv, d).start()
        )
        pltpu.make_async_copy(pick.at[i], part.at[i], back_recv).start()

        @pl.when(s == plane)
        def _():
            bytes_wait(edge, edge_recv)
            pltpu.make_async_copy(edge, prev.at[0], prev_recv).start()

        @pl.when(s > plane)
        def _():
            bytes_wait(edge, edge_recv)
            remote(edge, prev.at[i], extra_send, prev_recv, base).start()

    def query(h):
        return qs[:, :, h * DH : (h + 1) * DH].reshape(BS, DH)

    def scored(h, key):
        x = lax.dot_general(
            query(h), key, (((1,), (1,)), ((), ())), preferred_element_type=jnp.float32
        )
        return x * inv_scale

    def stacked(ref, h):
        lanes = slice(h * DH, (h + 1) * DH)
        return (
            ref[0:half, :, lanes].reshape(BS, DH),
            ref[half:plane, :, lanes].reshape(BS, DH),
        )

    def local():
        for h in range(2):
            lanes = slice(h * DH, (h + 1) * DH)
            x = scored(h, kv[0:half, :, lanes].reshape(BS, DH))
            top = jnp.max(x, axis=1, keepdims=True)
            e = jnp.exp(x - top)
            top_all[h] = top
            den_all[h] = jnp.sum(e, axis=1, keepdims=True)
            mix_all[h] = jnp.dot(
                e.astype(jnp.bfloat16),
                kv[half:plane, :, lanes].reshape(BS, DH),
                preferred_element_type=jnp.float32,
            )

    def merged(h, ref, shift):
        key, val = stacked(ref, h)
        x = scored(h, key)
        if shift is not None:
            x = x + shift
        old = top_all[h]
        top = jnp.maximum(old, jnp.max(x, axis=1, keepdims=True))
        keep = jnp.exp(old - top)
        e = jnp.exp(x - top)
        den = den_all[h] * keep + jnp.sum(e, axis=1, keepdims=True)
        mix = mix_all[h] * keep + jnp.dot(
            e.astype(jnp.bfloat16), val, preferred_element_type=jnp.float32
        )
        return top, den, mix

    def previous(h):
        top, den, mix = merged(h, prev, None)
        top_all[h] = top
        den_all[h] = den
        mix_all[h] = mix

    def early_previous():
        @pl.when(i > 0)
        def _():
            bytes_wait(prev, prev_recv)
            for h in range(2):
                previous(h)

    def late_previous():
        @pl.when(s == plane)
        def _():
            bytes_wait(prev, prev_recv)
            for h in range(2):
                previous(h)

    def finish():
        late_previous()
        bytes_wait(part, back_recv)
        for h in range(2):
            _, den, mix = merged(h, part, bias[0, h : h + 1, 0:1])
            out[:, h * DH : (h + 1) * DH] = (mix * (1.0 / den)).astype(jnp.bfloat16)

    def owned():
        mine = i // stride
        each_peer(
            lambda j, d: remote(
                partial.at[mine], partial.at[mine], partial_send, partial_recv, d
            ).start()
        )

    def scores():
        queries = jnp.concatenate([feat[:, 0, 0, :], feat[:, 1, 0, :]], axis=0)
        keys = jnp.concatenate([feat[:, 2, 0, :], feat[:, 3, 0, :]], axis=0)
        x = lax.dot_general(
            queries,
            keys,
            (((1,), (1,)), ((), ())),
            precision=HIGHEST,
            preferred_element_type=jnp.float32,
        )
        x = x * (SHARPNESS / math.sqrt(2 * DH * groups))
        partial[i // stride, :, 0 : 2 * plane] = x[0:plane]
        partial[i // stride, :, 2 * plane : 4 * plane] = x[plane : 2 * plane]

    def sinkhorn():
        both = jnp.sum(partial[...], axis=0)
        x = jnp.concatenate([both[:, 0 : 2 * plane], both[:, 2 * plane : 4 * plane]], axis=0)

        def sweep(_, x):
            for along in (1, 0):
                top = jnp.max(x, axis=along, keepdims=True)
                x = x - (top + jnp.log(jnp.sum(jnp.exp(x - top), axis=along, keepdims=True)))
            return x

        x = lax.fori_loop(0, SINK_ITERS, sweep, x)
        row = lax.broadcasted_iota(jnp.int32, x.shape, 0)
        col = lax.broadcasted_iota(jnp.int32, x.shape, 1)
        for which, block in ((0, s), (1, mirror)):
            for h in range(2):
                chosen = (row == i + which * plane) & (col == partner[h, block])
                value = jnp.sum(
                    jnp.sum(jnp.where(chosen, x, 0.0), axis=1, keepdims=True), axis=0, keepdims=True
                )
                bias[which, h : h + 1, :] = jnp.broadcast_to(
                    value + math.log(2 * plane), (1, DH)
                )
            bias[which, 2:3, :] = jnp.max(counts[...], axis=0)

    @pl.when(p == 0)
    def _():
        crossing = count(0, both, across, True)
        counts[g] = jnp.full((1, DH), crossing, jnp.int32).astype(jnp.float32)
        pl.semaphore_wait(barrier, plane - 1 + groups - 1)
        each_group(lambda og: to_column(s, og))
        each_group(
            lambda og: remote(
                counts.at[g], counts.at[g], count_send, count_recv, s, og
            ).start()
        )
        spread()
        hand_on()
        tables()
        local()
        fill()
        pl.semaphore_wait(ready, 1)
        bytes_wait(feat.at[pl.ds(0, 2 * groups - 1)], col_recv)

        def to_owner(sl, c):
            owner = sl * stride

            @pl.when(owner != i)
            def _():
                remote(col.at[:, sl], feat.at[i], feat_send, feat_recv, base + owner).start()

            @pl.when(owner == i)
            def _():
                pltpu.make_async_copy(col.at[:, sl], feat.at[i], feat_recv).start()

            return c

        lax.fori_loop(0, slices, to_owner, 0)

        @pl.when(i % stride == 0)
        def _():
            bytes_wait(feat, feat_recv)
            scores()
            owned()

        edge_copy.start()
        exchange(0).start()
        exchange(1).start()
        early_previous()
        bytes_wait(counts.at[pl.ds(0, groups - 1)], count_recv)

        @pl.when(i % stride == 0)
        def _():
            bytes_wait(partial.at[pl.ds(0, slices - 1)], partial_recv)
            bytes_wait(feat.at[pl.ds(0, slices - 1)], feat_send)

        @pl.when(i % stride != 0)
        def _():
            bytes_wait(partial, partial_recv)
            bytes_wait(feat.at[pl.ds(0, slices)], feat_send)

        sinkhorn()
        crowd[...] = bias[0, 2:3, :]
        bias_copy.start()
        give_back()
        finish()
        bytes_wait(col.at[pl.ds(0, 2), pl.ds(0, 2 * (groups - 1))], col_send)

        @pl.when(i % stride == 0)
        def _():
            for _ in range(plane - 1):
                bytes_wait(partial.at[0], partial_send)

        bytes_wait(counts.at[pl.ds(0, groups - 1)], count_send)
        edge_copy.wait_send()
        exchange(0).wait_send()
        exchange(1).wait_send()
        bias_copy.wait_send()

    @pl.when(p == 1)
    def _():
        followers = sum(jnp.where(g == leader, 1, 0) for _, leader in turns)
        pl.semaphore_wait(barrier, plane - 1 + groups + followers)
        signal(ready, mirror)
        for og in range(groups):
            to_column(mirror, og)
        spread()
        tables()
        fill()

        for follower, _ in turns:

            @pl.when(g == follower)
            def _():
                pl.semaphore_wait(turn, 1)

        exchange(0).start()
        exchange(1).start()
        hand_on()
        exchange(0).wait_send()

        for follower, leader in turns:

            @pl.when(g == leader)
            def _():
                signal(turn, s, follower)

        local()
        early_previous()
        give_back()
        bias_copy.wait_recv()
        crowd[...] = bias[0, 2:3, :]
        finish()
        exchange(1).wait_send()
        bytes_wait(col.at[pl.ds(0, 2), pl.ds(0, slices)], col_send)

    bytes_wait(own.at[pl.ds(0, plane - 1)], spread_send)
    bytes_wait(pick.at[pl.ds(0, plane - 1)], back_send)

    @pl.when(i < plane - 1)
    def _():
        bytes_wait(prev, prev_send)

    @pl.when(s > plane)
    def _():
        bytes_wait(edge, extra_send)


def attention(plane, groups, slots, collective_id, name):
    piece = 2 * BS // plane
    seq = 2 * plane
    half = plane // 2
    width = 2 * DH
    slices = 2 * groups
    dma = pltpu.SemaphoreType.DMA
    hbm = pl.BlockSpec(memory_space=pl.ANY)
    vmem = pl.BlockSpec(memory_space=pltpu.VMEM)
    folded = (half, piece, width)
    one, two = dma(()), dma((2,))
    pieces = pltpu.VMEM((plane, piece, width), jnp.bfloat16)
    head_slots = pltpu.VMEM((slots, piece, DH), jnp.bfloat16)

    def call(queries, keys, values, partner):
        return pl.pallas_call(
            functools.partial(sparse_attention_kernel, plane, groups, slots),
            out_shape=(
                jax.ShapeDtypeStruct(queries.shape, queries.dtype),
                pltpu.VMEM((1, DH), jnp.float32),
            ),
            in_specs=[pl.BlockSpec(memory_space=pltpu.HBM), hbm, hbm, hbm],
            out_specs=(vmem, vmem),
            scratch_shapes=[
                pltpu.VMEM(folded, jnp.bfloat16),
                pieces,
                pieces,
                head_slots,
                head_slots,
                pltpu.VMEM((piece, width), jnp.bfloat16),
                pieces,
                pieces,
                pieces,
                pltpu.VMEM((4, slices, 1, DH), jnp.float32),
                pltpu.VMEM((plane, 4, 1, DH), jnp.float32),
                pltpu.VMEM((slices, plane, max(DH, 2 * seq)), jnp.float32),
                pltpu.VMEM((groups, 1, DH), jnp.float32),
                pltpu.VMEM((2, 3, DH), jnp.float32),
                pltpu.VMEM((2, BS, 1), jnp.float32),
                pltpu.VMEM((2, BS, 1), jnp.float32),
                pltpu.VMEM((2, BS, DH), jnp.float32),
                pltpu.SMEM((seq + 2,), jnp.int32),
                pltpu.SMEM((2, seq), jnp.int32),
                dma((4,)),
            ]
            + [one] * 12
            + [two] * 2
            + [one] * 7
            + [pltpu.SemaphoreType.REGULAR] * 2,
            compiler_params=pltpu.CompilerParams(
                collective_id=collective_id, has_side_effects=True
            ),
            name=name,
        )(partner, queries.reshape(folded), keys.reshape(folded), values.reshape(folded))

    return call


def solution(mesh):
    seq, groups = mesh.shape["seq"], mesh.shape["head"]
    plane = seq // 2
    slots = seq * SLOT_SHARE // 64
    packed = attention(plane, groups, slots, 0, "packed")
    whole = attention(plane, groups, seq, 1, "whole")

    def body(queries, keys, values, partner):
        attended, crowd = packed(queries, keys, values, partner)
        return lax.cond(
            crowd[0, 0] > slots,
            lambda: whole(queries, keys, values, partner)[0],
            lambda: attended,
        )

    return jax.shard_map(
        body,
        mesh=mesh,
        in_specs=(P("seq", "head"), P("seq", "head"), P("seq", "head"), P("head", None)),
        out_specs=P("seq", "head"),
        check_vma=False,
    )
```

```python
import functools
import math

import jax
import jax.numpy as jnp
from jax import lax
from jax.experimental import pallas as pl
from jax.experimental.pallas import tpu as pltpu
from jax.sharding import PartitionSpec as P

DH = 128
BS = 256
SINK_ITERS = 8
SHARPNESS = 2.0
SLOT_SHARE = 22
TURNS = ((3, 1), (5, 1), (7, 1), )
HIGHEST = lax.Precision.HIGHEST
MESH = pl.DeviceIdType.MESH


def far_first(size):
    return sorted(range(size), key=lambda o: (min(o, size - o) == 0, -min(o, size - o)))


def bytes_wait(ref, sem):
    pltpu.make_async_copy(ref, ref, sem).wait()


def sparse_attention_kernel(
    plane,
    groups,
    slots,
    partner_hbm,
    q_hbm,
    k_hbm,
    v_hbm,
    out,
    crowd,
    qs,
    kv,
    own_a,
    own_b,
    pack_a,
    pack_b,
    slot_a,
    slot_b,
    edge,
    pick,
    part,
    prev,
    col,
    feat,
    partial,
    counts,
    bias,
    top_all,
    den_all,
    mix_all,
    after,
    partner,
    load_sem,
    col_send,
    col_recv,
    count_send,
    count_recv,
    feat_send,
    feat_recv,
    partial_send,
    partial_recv,
    bias_send,
    bias_recv,
    spread_send,
    spread_recv,
    z_send,
    z_recv,
    edge_send,
    edge_recv,
    back_send,
    back_recv,
    prev_send,
    extra_send,
    prev_recv,
    ready,
    turn,
):
    own = (own_a, own_b)
    pack = (pack_a, pack_b)
    slot = (slot_a, slot_b)
    s = lax.axis_index("seq")
    g = lax.axis_index("head")
    p = s // plane
    i = s % plane
    base = p * plane
    mirror = (s + plane) % (2 * plane)
    half = plane // 2
    across = plane - base
    slices = 2 * groups
    stride = plane // slices
    inv_scale = 1.0 / math.sqrt(DH)

    def remote(src, dst, ss, rs, seq, head=None):
        return pltpu.make_async_remote_copy(
            src_ref=src,
            dst_ref=dst,
            send_sem=ss,
            recv_sem=rs,
            device_id=(seq, g if head is None else head),
            device_id_type=MESH,
        )

    def signal(sem, seq, head=None):
        pl.semaphore_signal(
            sem,
            inc=1,
            device_id=(seq, g if head is None else head),
            device_id_type=MESH,
        )

    x_size = 4 if plane % 8 == 0 else 1
    y_size = plane // (2 * x_size)
    x_at, y_at = i // (2 * y_size), i // 2 % y_size
    y_order = [(y_at + o) % y_size * 2 for o in far_first(y_size)]
    cores = [1 - i % 2, i % 2]

    def each_peer(body):
        def line(k, carry):
            o = 0
            for at, offset in enumerate(far_first(x_size)):
                o = jnp.where(k == at, offset, o)
            x = (x_at + o) % x_size * (2 * y_size)
            near = None
            for y in y_order:
                for core in cores:
                    near = x + y + core
                    if y is y_order[-1] and core is cores[-1]:
                        break
                    body(near, base + near)

            @pl.when(k < x_size - 1)
            def _():
                body(near, base + near)

            return carry

        lax.fori_loop(0, x_size, line, 0)

    def each_group(body):
        def wrapped(o, c):
            body((g + o) % groups)
            return c

        lax.fori_loop(1, groups, wrapped, 0)

    turns = [(f, l) for f, l in TURNS if f < groups]
    barrier = pltpu.get_barrier_semaphore()

    @pl.when(p == 0)
    def _():
        for og in range(groups):
            signal(barrier, mirror, og)
        each_group(lambda og: signal(barrier, s, og))

    for follower, leader in turns:

        @pl.when((p == 1) & (g == follower))
        def _():
            signal(barrier, s, leader)

    each_peer(lambda j, d: signal(barrier, d))

    loads = (
        pltpu.make_async_copy(partner_hbm, partner, load_sem.at[3]),
        pltpu.make_async_copy(q_hbm, qs, load_sem.at[0]),
        pltpu.make_async_copy(k_hbm, kv.at[pl.ds(0, half)], load_sem.at[1]),
        pltpu.make_async_copy(v_hbm, kv.at[pl.ds(half, half)], load_sem.at[2]),
    )
    for c in loads:
        c.start()
    for c in loads:
        c.wait()
    pooled_q = jnp.sum(jnp.sum(qs[...].astype(jnp.float32), axis=0), axis=0, keepdims=True)
    pooled_k = jnp.sum(
        jnp.sum(kv[pl.ds(0, half)].astype(jnp.float32), axis=0), axis=0, keepdims=True
    )
    for h in range(2):
        lanes = slice(h * DH, (h + 1) * DH)
        col[p, 2 * g + h] = pooled_q[:, lanes] / math.sqrt(BS)
        col[2 + p, 2 * g + h] = pooled_k[:, lanes] / math.sqrt(BS)

    def here(block):
        return (block >= base) & (block < base + plane)

    def tables():
        for h in range(2):
            after[h, plane] = plane
            after[h, plane + 1] = plane

            def link(o, c):
                d = plane - 1 - o
                after[h, d] = jnp.where(here(partner[h, across + d]), d, after[h, d + 1])
                return c

            lax.fori_loop(0, plane, link, 0)

    def count(h):
        def add(d, n):
            return n + jnp.where(here(partner[h, across + d]), 1, 0)

        return lax.fori_loop(0, plane, add, 0)

    def to_column(seq, head):
        rows = pl.ds(2 * g, 2)
        for kind in (p, 2 + p):
            remote(col.at[kind, rows], col.at[kind, rows], col_send, col_recv, seq, head).start()

    bias_copy = remote(bias.at[1], bias.at[0], bias_send, bias_recv, mirror)

    def spread(h):
        lanes = pl.ds(h * DH, DH)
        pltpu.make_async_copy(kv.at[i, :, lanes], own[h].at[i], spread_recv.at[h]).start()
        each_peer(
            lambda j, d: remote(
                kv.at[j, :, lanes], own[h].at[i], spread_send.at[h], spread_recv.at[h], d
            ).start()
        )

    def hand_on():
        @pl.when(i < plane - 1)
        def _():
            for h in range(2):
                lanes = pl.ds(h * DH, DH)
                remote(
                    kv.at[:, :, lanes], prev.at[h], prev_send.at[h], prev_recv.at[h], s + 1
                ).start()

    cuts = (0, slots - slots * 5 // 8, slots)

    def exchange(h, part_id):
        rows = pl.ds(cuts[part_id], cuts[part_id + 1] - cuts[part_id])
        sems = 2 * h + part_id
        return remote(
            pack[h].at[rows], slot[h].at[rows], z_send.at[sems], z_recv.at[sems], mirror
        )

    def exchange_start(h):
        exchange(h, 0).start()
        exchange(h, 1).start()

    def edge_copy(h):
        return remote(own[h].at[plane - 1], edge.at[h], edge_send.at[h], edge_recv.at[h], mirror)

    def spread_done(h):
        bytes_wait(own[h], spread_recv.at[h])

    def fill(h):
        def take(k, at):
            d = after[h, at]
            block = partner[h, across + jnp.minimum(d, plane - 1)]
            pack[h][k] = own[h][jnp.clip(block - base, 0, plane - 1)]
            return d + 1

        lax.fori_loop(0, slots, take, 0)

    def give_back(h):
        exchange(h, 0).wait_recv()
        exchange(h, 1).wait_recv()

        def choose(j, taken):
            block = partner[h, base + j]
            near = here(block)
            mine = own[h][jnp.clip(block - base, 0, plane - 1)]
            theirs = slot[h][jnp.minimum(taken, slots - 1)]
            pick[h, j] = jnp.where(near, mine, theirs)
            return taken + jnp.where(near, 0, 1)

        lax.fori_loop(0, plane, choose, 0)
        each_peer(
            lambda j, d: remote(
                pick.at[h, j], part.at[h, i], back_send.at[h], back_recv.at[h], d
            ).start()
        )
        pltpu.make_async_copy(pick.at[h, i], part.at[h, i], back_recv.at[h]).start()

        @pl.when(s == plane)
        def _():
            bytes_wait(edge.at[h], edge_recv.at[h])
            pltpu.make_async_copy(edge.at[h], prev.at[h, 0], prev_recv.at[h]).start()

        @pl.when(s > plane)
        def _():
            bytes_wait(edge.at[h], edge_recv.at[h])
            remote(edge.at[h], prev.at[h, i], extra_send.at[h], prev_recv.at[h], base).start()

    def query(h):
        return qs[:, :, h * DH : (h + 1) * DH].reshape(BS, DH)

    def scored(h, key):
        x = lax.dot_general(
            query(h), key, (((1,), (1,)), ((), ())), preferred_element_type=jnp.float32
        )
        return x * inv_scale

    def stacked(ref, h):
        return (
            ref[h, 0:half].reshape(BS, DH),
            ref[h, half:plane].reshape(BS, DH),
        )

    def local():
        for h in range(2):
            lanes = slice(h * DH, (h + 1) * DH)
            x = scored(h, kv[0:half, :, lanes].reshape(BS, DH))
            top = jnp.max(x, axis=1, keepdims=True)
            e = jnp.exp(x - top)
            top_all[h] = top
            den_all[h] = jnp.sum(e, axis=1, keepdims=True)
            mix_all[h] = jnp.dot(
                e.astype(jnp.bfloat16),
                kv[half:plane, :, lanes].reshape(BS, DH),
                preferred_element_type=jnp.float32,
            )

    def merged(h, ref, shift):
        key, val = stacked(ref, h)
        x = scored(h, key)
        if shift is not None:
            x = x + shift
        old = top_all[h]
        top = jnp.maximum(old, jnp.max(x, axis=1, keepdims=True))
        keep = jnp.exp(old - top)
        e = jnp.exp(x - top)
        den = den_all[h] * keep + jnp.sum(e, axis=1, keepdims=True)
        mix = mix_all[h] * keep + jnp.dot(
            e.astype(jnp.bfloat16), val, preferred_element_type=jnp.float32
        )
        return top, den, mix

    def previous(h):
        top, den, mix = merged(h, prev, None)
        top_all[h] = top
        den_all[h] = den
        mix_all[h] = mix

    def early_previous():
        @pl.when(i > 0)
        def _():
            for h in range(2):
                bytes_wait(prev.at[h], prev_recv.at[h])
                previous(h)

    def late_previous(h):
        @pl.when(s == plane)
        def _():
            bytes_wait(prev.at[h], prev_recv.at[h])
            previous(h)

    def finish(h):
        late_previous(h)
        bytes_wait(part.at[h], back_recv.at[h])
        _, den, mix = merged(h, part, bias[0, h : h + 1, 0:1])
        out[:, h * DH : (h + 1) * DH] = (mix * (1.0 / den)).astype(jnp.bfloat16)

    def owned():
        mine = i // stride
        each_peer(
            lambda j, d: remote(
                partial.at[mine], partial.at[mine], partial_send, partial_recv, d
            ).start()
        )

    def scores():
        queries = jnp.concatenate([feat[:, 0, 0, :], feat[:, 1, 0, :]], axis=0)
        keys = jnp.concatenate([feat[:, 2, 0, :], feat[:, 3, 0, :]], axis=0)
        x = lax.dot_general(
            queries,
            keys,
            (((1,), (1,)), ((), ())),
            precision=HIGHEST,
            preferred_element_type=jnp.float32,
        )
        x = x * (SHARPNESS / math.sqrt(2 * DH * groups))
        partial[i // stride, :, 0 : 2 * plane] = x[0:plane]
        partial[i // stride, :, 2 * plane : 4 * plane] = x[plane : 2 * plane]

    def sinkhorn():
        both = jnp.sum(partial[...], axis=0)
        x = jnp.concatenate([both[:, 0 : 2 * plane], both[:, 2 * plane : 4 * plane]], axis=0)

        def sweep(_, x):
            for along in (1, 0):
                top = jnp.max(x, axis=along, keepdims=True)
                x = x - (top + jnp.log(jnp.sum(jnp.exp(x - top), axis=along, keepdims=True)))
            return x

        x = lax.fori_loop(0, SINK_ITERS, sweep, x)
        row = lax.broadcasted_iota(jnp.int32, x.shape, 0)
        col = lax.broadcasted_iota(jnp.int32, x.shape, 1)
        for which, block in ((0, s), (1, mirror)):
            for h in range(2):
                chosen = (row == i + which * plane) & (col == partner[h, block])
                value = jnp.sum(
                    jnp.sum(jnp.where(chosen, x, 0.0), axis=1, keepdims=True), axis=0, keepdims=True
                )
                bias[which, h : h + 1, :] = jnp.broadcast_to(
                    value + math.log(2 * plane), (1, DH)
                )
            bias[which, 2:3, :] = jnp.max(counts[...], axis=0)

    @pl.when(p == 0)
    def _():
        most = jnp.maximum(count(0), count(1))
        counts[g] = jnp.full((1, DH), most, jnp.int32).astype(jnp.float32)
        pl.semaphore_wait(barrier, plane - 1 + groups - 1)
        each_group(lambda og: to_column(s, og))
        each_group(
            lambda og: remote(
                counts.at[g], counts.at[g], count_send, count_recv, s, og
            ).start()
        )
        spread(0)
        spread(1)
        hand_on()
        tables()
        local()
        spread_done(0)
        fill(0)
        pl.semaphore_wait(ready, 1)
        bytes_wait(feat.at[pl.ds(0, 2 * groups - 1)], col_recv)

        def to_owner(sl, c):
            owner = sl * stride

            @pl.when(owner != i)
            def _():
                remote(col.at[:, sl], feat.at[i], feat_send, feat_recv, base + owner).start()

            @pl.when(owner == i)
            def _():
                pltpu.make_async_copy(col.at[:, sl], feat.at[i], feat_recv).start()

            return c

        lax.fori_loop(0, slices, to_owner, 0)
        spread_done(1)
        fill(1)

        @pl.when(i % stride == 0)
        def _():
            bytes_wait(feat, feat_recv)
            scores()
            owned()

        for h in range(2):
            edge_copy(h).start()
            exchange_start(h)
        early_previous()
        bytes_wait(counts.at[pl.ds(0, groups - 1)], count_recv)

        @pl.when(i % stride == 0)
        def _():
            bytes_wait(partial.at[pl.ds(0, slices - 1)], partial_recv)
            bytes_wait(feat.at[pl.ds(0, slices - 1)], feat_send)

        @pl.when(i % stride != 0)
        def _():
            bytes_wait(partial, partial_recv)
            bytes_wait(feat.at[pl.ds(0, slices)], feat_send)

        sinkhorn()
        crowd[...] = bias[0, 2:3, :]
        bias_copy.start()
        give_back(0)
        give_back(1)
        finish(0)
        finish(1)
        bytes_wait(col.at[pl.ds(0, 2), pl.ds(0, 2 * (groups - 1))], col_send)

        @pl.when(i % stride == 0)
        def _():
            for _ in range(plane - 1):
                bytes_wait(partial.at[0], partial_send)

        bytes_wait(counts.at[pl.ds(0, groups - 1)], count_send)
        for h in range(2):
            edge_copy(h).wait_send()
            exchange(h, 0).wait_send()
            exchange(h, 1).wait_send()
        bias_copy.wait_send()

    @pl.when(p == 1)
    def _():
        followers = sum(jnp.where(g == leader, 1, 0) for _, leader in turns)
        pl.semaphore_wait(barrier, plane - 1 + groups + followers)
        signal(ready, mirror)
        for og in range(groups):
            to_column(mirror, og)
        spread(0)
        spread(1)
        tables()
        spread_done(0)
        fill(0)

        for follower, _ in turns:

            @pl.when(g == follower)
            def _():
                pl.semaphore_wait(turn, 1)

        exchange_start(0)
        spread_done(1)
        fill(1)
        exchange_start(1)
        hand_on()
        exchange(0, 0).wait_send()
        exchange(0, 1).wait_send()
        for follower, leader in turns:

            @pl.when(g == leader)
            def _():
                signal(turn, s, follower)

        exchange(1, 0).wait_send()

        local()
        early_previous()
        give_back(0)
        give_back(1)
        bias_copy.wait_recv()
        crowd[...] = bias[0, 2:3, :]
        finish(0)
        finish(1)
        exchange(1, 1).wait_send()
        bytes_wait(col.at[pl.ds(0, 2), pl.ds(0, slices)], col_send)

    for h in range(2):
        bytes_wait(own[h].at[pl.ds(0, plane - 1)], spread_send.at[h])
        bytes_wait(pick.at[h, pl.ds(0, plane - 1)], back_send.at[h])

    @pl.when(i < plane - 1)
    def _():
        for h in range(2):
            bytes_wait(prev.at[h], prev_send.at[h])

    @pl.when(s > plane)
    def _():
        for h in range(2):
            bytes_wait(edge.at[h], extra_send.at[h])


def attention(plane, groups, slots, collective_id, name):
    piece = 2 * BS // plane
    seq = 2 * plane
    half = plane // 2
    width = 2 * DH
    slices = 2 * groups
    dma = pltpu.SemaphoreType.DMA
    hbm = pl.BlockSpec(memory_space=pl.ANY)
    vmem = pl.BlockSpec(memory_space=pltpu.VMEM)
    folded = (half, piece, width)
    one, two = dma(()), dma((2,))
    pieces = pltpu.VMEM((2, plane, piece, DH), jnp.bfloat16)
    head_pieces = pltpu.VMEM((plane, piece, DH), jnp.bfloat16)
    head_slots = pltpu.VMEM((slots, piece, DH), jnp.bfloat16)

    def call(queries, keys, values, partner):
        return pl.pallas_call(
            functools.partial(sparse_attention_kernel, plane, groups, slots),
            out_shape=(
                jax.ShapeDtypeStruct(queries.shape, queries.dtype),
                pltpu.VMEM((1, DH), jnp.float32),
            ),
            in_specs=[pl.BlockSpec(memory_space=pltpu.HBM), hbm, hbm, hbm],
            out_specs=(vmem, vmem),
            scratch_shapes=[
                pltpu.VMEM(folded, jnp.bfloat16),
                pltpu.VMEM((plane, piece, width), jnp.bfloat16),
                head_pieces,
                head_pieces,
                head_slots,
                head_slots,
                head_slots,
                head_slots,
                pltpu.VMEM((2, piece, DH), jnp.bfloat16),
                pieces,
                pieces,
                pieces,
                pltpu.VMEM((4, slices, 1, DH), jnp.float32),
                pltpu.VMEM((plane, 4, 1, DH), jnp.float32),
                pltpu.VMEM((slices, plane, max(DH, 2 * seq)), jnp.float32),
                pltpu.VMEM((groups, 1, DH), jnp.float32),
                pltpu.VMEM((2, 3, DH), jnp.float32),
                pltpu.VMEM((2, BS, 1), jnp.float32),
                pltpu.VMEM((2, BS, 1), jnp.float32),
                pltpu.VMEM((2, BS, DH), jnp.float32),
                pltpu.SMEM((2, plane + 2), jnp.int32),
                pltpu.SMEM((2, seq), jnp.int32),
                dma((4,)),
            ]
            + [one] * 10
            + [two] * 2
            + [dma((4,))] * 2
            + [two] * 7
            + [pltpu.SemaphoreType.REGULAR] * 2,
            compiler_params=pltpu.CompilerParams(
                collective_id=collective_id, has_side_effects=True
            ),
            name=name,
        )(partner, queries.reshape(folded), keys.reshape(folded), values.reshape(folded))

    return call


def solution(mesh):
    seq, groups = mesh.shape["seq"], mesh.shape["head"]
    plane = seq // 2
    slots = plane * SLOT_SHARE // 32
    packed = attention(plane, groups, slots, 0, "packed")
    whole = attention(plane, groups, plane, 1, "whole")

    def body(queries, keys, values, partner):
        attended, crowd = packed(queries, keys, values, partner)
        return lax.cond(
            crowd[0, 0] > slots,
            lambda: whole(queries, keys, values, partner)[0],
            lambda: attended,
        )

    return jax.shard_map(
        body,
        mesh=mesh,
        in_specs=(P("seq", "head"), P("seq", "head"), P("seq", "head"), P("head", None)),
        out_specs=P("seq", "head"),
        check_vma=False,
    )
```

```python
import functools
import math

import jax
import jax.numpy as jnp
from jax import lax
from jax.experimental import pallas as pl
from jax.experimental.pallas import tpu as pltpu
from jax.sharding import PartitionSpec as P

DH = 128
BS = 256
SINK_ITERS = 8
SHARPNESS = 2.0
SLOT_SHARE = 22
TURNS = ((3, 1), (5, 1), (7, 5))
HIGHEST = lax.Precision.HIGHEST
MESH = pl.DeviceIdType.MESH


def far_first(size):
    return sorted(range(size), key=lambda o: (min(o, size - o) == 0, -min(o, size - o)))


def bytes_wait(ref, sem):
    pltpu.make_async_copy(ref, ref, sem).wait()


def sparse_attention_kernel(
    plane,
    groups,
    slots,
    partner_hbm,
    q_hbm,
    k_hbm,
    v_hbm,
    out,
    crowd,
    qs,
    kv,
    own_a,
    own_b,
    pack_a,
    pack_b,
    slot_a,
    slot_b,
    edge,
    pick,
    part,
    prev,
    col,
    feat,
    partial,
    counts,
    bias,
    top_all,
    den_all,
    mix_all,
    after,
    partner,
    load_sem,
    col_send,
    col_recv,
    count_send,
    count_recv,
    feat_send,
    feat_recv,
    partial_send,
    partial_recv,
    bias_send,
    bias_recv,
    spread_send,
    spread_recv,
    z_send,
    z_recv,
    edge_send,
    edge_recv,
    back_send,
    back_recv,
    prev_send,
    extra_send,
    prev_recv,
    ready,
    turn,
):
    own = (own_a, own_b)
    pack = (pack_a, pack_b)
    slot = (slot_a, slot_b)
    s = lax.axis_index("seq")
    g = lax.axis_index("head")
    p = s // plane
    i = s % plane
    base = p * plane
    mirror = (s + plane) % (2 * plane)
    half = plane // 2
    across = plane - base
    slices = 2 * groups
    stride = plane // slices
    inv_scale = 1.0 / math.sqrt(DH)

    def remote(src, dst, ss, rs, seq, head=None):
        return pltpu.make_async_remote_copy(
            src_ref=src,
            dst_ref=dst,
            send_sem=ss,
            recv_sem=rs,
            device_id=(seq, g if head is None else head),
            device_id_type=MESH,
        )

    def signal(sem, seq, head=None):
        pl.semaphore_signal(
            sem,
            inc=1,
            device_id=(seq, g if head is None else head),
            device_id_type=MESH,
        )

    x_size = 4 if plane % 8 == 0 else 1
    y_size = plane // (2 * x_size)
    x_at, y_at = i // (2 * y_size), i // 2 % y_size
    y_order = [(y_at + o) % y_size * 2 for o in far_first(y_size)]
    cores = [1 - i % 2, i % 2]

    def each_peer(body):
        def line(k, carry):
            o = 0
            for at, offset in enumerate(far_first(x_size)):
                o = jnp.where(k == at, offset, o)
            x = (x_at + o) % x_size * (2 * y_size)
            near = None
            for y in y_order:
                for core in cores:
                    near = x + y + core
                    if y is y_order[-1] and core is cores[-1]:
                        break
                    body(near, base + near)

            @pl.when(k < x_size - 1)
            def _():
                body(near, base + near)

            return carry

        lax.fori_loop(0, x_size, line, 0)

    def each_group(body):
        def wrapped(o, c):
            body((g + o) % groups)
            return c

        lax.fori_loop(1, groups, wrapped, 0)

    turns = [(f, l) for f, l in TURNS if f < groups]
    barrier = pltpu.get_barrier_semaphore()

    @pl.when(p == 0)
    def _():
        for og in range(groups):
            signal(barrier, mirror, og)
        each_group(lambda og: signal(barrier, s, og))

    for follower, leader in turns:

        @pl.when((p == 1) & (g == follower))
        def _():
            signal(barrier, s, leader)

    each_peer(lambda j, d: signal(barrier, d))

    loads = (
        pltpu.make_async_copy(partner_hbm, partner, load_sem.at[3]),
        pltpu.make_async_copy(q_hbm, qs, load_sem.at[0]),
        pltpu.make_async_copy(k_hbm, kv.at[pl.ds(0, half)], load_sem.at[1]),
        pltpu.make_async_copy(v_hbm, kv.at[pl.ds(half, half)], load_sem.at[2]),
    )
    for c in loads:
        c.start()
    for c in loads:
        c.wait()
    pooled_q = jnp.sum(jnp.sum(qs[...].astype(jnp.float32), axis=0), axis=0, keepdims=True)
    pooled_k = jnp.sum(
        jnp.sum(kv[pl.ds(0, half)].astype(jnp.float32), axis=0), axis=0, keepdims=True
    )
    for h in range(2):
        lanes = slice(h * DH, (h + 1) * DH)
        col[p, 2 * g + h] = pooled_q[:, lanes] / math.sqrt(BS)
        col[2 + p, 2 * g + h] = pooled_k[:, lanes] / math.sqrt(BS)

    def here(block):
        return (block >= base) & (block < base + plane)

    def tables():
        for h in range(2):
            after[h, plane] = plane
            after[h, plane + 1] = plane

            def link(o, c):
                d = plane - 1 - o
                after[h, d] = jnp.where(here(partner[h, across + d]), d, after[h, d + 1])
                return c

            lax.fori_loop(0, plane, link, 0)

    def count(h):
        def add(d, n):
            return n + jnp.where(here(partner[h, across + d]), 1, 0)

        return lax.fori_loop(0, plane, add, 0)

    def to_column(seq, head):
        rows = pl.ds(2 * g, 2)
        for kind in (p, 2 + p):
            remote(col.at[kind, rows], col.at[kind, rows], col_send, col_recv, seq, head).start()

    bias_copy = remote(bias.at[1], bias.at[0], bias_send, bias_recv, mirror)

    def spread(h):
        lanes = pl.ds(h * DH, DH)
        pltpu.make_async_copy(kv.at[i, :, lanes], own[h].at[i], spread_recv.at[h]).start()
        each_peer(
            lambda j, d: remote(
                kv.at[j, :, lanes], own[h].at[i], spread_send.at[h], spread_recv.at[h], d
            ).start()
        )

    def hand_on():
        @pl.when(i < plane - 1)
        def _():
            for h in range(2):
                lanes = pl.ds(h * DH, DH)
                remote(
                    kv.at[:, :, lanes], prev.at[h], prev_send.at[h], prev_recv.at[h], s + 1
                ).start()

    cuts = (0, slots - slots * 5 // 8, slots)

    def exchange(h, part_id):
        rows = pl.ds(cuts[part_id], cuts[part_id + 1] - cuts[part_id])
        sems = 2 * h + part_id
        return remote(
            pack[h].at[rows], slot[h].at[rows], z_send.at[sems], z_recv.at[sems], mirror
        )

    def exchange_start(h):
        exchange(h, 0).start()
        exchange(h, 1).start()

    def edge_copy(h):
        return remote(own[h].at[plane - 1], edge.at[h], edge_send.at[h], edge_recv.at[h], mirror)

    def spread_done(h):
        bytes_wait(own[h], spread_recv.at[h])

    def fill(h):
        def take(k, at):
            d = after[h, at]
            block = partner[h, across + jnp.minimum(d, plane - 1)]
            pack[h][k] = own[h][jnp.clip(block - base, 0, plane - 1)]
            return d + 1

        lax.fori_loop(0, slots, take, 0)

    def give_back(h):
        exchange(h, 0).wait_recv()
        exchange(h, 1).wait_recv()

        def choose(j, taken):
            block = partner[h, base + j]
            near = here(block)
            mine = own[h][jnp.clip(block - base, 0, plane - 1)]
            theirs = slot[h][jnp.minimum(taken, slots - 1)]
            pick[h, j] = jnp.where(near, mine, theirs)
            return taken + jnp.where(near, 0, 1)

        lax.fori_loop(0, plane, choose, 0)
        each_peer(
            lambda j, d: remote(
                pick.at[h, j], part.at[h, i], back_send.at[h], back_recv.at[h], d
            ).start()
        )
        pltpu.make_async_copy(pick.at[h, i], part.at[h, i], back_recv.at[h]).start()

        @pl.when(s == plane)
        def _():
            bytes_wait(edge.at[h], edge_recv.at[h])
            pltpu.make_async_copy(edge.at[h], prev.at[h, 0], prev_recv.at[h]).start()

        @pl.when(s > plane)
        def _():
            bytes_wait(edge.at[h], edge_recv.at[h])
            remote(edge.at[h], prev.at[h, i], extra_send.at[h], prev_recv.at[h], base).start()

    def query(h):
        return qs[:, :, h * DH : (h + 1) * DH].reshape(BS, DH)

    def scored(h, key):
        x = lax.dot_general(
            query(h), key, (((1,), (1,)), ((), ())), preferred_element_type=jnp.float32
        )
        return x * inv_scale

    def stacked(ref, h):
        return (
            ref[h, 0:half].reshape(BS, DH),
            ref[h, half:plane].reshape(BS, DH),
        )

    def local():
        for h in range(2):
            lanes = slice(h * DH, (h + 1) * DH)
            x = scored(h, kv[0:half, :, lanes].reshape(BS, DH))
            top = jnp.max(x, axis=1, keepdims=True)
            e = jnp.exp(x - top)
            top_all[h] = top
            den_all[h] = jnp.sum(e, axis=1, keepdims=True)
            mix_all[h] = jnp.dot(
                e.astype(jnp.bfloat16),
                kv[half:plane, :, lanes].reshape(BS, DH),
                preferred_element_type=jnp.float32,
            )

    def merged(h, ref, shift):
        key, val = stacked(ref, h)
        x = scored(h, key)
        if shift is not None:
            x = x + shift
        old = top_all[h]
        top = jnp.maximum(old, jnp.max(x, axis=1, keepdims=True))
        keep = jnp.exp(old - top)
        e = jnp.exp(x - top)
        den = den_all[h] * keep + jnp.sum(e, axis=1, keepdims=True)
        mix = mix_all[h] * keep + jnp.dot(
            e.astype(jnp.bfloat16), val, preferred_element_type=jnp.float32
        )
        return top, den, mix

    def previous(h):
        top, den, mix = merged(h, prev, None)
        top_all[h] = top
        den_all[h] = den
        mix_all[h] = mix

    def early_previous():
        @pl.when(i > 0)
        def _():
            for h in range(2):
                bytes_wait(prev.at[h], prev_recv.at[h])
                previous(h)

    def late_previous(h):
        @pl.when(s == plane)
        def _():
            bytes_wait(prev.at[h], prev_recv.at[h])
            previous(h)

    def finish(h):
        late_previous(h)
        bytes_wait(part.at[h], back_recv.at[h])
        _, den, mix = merged(h, part, bias[0, h : h + 1, 0:1])
        out[:, h * DH : (h + 1) * DH] = (mix * (1.0 / den)).astype(jnp.bfloat16)

    def owned():
        mine = i // stride
        each_peer(
            lambda j, d: remote(
                partial.at[mine], partial.at[mine], partial_send, partial_recv, d
            ).start()
        )

    def scores():
        queries = jnp.concatenate([feat[:, 0, 0, :], feat[:, 1, 0, :]], axis=0)
        keys = jnp.concatenate([feat[:, 2, 0, :], feat[:, 3, 0, :]], axis=0)
        x = lax.dot_general(
            queries,
            keys,
            (((1,), (1,)), ((), ())),
            precision=HIGHEST,
            preferred_element_type=jnp.float32,
        )
        x = x * (SHARPNESS / math.sqrt(2 * DH * groups))
        partial[i // stride, :, 0 : 2 * plane] = x[0:plane]
        partial[i // stride, :, 2 * plane : 4 * plane] = x[plane : 2 * plane]

    def sinkhorn():
        both = jnp.sum(partial[...], axis=0)
        x = jnp.concatenate([both[:, 0 : 2 * plane], both[:, 2 * plane : 4 * plane]], axis=0)

        def sweep(_, x):
            for along in (1, 0):
                top = jnp.max(x, axis=along, keepdims=True)
                x = x - (top + jnp.log(jnp.sum(jnp.exp(x - top), axis=along, keepdims=True)))
            return x

        x = lax.fori_loop(0, SINK_ITERS, sweep, x)
        row = lax.broadcasted_iota(jnp.int32, x.shape, 0)
        col = lax.broadcasted_iota(jnp.int32, x.shape, 1)
        for which, block in ((0, s), (1, mirror)):
            for h in range(2):
                chosen = (row == i + which * plane) & (col == partner[h, block])
                value = jnp.sum(
                    jnp.sum(jnp.where(chosen, x, 0.0), axis=1, keepdims=True), axis=0, keepdims=True
                )
                bias[which, h : h + 1, :] = jnp.broadcast_to(
                    value + math.log(2 * plane), (1, DH)
                )
            bias[which, 2:3, :] = jnp.max(counts[...], axis=0)

    @pl.when(p == 0)
    def _():
        most = jnp.maximum(count(0), count(1))
        counts[g] = jnp.full((1, DH), most, jnp.int32).astype(jnp.float32)
        pl.semaphore_wait(barrier, plane - 1 + groups - 1)
        each_group(lambda og: to_column(s, og))
        each_group(
            lambda og: remote(
                counts.at[g], counts.at[g], count_send, count_recv, s, og
            ).start()
        )
        spread(0)
        spread(1)
        hand_on()
        tables()
        local()
        spread_done(0)
        fill(0)
        pl.semaphore_wait(ready, 1)
        bytes_wait(feat.at[pl.ds(0, 2 * groups - 1)], col_recv)

        def to_owner(sl, c):
            owner = sl * stride

            @pl.when(owner != i)
            def _():
                remote(col.at[:, sl], feat.at[i], feat_send, feat_recv, base + owner).start()

            @pl.when(owner == i)
            def _():
                pltpu.make_async_copy(col.at[:, sl], feat.at[i], feat_recv).start()

            return c

        lax.fori_loop(0, slices, to_owner, 0)
        spread_done(1)
        fill(1)

        @pl.when(i % stride == 0)
        def _():
            bytes_wait(feat, feat_recv)
            scores()
            owned()

        for h in range(2):
            edge_copy(h).start()
            exchange_start(h)
        early_previous()
        bytes_wait(counts.at[pl.ds(0, groups - 1)], count_recv)

        @pl.when(i % stride == 0)
        def _():
            bytes_wait(partial.at[pl.ds(0, slices - 1)], partial_recv)
            bytes_wait(feat.at[pl.ds(0, slices - 1)], feat_send)

        @pl.when(i % stride != 0)
        def _():
            bytes_wait(partial, partial_recv)
            bytes_wait(feat.at[pl.ds(0, slices)], feat_send)

        sinkhorn()
        crowd[...] = bias[0, 2:3, :]
        bias_copy.start()
        give_back(0)
        give_back(1)
        finish(0)
        finish(1)
        bytes_wait(col.at[pl.ds(0, 2), pl.ds(0, 2 * (groups - 1))], col_send)

        @pl.when(i % stride == 0)
        def _():
            for _ in range(plane - 1):
                bytes_wait(partial.at[0], partial_send)

        bytes_wait(counts.at[pl.ds(0, groups - 1)], count_send)
        for h in range(2):
            edge_copy(h).wait_send()
            exchange(h, 0).wait_send()
            exchange(h, 1).wait_send()
        bias_copy.wait_send()

    @pl.when(p == 1)
    def _():
        followers = sum(jnp.where(g == leader, 1, 0) for _, leader in turns)
        pl.semaphore_wait(barrier, plane - 1 + groups + followers)
        signal(ready, mirror)
        for og in range(groups):
            to_column(mirror, og)
        spread(0)
        spread(1)
        tables()
        spread_done(0)
        fill(0)

        for follower, _ in turns:

            @pl.when(g == follower)
            def _():
                pl.semaphore_wait(turn, 1)

        exchange_start(0)
        spread_done(1)
        fill(1)
        exchange_start(1)
        hand_on()
        exchange(0, 0).wait_send()
        exchange(0, 1).wait_send()
        for follower, leader in turns:

            @pl.when(g == leader)
            def _():
                signal(turn, s, follower)

        exchange(1, 0).wait_send()

        local()
        early_previous()
        give_back(0)
        give_back(1)
        bias_copy.wait_recv()
        crowd[...] = bias[0, 2:3, :]
        finish(0)
        finish(1)
        exchange(1, 1).wait_send()
        bytes_wait(col.at[pl.ds(0, 2), pl.ds(0, slices)], col_send)

    for h in range(2):
        bytes_wait(own[h].at[pl.ds(0, plane - 1)], spread_send.at[h])
        bytes_wait(pick.at[h, pl.ds(0, plane - 1)], back_send.at[h])

    @pl.when(i < plane - 1)
    def _():
        for h in range(2):
            bytes_wait(prev.at[h], prev_send.at[h])

    @pl.when(s > plane)
    def _():
        for h in range(2):
            bytes_wait(edge.at[h], extra_send.at[h])


def attention(plane, groups, slots, collective_id, name):
    piece = 2 * BS // plane
    seq = 2 * plane
    half = plane // 2
    width = 2 * DH
    slices = 2 * groups
    dma = pltpu.SemaphoreType.DMA
    hbm = pl.BlockSpec(memory_space=pl.ANY)
    vmem = pl.BlockSpec(memory_space=pltpu.VMEM)
    folded = (half, piece, width)
    one, two = dma(()), dma((2,))
    pieces = pltpu.VMEM((2, plane, piece, DH), jnp.bfloat16)
    head_pieces = pltpu.VMEM((plane, piece, DH), jnp.bfloat16)
    head_slots = pltpu.VMEM((slots, piece, DH), jnp.bfloat16)

    def call(queries, keys, values, partner):
        return pl.pallas_call(
            functools.partial(sparse_attention_kernel, plane, groups, slots),
            out_shape=(
                jax.ShapeDtypeStruct(queries.shape, queries.dtype),
                pltpu.VMEM((1, DH), jnp.float32),
            ),
            in_specs=[pl.BlockSpec(memory_space=pltpu.HBM), hbm, hbm, hbm],
            out_specs=(vmem, vmem),
            scratch_shapes=[
                pltpu.VMEM(folded, jnp.bfloat16),
                pltpu.VMEM((plane, piece, width), jnp.bfloat16),
                head_pieces,
                head_pieces,
                head_slots,
                head_slots,
                head_slots,
                head_slots,
                pltpu.VMEM((2, piece, DH), jnp.bfloat16),
                pieces,
                pieces,
                pieces,
                pltpu.VMEM((4, slices, 1, DH), jnp.float32),
                pltpu.VMEM((plane, 4, 1, DH), jnp.float32),
                pltpu.VMEM((slices, plane, max(DH, 2 * seq)), jnp.float32),
                pltpu.VMEM((groups, 1, DH), jnp.float32),
                pltpu.VMEM((2, 3, DH), jnp.float32),
                pltpu.VMEM((2, BS, 1), jnp.float32),
                pltpu.VMEM((2, BS, 1), jnp.float32),
                pltpu.VMEM((2, BS, DH), jnp.float32),
                pltpu.SMEM((2, plane + 2), jnp.int32),
                pltpu.SMEM((2, seq), jnp.int32),
                dma((4,)),
            ]
            + [one] * 10
            + [two] * 2
            + [dma((4,))] * 2
            + [two] * 7
            + [pltpu.SemaphoreType.REGULAR] * 2,
            compiler_params=pltpu.CompilerParams(
                collective_id=collective_id, has_side_effects=True
            ),
            name=name,
        )(partner, queries.reshape(folded), keys.reshape(folded), values.reshape(folded))

    return call


def solution(mesh):
    seq, groups = mesh.shape["seq"], mesh.shape["head"]
    plane = seq // 2
    slots = plane * SLOT_SHARE // 32
    packed = attention(plane, groups, slots, 0, "packed")
    whole = attention(plane, groups, plane, 1, "whole")

    def body(queries, keys, values, partner):
        attended, crowd = packed(queries, keys, values, partner)
        return lax.cond(
            crowd[0, 0] > slots,
            lambda: whole(queries, keys, values, partner)[0],
            lambda: attended,
        )

    return jax.shard_map(
        body,
        mesh=mesh,
        in_specs=(P("seq", "head"), P("seq", "head"), P("seq", "head"), P("head", None)),
        out_specs=P("seq", "head"),
        check_vma=False,
    )
```

```python
import functools
import math

import jax
import jax.numpy as jnp
from jax import lax
from jax.experimental import pallas as pl
from jax.experimental.pallas import tpu as pltpu
from jax.sharding import PartitionSpec as P

DH = 128
BS = 256
SINK_ITERS = 8
SHARPNESS = 2.0
SLOT_SHARE = 22
TURNS = ((3, 1), (5, 1), (7, 5))
HIGHEST = lax.Precision.HIGHEST
MESH = pl.DeviceIdType.MESH


def far_first(size):
    return sorted(range(size), key=lambda o: (min(o, size - o) == 0, -min(o, size - o)))


def bytes_wait(ref, sem):
    pltpu.make_async_copy(ref, ref, sem).wait()


def sparse_attention_kernel(
    plane,
    groups,
    slots,
    partner_hbm,
    q_hbm,
    k_hbm,
    v_hbm,
    out,
    crowd,
    qs,
    kv,
    own_a,
    own_b,
    pack_a,
    pack_b,
    slot_a,
    slot_b,
    edge,
    pick,
    part,
    prev,
    col,
    feat,
    partial,
    counts,
    bias,
    top_all,
    den_all,
    mix_all,
    after,
    partner,
    load_sem,
    col_send,
    col_recv,
    count_send,
    count_recv,
    feat_send,
    feat_recv,
    partial_send,
    partial_recv,
    bias_send,
    bias_recv,
    spread_send,
    spread_recv,
    z_send,
    z_recv,
    edge_send,
    edge_recv,
    back_send,
    back_recv,
    prev_send,
    extra_send,
    prev_recv,
    ready,
    turn,
):
    own = (own_a, own_b)
    pack = (pack_a, pack_b)
    slot = (slot_a, slot_b)
    s = lax.axis_index("seq")
    g = lax.axis_index("head")
    p = s // plane
    i = s % plane
    base = p * plane
    mirror = (s + plane) % (2 * plane)
    half = plane // 2
    across = plane - base
    slices = 2 * groups
    stride = plane // slices
    inv_scale = 1.0 / math.sqrt(DH)

    def remote(src, dst, ss, rs, seq, head=None):
        return pltpu.make_async_remote_copy(
            src_ref=src,
            dst_ref=dst,
            send_sem=ss,
            recv_sem=rs,
            device_id=(seq, g if head is None else head),
            device_id_type=MESH,
        )

    def signal(sem, seq, head=None):
        pl.semaphore_signal(
            sem,
            inc=1,
            device_id=(seq, g if head is None else head),
            device_id_type=MESH,
        )

    x_size = 4 if plane % 8 == 0 else 1
    y_size = plane // (2 * x_size)
    x_at, y_at = i // (2 * y_size), i // 2 % y_size
    y_order = [(y_at + o) % y_size * 2 for o in far_first(y_size)]
    cores = [1 - i % 2, i % 2]

    def each_peer(body):
        def line(k, carry):
            o = 0
            for at, offset in enumerate(far_first(x_size)):
                o = jnp.where(k == at, offset, o)
            x = (x_at + o) % x_size * (2 * y_size)
            near = None
            for y in y_order:
                for core in cores:
                    near = x + y + core
                    if y is y_order[-1] and core is cores[-1]:
                        break
                    body(near, base + near)

            @pl.when(k < x_size - 1)
            def _():
                body(near, base + near)

            return carry

        lax.fori_loop(0, x_size, line, 0)

    def each_group(body):
        def wrapped(o, c):
            body((g + o) % groups)
            return c

        lax.fori_loop(1, groups, wrapped, 0)

    turns = [(f, l) for f, l in TURNS if f < groups]
    barrier = pltpu.get_barrier_semaphore()

    @pl.when(p == 0)
    def _():
        for og in range(groups):
            signal(barrier, mirror, og)
        each_group(lambda og: signal(barrier, s, og))

    for follower, leader in turns:

        @pl.when((p == 1) & (g == follower))
        def _():
            signal(barrier, s, leader)

    each_peer(lambda j, d: signal(barrier, d))

    loads = (
        pltpu.make_async_copy(partner_hbm, partner, load_sem.at[3]),
        pltpu.make_async_copy(q_hbm, qs, load_sem.at[0]),
        pltpu.make_async_copy(k_hbm, kv.at[pl.ds(0, half)], load_sem.at[1]),
        pltpu.make_async_copy(v_hbm, kv.at[pl.ds(half, half)], load_sem.at[2]),
    )
    for c in loads:
        c.start()
    for c in loads:
        c.wait()
    pooled_q = jnp.sum(jnp.sum(qs[...].astype(jnp.float32), axis=0), axis=0, keepdims=True)
    pooled_k = jnp.sum(
        jnp.sum(kv[pl.ds(0, half)].astype(jnp.float32), axis=0), axis=0, keepdims=True
    )
    for h in range(2):
        lanes = slice(h * DH, (h + 1) * DH)
        col[p, 2 * g + h] = pooled_q[:, lanes] / math.sqrt(BS)
        col[2 + p, 2 * g + h] = pooled_k[:, lanes] / math.sqrt(BS)

    def here(block):
        return (block >= base) & (block < base + plane)

    def tables():
        for h in range(2):
            after[h, plane] = plane
            after[h, plane + 1] = plane

            def link(o, c):
                d = plane - 1 - o
                after[h, d] = jnp.where(here(partner[h, across + d]), d, after[h, d + 1])
                return c

            lax.fori_loop(0, plane, link, 0)

    def count(h):
        def add(d, n):
            return n + jnp.where(here(partner[h, across + d]), 1, 0)

        return lax.fori_loop(0, plane, add, 0)

    def to_column(seq, head):
        rows = pl.ds(2 * g, 2)
        for kind in (p, 2 + p):
            remote(col.at[kind, rows], col.at[kind, rows], col_send, col_recv, seq, head).start()

    bias_copy = remote(bias.at[1], bias.at[0], bias_send, bias_recv, mirror)

    def spread(h):
        lanes = pl.ds(h * DH, DH)
        pltpu.make_async_copy(kv.at[i, :, lanes], own[h].at[i], spread_recv.at[h]).start()
        each_peer(
            lambda j, d: remote(
                kv.at[j, :, lanes], own[h].at[i], spread_send.at[h], spread_recv.at[h], d
            ).start()
        )

    def hand_on():
        @pl.when(i < plane - 1)
        def _():
            for h in range(2):
                lanes = pl.ds(h * DH, DH)
                remote(
                    kv.at[:, :, lanes], prev.at[h], prev_send.at[h], prev_recv.at[h], s + 1
                ).start()

    cuts = (0, slots - slots * 5 // 8, slots)

    def exchange(h, part_id):
        rows = pl.ds(cuts[part_id], cuts[part_id + 1] - cuts[part_id])
        sems = 2 * h + part_id
        return remote(
            pack[h].at[rows], slot[h].at[rows], z_send.at[sems], z_recv.at[sems], mirror
        )

    def exchange_start(h):
        exchange(h, 0).start()
        exchange(h, 1).start()

    def edge_copy(h):
        return remote(own[h].at[plane - 1], edge.at[h], edge_send.at[h], edge_recv.at[h], mirror)

    def spread_done(h):
        bytes_wait(own[h], spread_recv.at[h])

    def fill(h):
        def take(k, at):
            d = after[h, at]
            block = partner[h, across + jnp.minimum(d, plane - 1)]
            pack[h][k] = own[h][jnp.clip(block - base, 0, plane - 1)]
            return d + 1

        lax.fori_loop(0, slots, take, 0, unroll=2)

    def give_back(h):
        exchange(h, 0).wait_recv()
        exchange(h, 1).wait_recv()

        def choose(j, taken):
            block = partner[h, base + j]
            near = here(block)
            mine = own[h][jnp.clip(block - base, 0, plane - 1)]
            theirs = slot[h][jnp.minimum(taken, slots - 1)]
            pick[h, j] = jnp.where(near, mine, theirs)
            return taken + jnp.where(near, 0, 1)

        lax.fori_loop(0, plane, choose, 0, unroll=4)
        each_peer(
            lambda j, d: remote(
                pick.at[h, j], part.at[h, i], back_send.at[h], back_recv.at[h], d
            ).start()
        )
        pltpu.make_async_copy(pick.at[h, i], part.at[h, i], back_recv.at[h]).start()

        @pl.when(s == plane)
        def _():
            bytes_wait(edge.at[h], edge_recv.at[h])
            pltpu.make_async_copy(edge.at[h], prev.at[h, 0], prev_recv.at[h]).start()

        @pl.when(s > plane)
        def _():
            bytes_wait(edge.at[h], edge_recv.at[h])
            remote(edge.at[h], prev.at[h, i], extra_send.at[h], prev_recv.at[h], base).start()

    def query(h):
        return qs[:, :, h * DH : (h + 1) * DH].reshape(BS, DH)

    def scored(h, key):
        x = lax.dot_general(
            query(h), key, (((1,), (1,)), ((), ())), preferred_element_type=jnp.float32
        )
        return x * inv_scale

    def stacked(ref, h):
        return (
            ref[h, 0:half].reshape(BS, DH),
            ref[h, half:plane].reshape(BS, DH),
        )

    def local():
        for h in range(2):
            lanes = slice(h * DH, (h + 1) * DH)
            x = scored(h, kv[0:half, :, lanes].reshape(BS, DH))
            top = jnp.max(x, axis=1, keepdims=True)
            e = jnp.exp(x - top)
            top_all[h] = top
            den_all[h] = jnp.sum(e, axis=1, keepdims=True)
            mix_all[h] = jnp.dot(
                e.astype(jnp.bfloat16),
                kv[half:plane, :, lanes].reshape(BS, DH),
                preferred_element_type=jnp.float32,
            )

    def merged(h, ref, shift):
        key, val = stacked(ref, h)
        x = scored(h, key)
        if shift is not None:
            x = x + shift
        old = top_all[h]
        top = jnp.maximum(old, jnp.max(x, axis=1, keepdims=True))
        keep = jnp.exp(old - top)
        e = jnp.exp(x - top)
        den = den_all[h] * keep + jnp.sum(e, axis=1, keepdims=True)
        mix = mix_all[h] * keep + jnp.dot(
            e.astype(jnp.bfloat16), val, preferred_element_type=jnp.float32
        )
        return top, den, mix

    def previous(h):
        top, den, mix = merged(h, prev, None)
        top_all[h] = top
        den_all[h] = den
        mix_all[h] = mix

    def early_previous():
        @pl.when(i > 0)
        def _():
            for h in range(2):
                bytes_wait(prev.at[h], prev_recv.at[h])
                previous(h)

    def late_previous(h):
        @pl.when(s == plane)
        def _():
            bytes_wait(prev.at[h], prev_recv.at[h])
            previous(h)

    def finish(h):
        late_previous(h)
        bytes_wait(part.at[h], back_recv.at[h])
        _, den, mix = merged(h, part, bias[0, h : h + 1, 0:1])
        out[:, h * DH : (h + 1) * DH] = (mix * (1.0 / den)).astype(jnp.bfloat16)

    def owned():
        mine = i // stride
        each_peer(
            lambda j, d: remote(
                partial.at[mine], partial.at[mine], partial_send, partial_recv, d
            ).start()
        )

    def scores():
        queries = jnp.concatenate([feat[:, 0, 0, :], feat[:, 1, 0, :]], axis=0)
        keys = jnp.concatenate([feat[:, 2, 0, :], feat[:, 3, 0, :]], axis=0)
        x = lax.dot_general(
            queries,
            keys,
            (((1,), (1,)), ((), ())),
            precision=HIGHEST,
            preferred_element_type=jnp.float32,
        )
        x = x * (SHARPNESS / math.sqrt(2 * DH * groups))
        partial[i // stride, :, 0 : 2 * plane] = x[0:plane]
        partial[i // stride, :, 2 * plane : 4 * plane] = x[plane : 2 * plane]

    def sinkhorn():
        both = jnp.sum(partial[...], axis=0)
        x = jnp.concatenate([both[:, 0 : 2 * plane], both[:, 2 * plane : 4 * plane]], axis=0)

        def sweep(_, x):
            for along in (1, 0):
                top = jnp.max(x, axis=along, keepdims=True)
                x = x - (top + jnp.log(jnp.sum(jnp.exp(x - top), axis=along, keepdims=True)))
            return x

        x = lax.fori_loop(0, SINK_ITERS, sweep, x)
        row = lax.broadcasted_iota(jnp.int32, x.shape, 0)
        col = lax.broadcasted_iota(jnp.int32, x.shape, 1)
        for which, block in ((0, s), (1, mirror)):
            for h in range(2):
                chosen = (row == i + which * plane) & (col == partner[h, block])
                value = jnp.sum(
                    jnp.sum(jnp.where(chosen, x, 0.0), axis=1, keepdims=True), axis=0, keepdims=True
                )
                bias[which, h : h + 1, :] = jnp.broadcast_to(
                    value + math.log(2 * plane), (1, DH)
                )
            bias[which, 2:3, :] = jnp.max(counts[...], axis=0)

    @pl.when(p == 0)
    def _():
        most = jnp.maximum(count(0), count(1))
        counts[g] = jnp.full((1, DH), most, jnp.int32).astype(jnp.float32)
        pl.semaphore_wait(barrier, plane - 1 + groups - 1)
        each_group(lambda og: to_column(s, og))
        each_group(
            lambda og: remote(
                counts.at[g], counts.at[g], count_send, count_recv, s, og
            ).start()
        )
        spread(0)
        spread(1)
        hand_on()
        tables()
        local()
        spread_done(0)
        fill(0)
        pl.semaphore_wait(ready, 1)
        bytes_wait(feat.at[pl.ds(0, 2 * groups - 1)], col_recv)

        def to_owner(sl, c):
            owner = sl * stride

            @pl.when(owner != i)
            def _():
                remote(col.at[:, sl], feat.at[i], feat_send, feat_recv, base + owner).start()

            @pl.when(owner == i)
            def _():
                pltpu.make_async_copy(col.at[:, sl], feat.at[i], feat_recv).start()

            return c

        lax.fori_loop(0, slices, to_owner, 0)
        spread_done(1)
        fill(1)

        @pl.when(i % stride == 0)
        def _():
            bytes_wait(feat, feat_recv)
            scores()
            owned()

        for h in range(2):
            edge_copy(h).start()
            exchange_start(h)
        early_previous()
        bytes_wait(counts.at[pl.ds(0, groups - 1)], count_recv)

        @pl.when(i % stride == 0)
        def _():
            bytes_wait(partial.at[pl.ds(0, slices - 1)], partial_recv)
            bytes_wait(feat.at[pl.ds(0, slices - 1)], feat_send)

        @pl.when(i % stride != 0)
        def _():
            bytes_wait(partial, partial_recv)
            bytes_wait(feat.at[pl.ds(0, slices)], feat_send)

        sinkhorn()
        crowd[...] = bias[0, 2:3, :]
        bias_copy.start()
        give_back(0)
        give_back(1)
        finish(0)
        finish(1)
        bytes_wait(col.at[pl.ds(0, 2), pl.ds(0, 2 * (groups - 1))], col_send)

        @pl.when(i % stride == 0)
        def _():
            for _ in range(plane - 1):
                bytes_wait(partial.at[0], partial_send)

        bytes_wait(counts.at[pl.ds(0, groups - 1)], count_send)
        for h in range(2):
            edge_copy(h).wait_send()
            exchange(h, 0).wait_send()
            exchange(h, 1).wait_send()
        bias_copy.wait_send()

    @pl.when(p == 1)
    def _():
        followers = sum(jnp.where(g == leader, 1, 0) for _, leader in turns)
        pl.semaphore_wait(barrier, plane - 1 + groups + followers)
        signal(ready, mirror)
        for og in range(groups):
            to_column(mirror, og)
        spread(0)
        spread(1)
        tables()
        spread_done(0)
        fill(0)

        for follower, _ in turns:

            @pl.when(g == follower)
            def _():
                pl.semaphore_wait(turn, 1)

        exchange_start(0)
        spread_done(1)
        fill(1)
        exchange_start(1)
        hand_on()
        exchange(0, 0).wait_send()
        exchange(0, 1).wait_send()
        for follower, leader in turns:

            @pl.when(g == leader)
            def _():
                signal(turn, s, follower)

        exchange(1, 0).wait_send()

        local()
        early_previous()
        give_back(0)
        give_back(1)
        bias_copy.wait_recv()
        crowd[...] = bias[0, 2:3, :]
        finish(0)
        finish(1)
        exchange(1, 1).wait_send()
        bytes_wait(col.at[pl.ds(0, 2), pl.ds(0, slices)], col_send)

    for h in range(2):
        bytes_wait(own[h].at[pl.ds(0, plane - 1)], spread_send.at[h])
        bytes_wait(pick.at[h, pl.ds(0, plane - 1)], back_send.at[h])

    @pl.when(i < plane - 1)
    def _():
        for h in range(2):
            bytes_wait(prev.at[h], prev_send.at[h])

    @pl.when(s > plane)
    def _():
        for h in range(2):
            bytes_wait(edge.at[h], extra_send.at[h])


def attention(plane, groups, slots, collective_id, name):
    piece = 2 * BS // plane
    seq = 2 * plane
    half = plane // 2
    width = 2 * DH
    slices = 2 * groups
    dma = pltpu.SemaphoreType.DMA
    hbm = pl.BlockSpec(memory_space=pl.ANY)
    vmem = pl.BlockSpec(memory_space=pltpu.VMEM)
    folded = (half, piece, width)
    one, two = dma(()), dma((2,))
    pieces = pltpu.VMEM((2, plane, piece, DH), jnp.bfloat16)
    head_pieces = pltpu.VMEM((plane, piece, DH), jnp.bfloat16)
    head_slots = pltpu.VMEM((slots, piece, DH), jnp.bfloat16)

    def call(queries, keys, values, partner):
        return pl.pallas_call(
            functools.partial(sparse_attention_kernel, plane, groups, slots),
            out_shape=(
                jax.ShapeDtypeStruct(queries.shape, queries.dtype),
                pltpu.VMEM((1, DH), jnp.float32),
            ),
            in_specs=[pl.BlockSpec(memory_space=pltpu.HBM), hbm, hbm, hbm],
            out_specs=(vmem, vmem),
            scratch_shapes=[
                pltpu.VMEM(folded, jnp.bfloat16),
                pltpu.VMEM((plane, piece, width), jnp.bfloat16),
                head_pieces,
                head_pieces,
                head_slots,
                head_slots,
                head_slots,
                head_slots,
                pltpu.VMEM((2, piece, DH), jnp.bfloat16),
                pieces,
                pieces,
                pieces,
                pltpu.VMEM((4, slices, 1, DH), jnp.float32),
                pltpu.VMEM((plane, 4, 1, DH), jnp.float32),
                pltpu.VMEM((slices, plane, max(DH, 2 * seq)), jnp.float32),
                pltpu.VMEM((groups, 1, DH), jnp.float32),
                pltpu.VMEM((2, 3, DH), jnp.float32),
                pltpu.VMEM((2, BS, 1), jnp.float32),
                pltpu.VMEM((2, BS, 1), jnp.float32),
                pltpu.VMEM((2, BS, DH), jnp.float32),
                pltpu.SMEM((2, plane + 2), jnp.int32),
                pltpu.SMEM((2, seq), jnp.int32),
                dma((4,)),
            ]
            + [one] * 10
            + [two] * 2
            + [dma((4,))] * 2
            + [two] * 7
            + [pltpu.SemaphoreType.REGULAR] * 2,
            compiler_params=pltpu.CompilerParams(
                collective_id=collective_id, has_side_effects=True
            ),
            name=name,
        )(partner, queries.reshape(folded), keys.reshape(folded), values.reshape(folded))

    return call


def solution(mesh):
    seq, groups = mesh.shape["seq"], mesh.shape["head"]
    plane = seq // 2
    slots = plane * SLOT_SHARE // 32
    packed = attention(plane, groups, slots, 0, "packed")
    whole = attention(plane, groups, plane, 1, "whole")

    def body(queries, keys, values, partner):
        attended, crowd = packed(queries, keys, values, partner)
        return lax.cond(
            crowd[0, 0] > slots,
            lambda: whole(queries, keys, values, partner)[0],
            lambda: attended,
        )

    return jax.shard_map(
        body,
        mesh=mesh,
        in_specs=(P("seq", "head"), P("seq", "head"), P("seq", "head"), P("head", None)),
        out_specs=P("seq", "head"),
        check_vma=False,
    )
```

```python
import functools
import math

import jax
import jax.numpy as jnp
from jax import lax
from jax.experimental import pallas as pl
from jax.experimental.pallas import tpu as pltpu
from jax.sharding import PartitionSpec as P

DH = 128
BS = 256
SINK_ITERS = 8
SHARPNESS = 2.0
SLOT_SHARE = 22
TURNS = ((3, 1), (5, 1), (7, 5))
HIGHEST = lax.Precision.HIGHEST
MESH = pl.DeviceIdType.MESH


def far_first(size):
    return sorted(range(size), key=lambda o: (min(o, size - o) == 0, -min(o, size - o)))


def bytes_wait(ref, sem):
    pltpu.make_async_copy(ref, ref, sem).wait()


def sparse_attention_kernel(
    plane,
    groups,
    slots,
    partner_hbm,
    q_hbm,
    k_hbm,
    v_hbm,
    out,
    crowd,
    qs,
    kv,
    own_a,
    own_b,
    pack_a,
    pack_b,
    slot_a,
    slot_b,
    edge,
    pick,
    part,
    prev,
    col,
    feat,
    partial,
    counts,
    bias,
    top_all,
    den_all,
    mix_all,
    after,
    partner,
    load_sem,
    col_send,
    col_recv,
    count_send,
    count_recv,
    feat_send,
    feat_recv,
    partial_send,
    partial_recv,
    bias_send,
    bias_recv,
    spread_send,
    spread_recv,
    z_send,
    z_recv,
    edge_send,
    edge_recv,
    back_send,
    back_recv,
    prev_send,
    extra_send,
    prev_recv,
    ready,
    turn,
):
    own = (own_a, own_b)
    pack = (pack_a, pack_b)
    slot = (slot_a, slot_b)
    s = lax.axis_index("seq")
    g = lax.axis_index("head")
    p = s // plane
    i = s % plane
    base = p * plane
    mirror = (s + plane) % (2 * plane)
    half = plane // 2
    across = plane - base
    slices = 2 * groups
    stride = plane // slices
    inv_scale = 1.0 / math.sqrt(DH)

    def remote(src, dst, ss, rs, seq, head=None):
        return pltpu.make_async_remote_copy(
            src_ref=src,
            dst_ref=dst,
            send_sem=ss,
            recv_sem=rs,
            device_id=(seq, g if head is None else head),
            device_id_type=MESH,
        )

    def signal(sem, seq, head=None):
        pl.semaphore_signal(
            sem,
            inc=1,
            device_id=(seq, g if head is None else head),
            device_id_type=MESH,
        )

    x_size = 4 if plane % 8 == 0 else 1
    y_size = plane // (2 * x_size)
    x_at, y_at = i // (2 * y_size), i // 2 % y_size
    y_order = [(y_at + o) % y_size * 2 for o in far_first(y_size)]
    cores = [1 - i % 2, i % 2]

    def each_peer(body):
        def line(k, carry):
            o = 0
            for at, offset in enumerate(far_first(x_size)):
                o = jnp.where(k == at, offset, o)
            x = (x_at + o) % x_size * (2 * y_size)
            near = None
            for y in y_order:
                for core in cores:
                    near = x + y + core
                    if y is y_order[-1] and core is cores[-1]:
                        break
                    body(near, base + near)

            @pl.when(k < x_size - 1)
            def _():
                body(near, base + near)

            return carry

        lax.fori_loop(0, x_size, line, 0)

    def each_group(body):
        def wrapped(o, c):
            body((g + o) % groups)
            return c

        lax.fori_loop(1, groups, wrapped, 0)

    turns = [(f, l) for f, l in TURNS if f < groups]
    barrier = pltpu.get_barrier_semaphore()

    @pl.when(p == 0)
    def _():
        for og in range(groups):
            signal(barrier, mirror, og)
        each_group(lambda og: signal(barrier, s, og))

    for follower, leader in turns:

        @pl.when((p == 1) & (g == follower))
        def _():
            signal(barrier, s, leader)

    each_peer(lambda j, d: signal(barrier, d))

    loads = (
        pltpu.make_async_copy(partner_hbm, partner, load_sem.at[3]),
        pltpu.make_async_copy(q_hbm, qs, load_sem.at[0]),
        pltpu.make_async_copy(k_hbm, kv.at[pl.ds(0, half)], load_sem.at[1]),
        pltpu.make_async_copy(v_hbm, kv.at[pl.ds(half, half)], load_sem.at[2]),
    )
    for c in loads:
        c.start()
    for c in loads:
        c.wait()
    pooled_q = jnp.sum(jnp.sum(qs[...].astype(jnp.float32), axis=0), axis=0, keepdims=True)
    pooled_k = jnp.sum(
        jnp.sum(kv[pl.ds(0, half)].astype(jnp.float32), axis=0), axis=0, keepdims=True
    )
    for h in range(2):
        lanes = slice(h * DH, (h + 1) * DH)
        col[p, 2 * g + h] = pooled_q[:, lanes] / math.sqrt(BS)
        col[2 + p, 2 * g + h] = pooled_k[:, lanes] / math.sqrt(BS)

    def here(block):
        return (block >= base) & (block < base + plane)

    def tables():
        for h in range(2):
            after[h, plane] = plane
            after[h, plane + 1] = plane

            def link(o, c):
                d = plane - 1 - o
                after[h, d] = jnp.where(here(partner[h, across + d]), d, after[h, d + 1])
                return c

            lax.fori_loop(0, plane, link, 0)

    def count(h):
        def add(d, n):
            return n + jnp.where(here(partner[h, across + d]), 1, 0)

        return lax.fori_loop(0, plane, add, 0)

    def to_column(seq, head):
        rows = pl.ds(2 * g, 2)
        for kind in (p, 2 + p):
            remote(col.at[kind, rows], col.at[kind, rows], col_send, col_recv, seq, head).start()

    bias_copy = remote(bias.at[1], bias.at[0], bias_send, bias_recv, mirror)

    def spread(h):
        lanes = pl.ds(h * DH, DH)
        pltpu.make_async_copy(kv.at[i, :, lanes], own[h].at[i], spread_recv.at[h]).start()
        each_peer(
            lambda j, d: remote(
                kv.at[j, :, lanes], own[h].at[i], spread_send.at[h], spread_recv.at[h], d
            ).start()
        )

    def hand_on():
        @pl.when(i < plane - 1)
        def _():
            for h in range(2):
                lanes = pl.ds(h * DH, DH)
                remote(
                    kv.at[:, :, lanes], prev.at[h], prev_send.at[h], prev_recv.at[h], s + 1
                ).start()

    cuts = (0, slots - slots * 5 // 8, slots)

    def exchange(h, part_id):
        rows = pl.ds(cuts[part_id], cuts[part_id + 1] - cuts[part_id])
        sems = 2 * h + part_id
        return remote(
            pack[h].at[rows], slot[h].at[rows], z_send.at[sems], z_recv.at[sems], mirror
        )

    def exchange_start(h):
        exchange(h, 0).start()
        exchange(h, 1).start()

    def edge_copy(h):
        return remote(own[h].at[plane - 1], edge.at[h], edge_send.at[h], edge_recv.at[h], mirror)

    def spread_done(h):
        bytes_wait(own[h], spread_recv.at[h])

    def fill(h):
        def take(k, at):
            d = after[h, at]
            block = partner[h, across + jnp.minimum(d, plane - 1)]
            pack[h][k] = own[h][jnp.clip(block - base, 0, plane - 1)]
            return d + 1

        lax.fori_loop(0, slots, take, 0, unroll=2)

    def give_back(h):
        exchange(h, 0).wait_recv()
        exchange(h, 1).wait_recv()

        def choose(j, taken):
            block = partner[h, base + j]
            near = here(block)
            mine = own[h][jnp.clip(block - base, 0, plane - 1)]
            theirs = slot[h][jnp.minimum(taken, slots - 1)]
            pick[h, j] = jnp.where(near, mine, theirs)
            return taken + jnp.where(near, 0, 1)

        lax.fori_loop(0, plane, choose, 0, unroll=4)
        each_peer(
            lambda j, d: remote(
                pick.at[h, j], part.at[h, i], back_send.at[h], back_recv.at[h], d
            ).start()
        )
        pltpu.make_async_copy(pick.at[h, i], part.at[h, i], back_recv.at[h]).start()

        @pl.when(s == plane)
        def _():
            bytes_wait(edge.at[h], edge_recv.at[h])
            pltpu.make_async_copy(edge.at[h], prev.at[h, 0], prev_recv.at[h]).start()

        @pl.when(s > plane)
        def _():
            bytes_wait(edge.at[h], edge_recv.at[h])
            remote(edge.at[h], prev.at[h, i], extra_send.at[h], prev_recv.at[h], base).start()

    def query(h):
        return qs[:, :, h * DH : (h + 1) * DH].reshape(BS, DH)

    def scored(h, key):
        x = lax.dot_general(
            query(h), key, (((1,), (1,)), ((), ())), preferred_element_type=jnp.float32
        )
        return x * inv_scale

    def stacked(ref, h):
        return (
            ref[h, 0:half].reshape(BS, DH),
            ref[h, half:plane].reshape(BS, DH),
        )

    def local():
        for h in range(2):
            lanes = slice(h * DH, (h + 1) * DH)
            x = scored(h, kv[0:half, :, lanes].reshape(BS, DH))
            top = jnp.max(x, axis=1, keepdims=True)
            e = jnp.exp(x - top)
            top_all[h] = top
            den_all[h] = jnp.sum(e, axis=1, keepdims=True)
            mix_all[h] = jnp.dot(
                e.astype(jnp.bfloat16),
                kv[half:plane, :, lanes].reshape(BS, DH),
                preferred_element_type=jnp.float32,
            )

    def merged(h, ref, shift):
        key, val = stacked(ref, h)
        x = scored(h, key)
        if shift is not None:
            x = x + shift
        old = top_all[h]
        top = jnp.maximum(old, jnp.max(x, axis=1, keepdims=True))
        keep = jnp.exp(old - top)
        e = jnp.exp(x - top)
        den = den_all[h] * keep + jnp.sum(e, axis=1, keepdims=True)
        mix = mix_all[h] * keep + jnp.dot(
            e.astype(jnp.bfloat16), val, preferred_element_type=jnp.float32
        )
        return top, den, mix

    def previous(h):
        top, den, mix = merged(h, prev, None)
        top_all[h] = top
        den_all[h] = den
        mix_all[h] = mix

    def early_previous():
        @pl.when(i > 0)
        def _():
            for h in range(2):
                bytes_wait(prev.at[h], prev_recv.at[h])
                previous(h)

    def late_previous(h):
        @pl.when(s == plane)
        def _():
            bytes_wait(prev.at[h], prev_recv.at[h])
            previous(h)

    def finish(h):
        late_previous(h)
        bytes_wait(part.at[h], back_recv.at[h])
        _, den, mix = merged(h, part, bias[0, h : h + 1, 0:1])
        out[:, h * DH : (h + 1) * DH] = (mix * (1.0 / den)).astype(jnp.bfloat16)

    def owned():
        mine = i // stride
        each_peer(
            lambda j, d: remote(
                partial.at[mine], partial.at[mine], partial_send, partial_recv, d
            ).start()
        )

    def scores():
        queries = jnp.concatenate([feat[:, 0, 0, :], feat[:, 1, 0, :]], axis=0)
        keys = jnp.concatenate([feat[:, 2, 0, :], feat[:, 3, 0, :]], axis=0)
        x = lax.dot_general(
            queries,
            keys,
            (((1,), (1,)), ((), ())),
            precision=HIGHEST,
            preferred_element_type=jnp.float32,
        )
        x = x * (SHARPNESS / math.sqrt(2 * DH * groups))
        partial[i // stride, :, 0 : 2 * plane] = x[0:plane]
        partial[i // stride, :, 2 * plane : 4 * plane] = x[plane : 2 * plane]

    def sinkhorn():
        both = jnp.sum(partial[...], axis=0)
        x = jnp.concatenate([both[:, 0 : 2 * plane], both[:, 2 * plane : 4 * plane]], axis=0)

        def sweep(_, x):
            for along in (1, 0):
                top = jnp.max(x, axis=along, keepdims=True)
                x = x - (top + jnp.log(jnp.sum(jnp.exp(x - top), axis=along, keepdims=True)))
            return x

        x = lax.fori_loop(0, SINK_ITERS, sweep, x)
        row = lax.broadcasted_iota(jnp.int32, x.shape, 0)
        col = lax.broadcasted_iota(jnp.int32, x.shape, 1)
        for which, block in ((0, s), (1, mirror)):
            for h in range(2):
                chosen = (row == i + which * plane) & (col == partner[h, block])
                value = jnp.sum(
                    jnp.sum(jnp.where(chosen, x, 0.0), axis=1, keepdims=True), axis=0, keepdims=True
                )
                bias[which, h : h + 1, :] = jnp.broadcast_to(
                    value + math.log(2 * plane), (1, DH)
                )
            bias[which, 2:3, :] = jnp.max(counts[...], axis=0)

    @pl.when(p == 0)
    def _():
        most = jnp.maximum(count(0), count(1))
        counts[g] = jnp.full((1, DH), most, jnp.int32).astype(jnp.float32)
        pl.semaphore_wait(barrier, plane - 1 + groups - 1)
        each_group(lambda og: to_column(s, og))
        each_group(
            lambda og: remote(
                counts.at[g], counts.at[g], count_send, count_recv, s, og
            ).start()
        )
        spread(0)
        spread(1)
        hand_on()
        tables()
        local()
        spread_done(0)
        fill(0)
        pl.semaphore_wait(ready, 1)
        bytes_wait(feat.at[pl.ds(0, 2 * groups - 1)], col_recv)

        def to_owner(sl, c):
            owner = sl * stride

            @pl.when(owner != i)
            def _():
                remote(col.at[:, sl], feat.at[i], feat_send, feat_recv, base + owner).start()

            @pl.when(owner == i)
            def _():
                pltpu.make_async_copy(col.at[:, sl], feat.at[i], feat_recv).start()

            return c

        lax.fori_loop(0, slices, to_owner, 0)
        spread_done(1)
        fill(1)

        @pl.when(i % stride == 0)
        def _():
            bytes_wait(feat, feat_recv)
            scores()
            owned()

        for h in range(2):
            edge_copy(h).start()
            exchange_start(h)
        early_previous()
        bytes_wait(counts.at[pl.ds(0, groups - 1)], count_recv)

        @pl.when(i % stride == 0)
        def _():
            bytes_wait(partial.at[pl.ds(0, slices - 1)], partial_recv)
            bytes_wait(feat.at[pl.ds(0, slices - 1)], feat_send)

        @pl.when(i % stride != 0)
        def _():
            bytes_wait(partial, partial_recv)
            bytes_wait(feat.at[pl.ds(0, slices)], feat_send)

        sinkhorn()
        crowd[...] = bias[0, 2:3, :]
        bias_copy.start()
        give_back(0)
        give_back(1)
        finish(0)
        finish(1)
        bytes_wait(col.at[pl.ds(0, 2), pl.ds(0, 2 * (groups - 1))], col_send)

        @pl.when(i % stride == 0)
        def _():
            for _ in range(plane - 1):
                bytes_wait(partial.at[0], partial_send)

        bytes_wait(counts.at[pl.ds(0, groups - 1)], count_send)
        for h in range(2):
            edge_copy(h).wait_send()
            exchange(h, 0).wait_send()
            exchange(h, 1).wait_send()
        bias_copy.wait_send()

    @pl.when(p == 1)
    def _():
        followers = sum(jnp.where(g == leader, 1, 0) for _, leader in turns)
        pl.semaphore_wait(barrier, plane - 1 + groups + followers)
        signal(ready, mirror)
        spread(0)
        for og in range(groups):
            to_column(mirror, og)
        spread(1)
        tables()
        spread_done(0)
        fill(0)

        for follower, _ in turns:

            @pl.when(g == follower)
            def _():
                pl.semaphore_wait(turn, 1)

        exchange_start(0)
        spread_done(1)
        fill(1)
        exchange_start(1)
        hand_on()
        exchange(0, 0).wait_send()
        exchange(0, 1).wait_send()
        for follower, leader in turns:

            @pl.when(g == leader)
            def _():
                signal(turn, s, follower)

        exchange(1, 0).wait_send()

        local()
        early_previous()
        give_back(0)
        give_back(1)
        bias_copy.wait_recv()
        crowd[...] = bias[0, 2:3, :]
        finish(0)
        finish(1)
        exchange(1, 1).wait_send()
        bytes_wait(col.at[pl.ds(0, 2), pl.ds(0, slices)], col_send)

    for h in range(2):
        bytes_wait(own[h].at[pl.ds(0, plane - 1)], spread_send.at[h])
        bytes_wait(pick.at[h, pl.ds(0, plane - 1)], back_send.at[h])

    @pl.when(i < plane - 1)
    def _():
        for h in range(2):
            bytes_wait(prev.at[h], prev_send.at[h])

    @pl.when(s > plane)
    def _():
        for h in range(2):
            bytes_wait(edge.at[h], extra_send.at[h])


def attention(plane, groups, slots, collective_id, name):
    piece = 2 * BS // plane
    seq = 2 * plane
    half = plane // 2
    width = 2 * DH
    slices = 2 * groups
    dma = pltpu.SemaphoreType.DMA
    hbm = pl.BlockSpec(memory_space=pl.ANY)
    vmem = pl.BlockSpec(memory_space=pltpu.VMEM)
    folded = (half, piece, width)
    one, two = dma(()), dma((2,))
    pieces = pltpu.VMEM((2, plane, piece, DH), jnp.bfloat16)
    head_pieces = pltpu.VMEM((plane, piece, DH), jnp.bfloat16)
    head_slots = pltpu.VMEM((slots, piece, DH), jnp.bfloat16)

    def call(queries, keys, values, partner):
        return pl.pallas_call(
            functools.partial(sparse_attention_kernel, plane, groups, slots),
            out_shape=(
                jax.ShapeDtypeStruct(queries.shape, queries.dtype),
                pltpu.VMEM((1, DH), jnp.float32),
            ),
            in_specs=[pl.BlockSpec(memory_space=pltpu.HBM), hbm, hbm, hbm],
            out_specs=(vmem, vmem),
            scratch_shapes=[
                pltpu.VMEM(folded, jnp.bfloat16),
                pltpu.VMEM((plane, piece, width), jnp.bfloat16),
                head_pieces,
                head_pieces,
                head_slots,
                head_slots,
                head_slots,
                head_slots,
                pltpu.VMEM((2, piece, DH), jnp.bfloat16),
                pieces,
                pieces,
                pieces,
                pltpu.VMEM((4, slices, 1, DH), jnp.float32),
                pltpu.VMEM((plane, 4, 1, DH), jnp.float32),
                pltpu.VMEM((slices, plane, max(DH, 2 * seq)), jnp.float32),
                pltpu.VMEM((groups, 1, DH), jnp.float32),
                pltpu.VMEM((2, 3, DH), jnp.float32),
                pltpu.VMEM((2, BS, 1), jnp.float32),
                pltpu.VMEM((2, BS, 1), jnp.float32),
                pltpu.VMEM((2, BS, DH), jnp.float32),
                pltpu.SMEM((2, plane + 2), jnp.int32),
                pltpu.SMEM((2, seq), jnp.int32),
                dma((4,)),
            ]
            + [one] * 10
            + [two] * 2
            + [dma((4,))] * 2
            + [two] * 7
            + [pltpu.SemaphoreType.REGULAR] * 2,
            compiler_params=pltpu.CompilerParams(
                collective_id=collective_id, has_side_effects=True
            ),
            name=name,
        )(partner, queries.reshape(folded), keys.reshape(folded), values.reshape(folded))

    return call


def solution(mesh):
    seq, groups = mesh.shape["seq"], mesh.shape["head"]
    plane = seq // 2
    slots = plane * SLOT_SHARE // 32
    packed = attention(plane, groups, slots, 0, "packed")
    whole = attention(plane, groups, plane, 1, "whole")

    def body(queries, keys, values, partner):
        attended, crowd = packed(queries, keys, values, partner)
        return lax.cond(
            crowd[0, 0] > slots,
            lambda: whole(queries, keys, values, partner)[0],
            lambda: attended,
        )

    return jax.shard_map(
        body,
        mesh=mesh,
        in_specs=(P("seq", "head"), P("seq", "head"), P("seq", "head"), P("head", None)),
        out_specs=P("seq", "head"),
        check_vma=False,
    )
```

```python
import functools
import math

import jax
import jax.numpy as jnp
from jax import lax
from jax.experimental import pallas as pl
from jax.experimental.pallas import tpu as pltpu
from jax.sharding import PartitionSpec as P

DH = 128
BS = 256
SINK_ITERS = 8
SHARPNESS = 2.0
SLOT_SHARE = 22
TURNS = ((3, 1), (5, 1), (7, 5))
HIGHEST = lax.Precision.HIGHEST
MESH = pl.DeviceIdType.MESH


def far_first(size):
    return sorted(range(size), key=lambda o: (min(o, size - o) == 0, -min(o, size - o)))


def bytes_wait(ref, sem):
    pltpu.make_async_copy(ref, ref, sem).wait()


def sparse_attention_kernel(
    plane,
    groups,
    slots,
    partner_hbm,
    q_hbm,
    k_hbm,
    v_hbm,
    out,
    crowd,
    qs,
    kv,
    own_a,
    own_b,
    pack_a,
    pack_b,
    slot_a,
    slot_b,
    edge,
    pick,
    part,
    prev,
    col,
    feat,
    partial,
    counts,
    bias,
    top_all,
    den_all,
    mix_all,
    after,
    partner,
    load_sem,
    col_send,
    col_recv,
    count_send,
    count_recv,
    feat_send,
    feat_recv,
    partial_send,
    partial_recv,
    bias_send,
    bias_recv,
    spread_send,
    spread_recv,
    z_send,
    z_recv,
    edge_send,
    edge_recv,
    back_send,
    back_recv,
    prev_send,
    extra_send,
    prev_recv,
    ready,
    turn,
):
    own = (own_a, own_b)
    pack = (pack_a, pack_b)
    slot = (slot_a, slot_b)
    s = lax.axis_index("seq")
    g = lax.axis_index("head")
    p = s // plane
    i = s % plane
    base = p * plane
    mirror = (s + plane) % (2 * plane)
    half = plane // 2
    across = plane - base
    slices = 2 * groups
    stride = plane // slices
    inv_scale = 1.0 / math.sqrt(DH)

    def remote(src, dst, ss, rs, seq, head=None):
        return pltpu.make_async_remote_copy(
            src_ref=src,
            dst_ref=dst,
            send_sem=ss,
            recv_sem=rs,
            device_id=(seq, g if head is None else head),
            device_id_type=MESH,
        )

    def signal(sem, seq, head=None):
        pl.semaphore_signal(
            sem,
            inc=1,
            device_id=(seq, g if head is None else head),
            device_id_type=MESH,
        )

    x_size = 4 if plane % 8 == 0 else 1
    y_size = plane // (2 * x_size)
    x_at, y_at = i // (2 * y_size), i // 2 % y_size
    y_order = [(y_at + o) % y_size * 2 for o in far_first(y_size)]
    cores = [1 - i % 2, i % 2]

    def each_peer(body):
        def line(k, carry):
            o = 0
            for at, offset in enumerate(far_first(x_size)):
                o = jnp.where(k == at, offset, o)
            x = (x_at + o) % x_size * (2 * y_size)
            near = None
            for y in y_order:
                for core in cores:
                    near = x + y + core
                    if y is y_order[-1] and core is cores[-1]:
                        break
                    body(near, base + near)

            @pl.when(k < x_size - 1)
            def _():
                body(near, base + near)

            return carry

        lax.fori_loop(0, x_size, line, 0)

    def each_group(body):
        def wrapped(o, c):
            body((g + o) % groups)
            return c

        lax.fori_loop(1, groups, wrapped, 0)

    turns = [(f, l) for f, l in TURNS if f < groups]
    barrier = pltpu.get_barrier_semaphore()

    @pl.when(p == 0)
    def _():
        for og in range(groups):
            signal(barrier, mirror, og)
        each_group(lambda og: signal(barrier, s, og))

    for follower, leader in turns:

        @pl.when((p == 1) & (g == follower))
        def _():
            signal(barrier, s, leader)

    each_peer(lambda j, d: signal(barrier, d))

    loads = (
        pltpu.make_async_copy(partner_hbm, partner, load_sem.at[3]),
        pltpu.make_async_copy(q_hbm, qs, load_sem.at[0]),
        pltpu.make_async_copy(k_hbm, kv.at[pl.ds(0, half)], load_sem.at[1]),
        pltpu.make_async_copy(v_hbm, kv.at[pl.ds(half, half)], load_sem.at[2]),
    )
    for c in loads:
        c.start()
    for c in loads:
        c.wait()
    pooled_q = jnp.sum(jnp.sum(qs[...].astype(jnp.float32), axis=0), axis=0, keepdims=True)
    pooled_k = jnp.sum(
        jnp.sum(kv[pl.ds(0, half)].astype(jnp.float32), axis=0), axis=0, keepdims=True
    )
    for h in range(2):
        lanes = slice(h * DH, (h + 1) * DH)
        col[p, 2 * g + h] = pooled_q[:, lanes] / math.sqrt(BS)
        col[2 + p, 2 * g + h] = pooled_k[:, lanes] / math.sqrt(BS)

    def here(block):
        return (block >= base) & (block < base + plane)

    def tables():
        for h in range(2):
            after[h, plane] = plane
            after[h, plane + 1] = plane

            def link(o, c):
                d = plane - 1 - o
                after[h, d] = jnp.where(here(partner[h, across + d]), d, after[h, d + 1])
                return c

            lax.fori_loop(0, plane, link, 0, unroll=4)

    def count(h):
        def add(d, n):
            return n + jnp.where(here(partner[h, across + d]), 1, 0)

        return lax.fori_loop(0, plane, add, 0, unroll=4)

    def to_column(seq, head):
        rows = pl.ds(2 * g, 2)
        for kind in (p, 2 + p):
            remote(col.at[kind, rows], col.at[kind, rows], col_send, col_recv, seq, head).start()

    bias_copy = remote(bias.at[1], bias.at[0], bias_send, bias_recv, mirror)

    def spread(h):
        lanes = pl.ds(h * DH, DH)
        pltpu.make_async_copy(kv.at[i, :, lanes], own[h].at[i], spread_recv.at[h]).start()
        each_peer(
            lambda j, d: remote(
                kv.at[j, :, lanes], own[h].at[i], spread_send.at[h], spread_recv.at[h], d
            ).start()
        )

    def hand_on():
        @pl.when(i < plane - 1)
        def _():
            for h in range(2):
                lanes = pl.ds(h * DH, DH)
                remote(
                    kv.at[:, :, lanes], prev.at[h], prev_send.at[h], prev_recv.at[h], s + 1
                ).start()

    cuts = (0, slots - slots * 5 // 8, slots)

    def exchange(h, part_id):
        rows = pl.ds(cuts[part_id], cuts[part_id + 1] - cuts[part_id])
        sems = 2 * h + part_id
        return remote(
            pack[h].at[rows], slot[h].at[rows], z_send.at[sems], z_recv.at[sems], mirror
        )

    def exchange_start(h):
        exchange(h, 0).start()
        exchange(h, 1).start()

    def edge_copy(h):
        return remote(own[h].at[plane - 1], edge.at[h], edge_send.at[h], edge_recv.at[h], mirror)

    def spread_done(h):
        bytes_wait(own[h], spread_recv.at[h])

    def fill(h):
        def take(k, at):
            d = after[h, at]
            block = partner[h, across + jnp.minimum(d, plane - 1)]
            pack[h][k] = own[h][jnp.clip(block - base, 0, plane - 1)]
            return d + 1

        lax.fori_loop(0, slots, take, 0, unroll=2)

    def give_back(h):
        exchange(h, 0).wait_recv()
        exchange(h, 1).wait_recv()

        def choose(j, taken):
            block = partner[h, base + j]
            near = here(block)
            mine = own[h][jnp.clip(block - base, 0, plane - 1)]
            theirs = slot[h][jnp.minimum(taken, slots - 1)]
            pick[h, j] = jnp.where(near, mine, theirs)
            return taken + jnp.where(near, 0, 1)

        lax.fori_loop(0, plane, choose, 0, unroll=8)
        each_peer(
            lambda j, d: remote(
                pick.at[h, j], part.at[h, i], back_send.at[h], back_recv.at[h], d
            ).start()
        )
        pltpu.make_async_copy(pick.at[h, i], part.at[h, i], back_recv.at[h]).start()

        @pl.when(s == plane)
        def _():
            bytes_wait(edge.at[h], edge_recv.at[h])
            pltpu.make_async_copy(edge.at[h], prev.at[h, 0], prev_recv.at[h]).start()

        @pl.when(s > plane)
        def _():
            bytes_wait(edge.at[h], edge_recv.at[h])
            remote(edge.at[h], prev.at[h, i], extra_send.at[h], prev_recv.at[h], base).start()

    def query(h):
        return qs[:, :, h * DH : (h + 1) * DH].reshape(BS, DH)

    def scored(h, key):
        x = lax.dot_general(
            query(h), key, (((1,), (1,)), ((), ())), preferred_element_type=jnp.float32
        )
        return x * inv_scale

    def stacked(ref, h):
        return (
            ref[h, 0:half].reshape(BS, DH),
            ref[h, half:plane].reshape(BS, DH),
        )

    def local():
        for h in range(2):
            lanes = slice(h * DH, (h + 1) * DH)
            x = scored(h, kv[0:half, :, lanes].reshape(BS, DH))
            top = jnp.max(x, axis=1, keepdims=True)
            e = jnp.exp(x - top)
            top_all[h] = top
            den_all[h] = jnp.sum(e, axis=1, keepdims=True)
            mix_all[h] = jnp.dot(
                e.astype(jnp.bfloat16),
                kv[half:plane, :, lanes].reshape(BS, DH),
                preferred_element_type=jnp.float32,
            )

    def merged(h, ref, shift):
        key, val = stacked(ref, h)
        x = scored(h, key)
        if shift is not None:
            x = x + shift
        old = top_all[h]
        top = jnp.maximum(old, jnp.max(x, axis=1, keepdims=True))
        keep = jnp.exp(old - top)
        e = jnp.exp(x - top)
        den = den_all[h] * keep + jnp.sum(e, axis=1, keepdims=True)
        mix = mix_all[h] * keep + jnp.dot(
            e.astype(jnp.bfloat16), val, preferred_element_type=jnp.float32
        )
        return top, den, mix

    def previous(h):
        top, den, mix = merged(h, prev, None)
        top_all[h] = top
        den_all[h] = den
        mix_all[h] = mix

    def early_previous():
        @pl.when(i > 0)
        def _():
            for h in range(2):
                bytes_wait(prev.at[h], prev_recv.at[h])
                previous(h)

    def late_previous(h):
        @pl.when(s == plane)
        def _():
            bytes_wait(prev.at[h], prev_recv.at[h])
            previous(h)

    def finish(h):
        late_previous(h)
        bytes_wait(part.at[h], back_recv.at[h])
        _, den, mix = merged(h, part, bias[0, h : h + 1, 0:1])
        out[:, h * DH : (h + 1) * DH] = (mix * (1.0 / den)).astype(jnp.bfloat16)

    def owned():
        mine = i // stride
        each_peer(
            lambda j, d: remote(
                partial.at[mine], partial.at[mine], partial_send, partial_recv, d
            ).start()
        )

    def scores():
        queries = jnp.concatenate([feat[:, 0, 0, :], feat[:, 1, 0, :]], axis=0)
        keys = jnp.concatenate([feat[:, 2, 0, :], feat[:, 3, 0, :]], axis=0)
        x = lax.dot_general(
            queries,
            keys,
            (((1,), (1,)), ((), ())),
            precision=HIGHEST,
            preferred_element_type=jnp.float32,
        )
        x = x * (SHARPNESS / math.sqrt(2 * DH * groups))
        partial[i // stride, :, 0 : 2 * plane] = x[0:plane]
        partial[i // stride, :, 2 * plane : 4 * plane] = x[plane : 2 * plane]

    def sinkhorn():
        both = jnp.sum(partial[...], axis=0)
        x = jnp.concatenate([both[:, 0 : 2 * plane], both[:, 2 * plane : 4 * plane]], axis=0)

        def sweep(_, x):
            for along in (1, 0):
                top = jnp.max(x, axis=along, keepdims=True)
                x = x - (top + jnp.log(jnp.sum(jnp.exp(x - top), axis=along, keepdims=True)))
            return x

        x = lax.fori_loop(0, SINK_ITERS, sweep, x, unroll=2)
        row = lax.broadcasted_iota(jnp.int32, x.shape, 0)
        col = lax.broadcasted_iota(jnp.int32, x.shape, 1)
        for which, block in ((0, s), (1, mirror)):
            for h in range(2):
                chosen = (row == i + which * plane) & (col == partner[h, block])
                value = jnp.sum(
                    jnp.sum(jnp.where(chosen, x, 0.0), axis=1, keepdims=True), axis=0, keepdims=True
                )
                bias[which, h : h + 1, :] = jnp.broadcast_to(
                    value + math.log(2 * plane), (1, DH)
                )
            bias[which, 2:3, :] = jnp.max(counts[...], axis=0)

    @pl.when(p == 0)
    def _():
        most = jnp.maximum(count(0), count(1))
        counts[g] = jnp.full((1, DH), most, jnp.int32).astype(jnp.float32)
        pl.semaphore_wait(barrier, plane - 1 + groups - 1)
        each_group(lambda og: to_column(s, og))
        each_group(
            lambda og: remote(
                counts.at[g], counts.at[g], count_send, count_recv, s, og
            ).start()
        )
        spread(0)
        spread(1)
        hand_on()
        tables()
        local()
        spread_done(0)
        fill(0)
        pl.semaphore_wait(ready, 1)
        bytes_wait(feat.at[pl.ds(0, 2 * groups - 1)], col_recv)

        def to_owner(sl, c):
            owner = sl * stride

            @pl.when(owner != i)
            def _():
                remote(col.at[:, sl], feat.at[i], feat_send, feat_recv, base + owner).start()

            @pl.when(owner == i)
            def _():
                pltpu.make_async_copy(col.at[:, sl], feat.at[i], feat_recv).start()

            return c

        lax.fori_loop(0, slices, to_owner, 0, unroll=2)
        spread_done(1)
        fill(1)

        @pl.when(i % stride == 0)
        def _():
            bytes_wait(feat, feat_recv)
            scores()
            owned()

        for h in range(2):
            edge_copy(h).start()
            exchange_start(h)
        early_previous()
        bytes_wait(counts.at[pl.ds(0, groups - 1)], count_recv)

        @pl.when(i % stride == 0)
        def _():
            bytes_wait(partial.at[pl.ds(0, slices - 1)], partial_recv)
            bytes_wait(feat.at[pl.ds(0, slices - 1)], feat_send)

        @pl.when(i % stride != 0)
        def _():
            bytes_wait(partial, partial_recv)
            bytes_wait(feat.at[pl.ds(0, slices)], feat_send)

        sinkhorn()
        crowd[...] = bias[0, 2:3, :]
        bias_copy.start()
        give_back(0)
        give_back(1)
        finish(0)
        finish(1)
        bytes_wait(col.at[pl.ds(0, 2), pl.ds(0, 2 * (groups - 1))], col_send)

        @pl.when(i % stride == 0)
        def _():
            for _ in range(plane - 1):
                bytes_wait(partial.at[0], partial_send)

        bytes_wait(counts.at[pl.ds(0, groups - 1)], count_send)
        for h in range(2):
            edge_copy(h).wait_send()
            exchange(h, 0).wait_send()
            exchange(h, 1).wait_send()
        bias_copy.wait_send()

    @pl.when(p == 1)
    def _():
        followers = sum(jnp.where(g == leader, 1, 0) for _, leader in turns)
        pl.semaphore_wait(barrier, plane - 1 + groups + followers)
        signal(ready, mirror)
        for og in range(groups):
            to_column(mirror, og)
        spread(0)
        spread(1)
        tables()
        spread_done(0)
        fill(0)

        for follower, _ in turns:

            @pl.when(g == follower)
            def _():
                pl.semaphore_wait(turn, 1)

        exchange_start(0)
        spread_done(1)
        fill(1)
        exchange_start(1)
        hand_on()
        exchange(0, 0).wait_send()
        exchange(0, 1).wait_send()
        for follower, leader in turns:

            @pl.when(g == leader)
            def _():
                signal(turn, s, follower)

        exchange(1, 0).wait_send()

        local()
        early_previous()
        give_back(0)
        give_back(1)
        bias_copy.wait_recv()
        crowd[...] = bias[0, 2:3, :]
        finish(0)
        finish(1)
        exchange(1, 1).wait_send()
        bytes_wait(col.at[pl.ds(0, 2), pl.ds(0, slices)], col_send)

    for h in range(2):
        bytes_wait(own[h].at[pl.ds(0, plane - 1)], spread_send.at[h])
        bytes_wait(pick.at[h, pl.ds(0, plane - 1)], back_send.at[h])

    @pl.when(i < plane - 1)
    def _():
        for h in range(2):
            bytes_wait(prev.at[h], prev_send.at[h])

    @pl.when(s > plane)
    def _():
        for h in range(2):
            bytes_wait(edge.at[h], extra_send.at[h])


def attention(plane, groups, slots, collective_id, name):
    piece = 2 * BS // plane
    seq = 2 * plane
    half = plane // 2
    width = 2 * DH
    slices = 2 * groups
    dma = pltpu.SemaphoreType.DMA
    hbm = pl.BlockSpec(memory_space=pl.ANY)
    vmem = pl.BlockSpec(memory_space=pltpu.VMEM)
    folded = (half, piece, width)
    one, two = dma(()), dma((2,))
    pieces = pltpu.VMEM((2, plane, piece, DH), jnp.bfloat16)
    head_pieces = pltpu.VMEM((plane, piece, DH), jnp.bfloat16)
    head_slots = pltpu.VMEM((slots, piece, DH), jnp.bfloat16)

    def call(queries, keys, values, partner):
        return pl.pallas_call(
            functools.partial(sparse_attention_kernel, plane, groups, slots),
            out_shape=(
                jax.ShapeDtypeStruct(queries.shape, queries.dtype),
                pltpu.VMEM((1, DH), jnp.float32),
            ),
            in_specs=[pl.BlockSpec(memory_space=pltpu.HBM), hbm, hbm, hbm],
            out_specs=(vmem, vmem),
            scratch_shapes=[
                pltpu.VMEM(folded, jnp.bfloat16),
                pltpu.VMEM((plane, piece, width), jnp.bfloat16),
                head_pieces,
                head_pieces,
                head_slots,
                head_slots,
                head_slots,
                head_slots,
                pltpu.VMEM((2, piece, DH), jnp.bfloat16),
                pieces,
                pieces,
                pieces,
                pltpu.VMEM((4, slices, 1, DH), jnp.float32),
                pltpu.VMEM((plane, 4, 1, DH), jnp.float32),
                pltpu.VMEM((slices, plane, max(DH, 2 * seq)), jnp.float32),
                pltpu.VMEM((groups, 1, DH), jnp.float32),
                pltpu.VMEM((2, 3, DH), jnp.float32),
                pltpu.VMEM((2, BS, 1), jnp.float32),
                pltpu.VMEM((2, BS, 1), jnp.float32),
                pltpu.VMEM((2, BS, DH), jnp.float32),
                pltpu.SMEM((2, plane + 2), jnp.int32),
                pltpu.SMEM((2, seq), jnp.int32),
                dma((4,)),
            ]
            + [one] * 10
            + [two] * 2
            + [dma((4,))] * 2
            + [two] * 7
            + [pltpu.SemaphoreType.REGULAR] * 2,
            compiler_params=pltpu.CompilerParams(
                collective_id=collective_id, has_side_effects=True
            ),
            name=name,
        )(partner, queries.reshape(folded), keys.reshape(folded), values.reshape(folded))

    return call


def solution(mesh):
    seq, groups = mesh.shape["seq"], mesh.shape["head"]
    plane = seq // 2
    slots = plane * SLOT_SHARE // 32
    packed = attention(plane, groups, slots, 0, "packed")
    whole = attention(plane, groups, plane, 1, "whole")

    def body(queries, keys, values, partner):
        attended, crowd = packed(queries, keys, values, partner)
        return lax.cond(
            crowd[0, 0] > slots,
            lambda: whole(queries, keys, values, partner)[0],
            lambda: attended,
        )

    return jax.shard_map(
        body,
        mesh=mesh,
        in_specs=(P("seq", "head"), P("seq", "head"), P("seq", "head"), P("head", None)),
        out_specs=P("seq", "head"),
        check_vma=False,
    )
```
